32 devices in a mesh: row: 8 (over y, x, core), col: 4 (over z).
Axes of the slice: x: 2, y: 2, z: 4, core: 2. Of those that a mesh axis runs over, the one named last changes fastest.
Arguments:
- tokens: bfloat16 [4, 4096, 384], P('col', 'row'), may hold values from -6 to 6
- segment_ids: int32 [8192], replicated, may hold values from 0 to 64, as said below
- gain_one: float32 [768], P('col'), may hold values from 0.5 to 1.5
- qkv_weight: bfloat16 [768, 3, 768], P('row', None, 'col'), may hold values from -0.21875 to 0.21875
- out_weight: bfloat16 [768, 768], P('row', 'col'), may hold values from -0.875 to 0.875
- gain_two: float32 [768], P('col'), may hold values from 0.5 to 1.5
- in_weight: bfloat16 [768, 2, 1152], P('row', None, 'col'), may hold values from -0.21875 to 0.21875
- down_weight: bfloat16 [1152, 768], P('row', 'col'), may hold values from -0.1875 to 0.1875
- cotangent: bfloat16 [4, 4096, 384], P('col', 'row'), may hold values from -6 to 6
Outputs:
- mixed: bfloat16 [4, 4096, 384], P('col', 'row')
- input_grad: float32 [4, 4096, 384], P('col', 'row')
- gain_one_grad: float32 [768], P('col')
- qkv_grad: float32 [768, 3, 768], P('row', None, 'col')
- out_grad: float32 [768, 768], P('row', 'col')
- gain_two_grad: float32 [768], P('col')
- in_grad: float32 [768, 2, 1152], P('row', None, 'col')
- down_grad: float32 [1152, 768], P('row', 'col')
The draws below stay inside these ranges and needn't reach their ends.
Inputs may be any that keep to these rules, and one draw needn't show every extreme that they name: `segment_ids`: document ids never fall along the stream and rise by one where a document begins. Within each aligned block of 1024 tokens exactly 8 documents begin, none within 64 tokens of either end of the block.
All inputs are finite; a program needn't handle non-finite values.
Results may differ from the reference program's by a relative error of at most 0.015.
Values may be sent and summed in bfloat16 or wider, within the bound.
A program may use at most 128 MiB of HBM per device.

```python
import jax
import jax.numpy as jnp
from jax import lax

HEADS = 12
HEAD_DIM = 64
D = 768
FF = 1152
WINDOW = 128
TOK_DEV = 1024
DOC_DEV = 8
TOKENS = 8192
LENGTH = 4096
N_COL = 4


def draw_segment_ids(key, part):
    blocks = TOKENS // TOK_DEV
    half_window = WINDOW // 2
    inner = TOK_DEV - 2 * half_window
    block_keys = jax.random.split(jax.random.fold_in(key, 17), blocks)
    picks = jax.vmap(lambda one_key: jax.random.permutation(one_key, inner)[:DOC_DEV])(block_keys) + half_window
    places = jnp.arange(TOK_DEV, dtype=jnp.int32)
    marks = jnp.sum((places[None, None, :] == picks[:, :, None]).astype(jnp.int32), axis=1)
    return jnp.cumsum(marks.reshape(TOKENS)).astype(jnp.int32)


def block_levels(stream_key, shape, cuts, low, high):
    factor_of, own = 1.0, jax.random.fold_in(stream_key, 6)
    for position, shards_of in cuts:
        draws = jnp.exp(jax.random.uniform(jax.random.fold_in(own, position), (shards_of,), jnp.float32, low / len(cuts), high / len(cuts)))
        factor_of = factor_of * jnp.repeat(draws, shape[position] // shards_of).reshape([-1 if axis == position else 1 for axis in range(len(shape))])
    return factor_of


def centred(own_key, dims, deviation, bound, pieces=(), kind=jnp.bfloat16):
    entries = jax.random.normal(own_key, dims, jnp.float32) * deviation
    if len(pieces) > 0:
        entries = block_levels(own_key, dims, pieces, -0.22, 0.18) * entries
    return jnp.clip(entries, min=-bound, max=bound).astype(kind)


def setup_inputs(seed: int = 0) -> dict:
    keys = jax.random.split(jax.random.key(seed), 10)
    return {
        "tokens": centred(keys[0], (N_COL, TOKENS // 2, 2 * D // N_COL), 1.0, 6.0, ((0, 4), (1, 8))),
        "segment_ids": draw_segment_ids(jax.random.fold_in(keys[9], 71), 0),
        "gain_one": jnp.clip(1.0 + 0.1 * jax.random.normal(keys[2], (D,), jnp.float32), 0.5, 1.5),
        "qkv_weight": centred(keys[3], (D, 3, D), D ** -0.5, 0.21875, ((0, 8), (2, 4))),
        "out_weight": centred(keys[4], (D, D), (D // 16) ** -0.5, 0.875, ((0, 8), (1, 4))),
        "gain_two": jnp.clip(1.0 + 0.1 * jax.random.normal(keys[5], (D,), jnp.float32), 0.5, 1.5),
        "in_weight": centred(keys[6], (D, 2, FF), D ** -0.5, 0.21875, ((0, 8), (2, 4))),
        "down_weight": centred(keys[7], (FF, D), FF ** -0.5, 0.1875, ((0, 8), (1, 4))),
        "cotangent": centred(keys[8], (N_COL, TOKENS // 2, 2 * D // N_COL), 1.0, 6.0, ((0, 4), (1, 8))),
    }


@jax.custom_vjp
def low(v):
    return lax.optimization_barrier(v.astype(jnp.bfloat16)).astype(jnp.float32)

@jax.custom_vjp
def low_back(v):
    return v

def low_keep(v):
    return (low(v), None)

def low_pass(kept, grad):
    return (grad,)

def back_keep(v):
    return (v, None)

def back_low(kept, grad):
    return (low(grad),)
low.defvjp(low_keep, low_pass)
low_back.defvjp(back_keep, back_low)

def unpack_rows(packed):
    width = D // N_COL
    return packed.reshape(N_COL, TOKENS // 2, 2, width).transpose(1, 2, 0, 3).reshape(TOKENS, D)

def pack_rows(matrix):
    width = D // N_COL
    return matrix.reshape(TOKENS // 2, 2, N_COL, width).transpose(2, 0, 1, 3).reshape(N_COL, TOKENS // 2, 2 * width)

def norm_rows(values, gain_row):
    mean_value = lax.optimization_barrier(jnp.mean(values, axis=-1, keepdims=True))
    variance = lax.optimization_barrier(jnp.mean(values * values, axis=-1, keepdims=True)) - mean_value * mean_value
    return (values - mean_value) * lax.rsqrt(variance + 1e-05) * gain_row

def rotate(values, cosine, sine_table):
    half_dim = values.shape[-1] // 2
    turned = jnp.concatenate([-values[..., half_dim:], values[..., :half_dim]], axis=-1)
    return values * cosine + turned * sine_table

def attend(queries, key_rows, value_rows, segment):
    half_window = WINDOW // 2
    length = queries.shape[0]
    block_rows = min(512, length)
    key_span = block_rows + 2 * half_window
    padded_keys = jnp.pad(key_rows, ((half_window, half_window), (0, 0), (0, 0)))
    padded_values = jnp.pad(value_rows, ((half_window, half_window), (0, 0), (0, 0)))
    padded_ids = jnp.pad(segment, half_window, constant_values=-1)
    offsets = jnp.arange(key_span, dtype=jnp.int32)[None, :] - half_window - jnp.arange(block_rows, dtype=jnp.int32)[:, None]
    in_window = jnp.abs(offsets) <= half_window
    score_scale = HEAD_DIM ** (-0.5)

    def one_block(block_start):
        block_queries = lax.dynamic_slice_in_dim(queries, block_start, block_rows, 0)
        block_keys = lax.dynamic_slice_in_dim(padded_keys, block_start, key_span, 0)
        block_values = lax.dynamic_slice_in_dim(padded_values, block_start, key_span, 0)
        query_ids = lax.dynamic_slice_in_dim(segment, block_start, block_rows, 0)
        key_ids = lax.dynamic_slice_in_dim(padded_ids, block_start, key_span, 0)
        allowed = in_window & (query_ids[:, None] == key_ids[None, :])
        scores = low_back(score_scale * jnp.einsum('qhd,khd->hqk', block_queries, block_keys, precision=lax.Precision.HIGHEST))
        masked = jnp.where(allowed[None], scores, -1e+30)
        largest = lax.optimization_barrier(jnp.max(masked, axis=-1, keepdims=True))
        log_total = largest + jnp.log(lax.optimization_barrier(jnp.sum(jnp.exp(masked - largest), axis=-1, keepdims=True)))
        weights = low(jnp.exp(masked - log_total))
        return jnp.einsum('hqk,khd->qhd', weights, block_values, precision=lax.Precision.HIGHEST)
    starts = jnp.arange(length // block_rows, dtype=jnp.int32) * block_rows
    outputs = lax.map(jax.checkpoint(one_block), starts)
    return outputs.reshape(length, queries.shape[1] * queries.shape[2])

def layer_forward(token_rows, gain_first, qkv_matrix, out_matrix, gain_second, in_matrix, down_matrix, segment, cosine, sine_table):
    length = token_rows.shape[0]
    normed_one = low(norm_rows(token_rows, gain_first))
    projected = low_back(jnp.einsum('td,dsf->tsf', normed_one, qkv_matrix, precision=lax.Precision.HIGHEST))
    shaped = projected.reshape(length, 3, HEADS, HEAD_DIM)
    queries = low(rotate(shaped[:, 0], cosine, sine_table))
    key_rows = low(rotate(shaped[:, 1], cosine, sine_table))
    value_rows = low(shaped[:, 2])
    attended = low_back(low(attend(queries, key_rows, value_rows, segment)))
    branch = low_back(jnp.dot(attended, out_matrix, precision=lax.Precision.HIGHEST))
    middle = token_rows + branch
    normed_two = low(norm_rows(middle, gain_second))
    gate_up = low_back(jnp.einsum('td,dsf->tsf', normed_two, in_matrix, precision=lax.Precision.HIGHEST))
    hidden = low(jax.nn.gelu(gate_up[:, 0], approximate=False) * gate_up[:, 1])
    return middle + low_back(jnp.dot(hidden, down_matrix, precision=lax.Precision.HIGHEST))

def reference(tokens, segment_ids, gain_one, qkv_weight, out_weight, gain_two, in_weight, down_weight, cotangent):
    sequences = TOKENS // LENGTH
    token_values = unpack_rows(tokens.astype(jnp.float32)).reshape(sequences, LENGTH, D)
    grad_values = unpack_rows(cotangent.astype(jnp.float32)).reshape(sequences, LENGTH, D)
    id_rows = segment_ids.reshape(sequences, LENGTH)
    params = (gain_one.astype(jnp.float32), qkv_weight.astype(jnp.float32), out_weight.astype(jnp.float32), gain_two.astype(jnp.float32), in_weight.astype(jnp.float32), down_weight.astype(jnp.float32))
    places = jnp.arange(LENGTH, dtype=jnp.float32)
    frequencies = 10000.0 ** (-(jnp.arange(HEAD_DIM // 2, dtype=jnp.float32) * 2.0) / HEAD_DIM)
    angles = places[:, None] * frequencies[None, :]
    angles = jnp.concatenate([angles, angles], axis=1)[:, None, :]
    cosine = jnp.cos(angles)
    sine_table = jnp.sin(angles)

    def per_sequence(totals, items):
        seq_tokens, seq_grads, seq_ids = items

        def forward(token_rows, gain_first, qkv_matrix, out_matrix, gain_second, in_matrix, down_matrix):
            return layer_forward(token_rows, gain_first, qkv_matrix, out_matrix, gain_second, in_matrix, down_matrix, seq_ids, cosine, sine_table)
        outputs, pullback = jax.vjp(forward, seq_tokens, *params)
        grads = pullback(seq_grads)
        return (jax.tree.map(jnp.add, totals, tuple(grads[1:])), (outputs, grads[0]))
    zeros = jax.tree.map(jnp.zeros_like, params)
    totals, (outputs, token_grads) = lax.scan(per_sequence, zeros, (token_values, grad_values, id_rows))
    mixed = pack_rows(outputs.reshape(TOKENS, D)).astype(jnp.bfloat16)
    input_grad = pack_rows(token_grads.reshape(TOKENS, D))
    return (mixed, input_grad, totals[0], totals[1], totals[2], totals[3], totals[4], totals[5])
```

```python
import functools

import jax
import jax.numpy as jnp
import numpy as np
from jax import lax
from jax.experimental import pallas as pl
from jax.experimental.pallas import tpu as pltpu
from jax.sharding import PartitionSpec as P

HEAD_DIM = 64
WINDOW = 128
SEQ_MAX = 4096


EPSILON = 1e-05


def with_halo(block, sides, width):
    for axis, dim in sides:
        count = lax.axis_size(axis)
        forward = [(i, i + 1) for i in range(count - 1)]
        backward = [(target, source) for source, target in forward]
        low = lax.ppermute(
            lax.slice_in_dim(block, block.shape[dim] - width, None, axis=dim), axis, forward
        )
        high = lax.ppermute(lax.slice_in_dim(block, 0, width, axis=dim), axis, backward)
        block = jnp.concatenate([low, block, high], axis=dim)
    return block


def rotate(values, cosine, sine_table):
    half_dim = values.shape[-1] // 2
    turned = jnp.concatenate([-values[..., half_dim:], values[..., :half_dim]], axis=-1)
    return values * cosine + turned * sine_table


def rotate_back(grad_rows, cosine, sine_table):
    half_dim = grad_rows.shape[-1] // 2
    turned = jnp.concatenate([-grad_rows[..., half_dim:], grad_rows[..., :half_dim]], axis=-1)
    return grad_rows * cosine - turned * sine_table


def spread(values):
    return lax.all_gather(values, "col", axis=1, tiled=True)


def collect(partial_rows):
    return lax.psum_scatter(partial_rows, "col", scatter_dimension=1, tiled=True)


def norm_forward(values, full_width):
    row_sums = lax.psum((jnp.sum(values, axis=1), jnp.sum(values * values, axis=1)), "col")
    mean_value = row_sums[0] / full_width
    variance = row_sums[1] / full_width - mean_value * mean_value
    inverse = lax.rsqrt(variance + EPSILON)
    return ((values - mean_value[:, None]) * inverse[:, None], inverse)


def norm_backward(grad_rows, scaled, inverse, gain_part, full_width):
    weighted = grad_rows * gain_part
    row_sums = lax.psum((jnp.sum(weighted, axis=1), jnp.sum(weighted * scaled, axis=1)), "col")
    input_part = inverse[:, None] * (
        weighted - row_sums[0][:, None] / full_width - scaled * (row_sums[1][:, None] / full_width)
    )
    return (input_part, jnp.sum(grad_rows * scaled, axis=0))


def geglu(gate_up):
    return jax.nn.gelu(gate_up[:, 0], approximate=False) * gate_up[:, 1]


def local(
    tokens,
    segment_ids,
    gain_one,
    qkv_weight,
    out_weight,
    gain_two,
    in_weight,
    down_weight,
    cotangent,
):
    pair_rows = tokens.shape[1]
    rows_here = pair_rows * 2
    tok_width = tokens.shape[2] // 2
    full_width = tok_width * lax.axis_size("col")
    heads_here = qkv_weight.shape[2] // HEAD_DIM
    head_width = heads_here * HEAD_DIM
    half_window = WINDOW // 2
    block_rows = min(512, rows_here)
    block_count = rows_here // block_rows
    key_span = block_rows + 2 * half_window
    score_scale = HEAD_DIM ** (-0.5)
    length = min(SEQ_MAX, rows_here * lax.axis_size("row"))
    first_row = lax.axis_index("row") * rows_here
    grad_rows = cotangent.reshape(rows_here, tok_width)
    qkv_full, out_full, in_full, down_full = (
        lax.all_gather(qkv_weight, "row", axis=0, tiled=True),
        lax.all_gather(out_weight, "row", axis=0, tiled=True),
        lax.all_gather(in_weight, "row", axis=0, tiled=True),
        lax.all_gather(down_weight, "row", axis=0, tiled=True),
    )
    global_rows = first_row + jnp.arange(rows_here, dtype=jnp.int32)
    places = (global_rows % length).astype(jnp.float32)
    frequencies = 10000.0 ** (-(jnp.arange(HEAD_DIM // 2, dtype=jnp.float32) * 2.0) / HEAD_DIM)
    angles = places[:, None] * frequencies[None, :]
    angles = jnp.concatenate([angles, angles], axis=1)[:, None, :]
    cosine = jnp.cos(angles)
    sine_table = jnp.sin(angles)
    query_ids = lax.dynamic_slice_in_dim(segment_ids, first_row, rows_here)
    padded_ids = jnp.pad(segment_ids, half_window, constant_values=-1)
    key_ids = lax.dynamic_slice_in_dim(padded_ids, first_row, rows_here + 2 * half_window)
    query_seqs = global_rows // length
    key_seqs = (
        first_row - half_window + jnp.arange(rows_here + 2 * half_window, dtype=jnp.int32)
    ) // length
    offsets = (
        jnp.arange(key_span, dtype=jnp.int32)[None, :]
        - half_window
        - jnp.arange(block_rows, dtype=jnp.int32)[:, None]
    )
    in_window = jnp.abs(offsets) <= half_window

    def block_scores(block_start, block_queries, block_keys):
        same_doc = (
            query_ids[block_start : block_start + block_rows, None]
            == key_ids[None, block_start : block_start + key_span]
        )
        same_seq = (
            query_seqs[block_start : block_start + block_rows, None]
            == key_seqs[None, block_start : block_start + key_span]
        )
        allowed = in_window & same_doc & same_seq
        scores = (
            jnp.einsum(
                "qhd,khd->hqk", block_queries, block_keys, preferred_element_type=jnp.float32
            )
            * score_scale
        )
        return jnp.where(allowed[None], scores, -1e30)

    token_values = tokens.reshape(rows_here, tok_width).astype(jnp.float32)
    scaled_one, inverse_one = norm_forward(token_values, full_width)
    normed_one_full = spread((scaled_one * gain_one).astype(jnp.bfloat16))
    projected = jnp.einsum(
        "td,dsf->tsf", normed_one_full, qkv_full, preferred_element_type=jnp.float32
    )
    projected = projected.reshape(rows_here, 3, heads_here, HEAD_DIM)
    queries = rotate(projected[:, 0], cosine, sine_table).astype(jnp.bfloat16)
    key_rows = rotate(projected[:, 1], cosine, sine_table).astype(jnp.bfloat16)
    value_rows = projected[:, 2].astype(jnp.bfloat16)
    key_value = jnp.concatenate(
        [key_rows.reshape(rows_here, head_width), value_rows.reshape(rows_here, head_width)], axis=1
    )
    padded_pair = with_halo(key_value, (("row", 0),), half_window)
    padded_keys = padded_pair[:, :head_width].reshape(
        rows_here + 2 * half_window, heads_here, HEAD_DIM
    )
    padded_values = padded_pair[:, head_width:].reshape(
        rows_here + 2 * half_window, heads_here, HEAD_DIM
    )
    output_blocks = []
    total_blocks = []
    for block_number in range(block_count):
        block_start = block_number * block_rows
        masked = block_scores(
            block_start,
            queries[block_start : block_start + block_rows],
            padded_keys[block_start : block_start + key_span],
        )
        largest = jnp.max(masked, axis=-1, keepdims=True)
        log_total = largest + jnp.log(jnp.sum(jnp.exp(masked - largest), axis=-1, keepdims=True))
        weights = jnp.exp(masked - log_total).astype(jnp.bfloat16)
        output_blocks.append(
            jnp.einsum(
                "hqk,khd->qhd",
                weights,
                padded_values[block_start : block_start + key_span],
                preferred_element_type=jnp.float32,
            )
        )
        total_blocks.append(log_total)
    attended = (
        jnp.concatenate(output_blocks, axis=0).reshape(rows_here, head_width).astype(jnp.bfloat16)
    )
    attended_full = spread(attended)
    middle = token_values + jnp.dot(attended_full, out_full, preferred_element_type=jnp.float32)
    scaled_two, inverse_two = norm_forward(middle, full_width)
    normed_two_full = spread((scaled_two * gain_two).astype(jnp.bfloat16))
    gate_up = jnp.einsum(
        "td,dsf->tsf", normed_two_full, in_full, preferred_element_type=jnp.float32
    )
    hidden_value, geglu_pull = jax.vjp(geglu, gate_up)
    hidden_full = spread(hidden_value.astype(jnp.bfloat16))
    mixed = (middle + jnp.dot(hidden_full, down_full, preferred_element_type=jnp.float32)).astype(
        jnp.bfloat16
    )
    qkv_back, out_back, in_back, down_back = (
        lax.all_gather(qkv_weight, "row", axis=0, tiled=True),
        lax.all_gather(out_weight, "row", axis=0, tiled=True),
        lax.all_gather(in_weight, "row", axis=0, tiled=True),
        lax.all_gather(down_weight, "row", axis=0, tiled=True),
    )
    down_part = jnp.einsum("tf,td->fd", hidden_full, grad_rows, preferred_element_type=jnp.float32)
    hidden_grad = collect(
        jnp.einsum("td,fd->tf", grad_rows, down_back, preferred_element_type=jnp.float32)
    )
    gate_up_grad = geglu_pull(hidden_grad)[0].astype(jnp.bfloat16)
    in_part = jnp.einsum(
        "td,tsf->dsf", normed_two_full, gate_up_grad, preferred_element_type=jnp.float32
    )
    normed_two_grad = collect(
        jnp.einsum("tsf,dsf->td", gate_up_grad, in_back, preferred_element_type=jnp.float32)
    )
    middle_norm_grad, gain_two_part = norm_backward(
        normed_two_grad, scaled_two, inverse_two, gain_two, full_width
    )
    middle_grad = grad_rows.astype(jnp.float32) + middle_norm_grad
    branch_grad = middle_grad.astype(jnp.bfloat16)
    out_part = jnp.einsum(
        "td,tf->df", attended_full, branch_grad, preferred_element_type=jnp.float32
    )
    attended_grad = collect(
        jnp.einsum("tf,df->td", branch_grad, out_back, preferred_element_type=jnp.float32)
    ).astype(jnp.bfloat16)
    attended_heads = attended_grad.reshape(rows_here, heads_here, HEAD_DIM)
    query_blocks = []
    key_grad_ext = jnp.zeros((rows_here + 2 * half_window, heads_here, HEAD_DIM), jnp.float32)
    value_grad_ext = jnp.zeros((rows_here + 2 * half_window, heads_here, HEAD_DIM), jnp.float32)
    for block_number in range(block_count):
        block_start = block_number * block_rows
        block_queries = queries[block_start : block_start + block_rows]
        block_keys = padded_keys[block_start : block_start + key_span]
        block_values = padded_values[block_start : block_start + key_span]
        block_grads = attended_heads[block_start : block_start + block_rows]
        masked = block_scores(block_start, block_queries, block_keys)
        probs = jnp.exp(masked - total_blocks[block_number])
        prob_grad = jnp.einsum(
            "qhd,khd->hqk", block_grads, block_values, preferred_element_type=jnp.float32
        )
        inner = jnp.sum(probs * prob_grad, axis=-1, keepdims=True)
        score_grad = (probs * (prob_grad - inner)).astype(jnp.bfloat16)
        query_blocks.append(
            jnp.einsum("hqk,khd->qhd", score_grad, block_keys, preferred_element_type=jnp.float32)
            * score_scale
        )
        key_grad_ext = key_grad_ext.at[block_start : block_start + key_span].add(
            jnp.einsum(
                "hqk,qhd->khd", score_grad, block_queries, preferred_element_type=jnp.float32
            )
            * score_scale
        )
        value_grad_ext = value_grad_ext.at[block_start : block_start + key_span].add(
            jnp.einsum(
                "hqk,qhd->khd",
                probs.astype(jnp.bfloat16),
                block_grads,
                preferred_element_type=jnp.float32,
            )
        )
    grad_pair = jnp.concatenate(
        [key_grad_ext.reshape(-1, head_width), value_grad_ext.reshape(-1, head_width)], axis=1
    )
    rim_rows = jnp.concatenate(
        [grad_pair[:half_window], grad_pair[rows_here + half_window :]], axis=0
    )
    beside_all = with_halo(rim_rows.astype(jnp.bfloat16), (("row", 0),), half_window).astype(
        rim_rows.dtype
    )
    own_grad = grad_pair[half_window : half_window + rows_here]
    own_grad = own_grad.at[:half_window].add(beside_all[:half_window])
    own_grad = own_grad.at[rows_here - half_window :].add(beside_all[3 * half_window :])
    key_grad = own_grad[:, :head_width].reshape(rows_here, heads_here, HEAD_DIM)
    value_grad = own_grad[:, head_width:].reshape(rows_here, heads_here, HEAD_DIM)
    query_grad = jnp.concatenate(query_blocks, axis=0)
    projected_grad = jnp.stack(
        [
            rotate_back(query_grad, cosine, sine_table),
            rotate_back(key_grad, cosine, sine_table),
            value_grad,
        ],
        axis=1,
    )
    projected_grad = projected_grad.reshape(rows_here, 3, head_width).astype(jnp.bfloat16)
    qkv_part = jnp.einsum(
        "td,tsf->dsf", normed_one_full, projected_grad, preferred_element_type=jnp.float32
    )
    normed_one_grad = collect(
        jnp.einsum("tsf,dsf->td", projected_grad, qkv_back, preferred_element_type=jnp.float32)
    )
    token_norm_grad, gain_one_part = norm_backward(
        normed_one_grad, scaled_one, inverse_one, gain_one, full_width
    )
    input_grad = middle_grad + token_norm_grad
    weight_grads = (
        lax.psum_scatter(qkv_part, "row", scatter_dimension=0, tiled=True),
        lax.psum_scatter(out_part, "row", scatter_dimension=0, tiled=True),
        lax.psum_scatter(in_part, "row", scatter_dimension=0, tiled=True),
        lax.psum_scatter(down_part, "row", scatter_dimension=0, tiled=True),
    )
    gain_grads = lax.psum((gain_one_part, gain_two_part), "row")
    mixed_out = mixed.reshape(1, pair_rows, 2 * tok_width)
    input_out = input_grad.reshape(1, pair_rows, 2 * tok_width)
    return (
        mixed_out,
        input_out,
        gain_grads[0],
        weight_grads[0],
        weight_grads[1],
        gain_grads[1],
        weight_grads[2],
        weight_grads[3],
    )


F32 = jnp.float32
BF = jnp.bfloat16
MESH = pl.DeviceIdType.MESH
ROWS = (96, 96, 144)
COLS = (768, 512, 256)
SPLIT = (48, 48, 64)
OWN = 256
EXT = 384
HALF = 64


def dot(a, b):
    return lax.dot_general(a, b, (((1,), (0,)), ((), ())), preferred_element_type=F32)


def dot_nt(a, b):
    return lax.dot_general(a, b, (((1,), (1,)), ((), ())), preferred_element_type=F32)


def dot_tn(a, b):
    return lax.dot_general(a, b, (((0,), (0,)), ((), ())), preferred_element_type=F32)


class Link:
    def __init__(self, src, dst, send, recv, row, col, when=None):
        self.args = (src, dst, send, recv)
        self.device = {"row": row, "col": col}
        self.when = when

    def make(self):
        src, dst, send, recv = self.args
        return pltpu.make_async_remote_copy(
            src_ref=src,
            dst_ref=dst,
            send_sem=send,
            recv_sem=recv,
            device_id=self.device,
            device_id_type=MESH,
        )

    def run(self, step):
        if self.when is None:
            step()
        else:
            pl.when(self.when)(step)

    def start(self):
        self.run(lambda: self.make().start())

    def sent(self):
        self.run(lambda: self.make().wait_send())


def arrived(dst, recv, row, col):
    pltpu.make_async_remote_copy(
        src_ref=dst,
        dst_ref=dst,
        send_sem=recv,
        recv_sem=recv,
        device_id={"row": row, "col": col},
        device_id_type=MESH,
    ).wait_recv()


def at_rows(ref, lead, start, size):
    return ref.at[lead, pl.ds(start, size), :]


def lane_iota(shape):
    return lax.broadcasted_iota(jnp.int32, shape, 1)


def swap_halves(tile):
    first = (lane_iota(tile.shape) % 64) < 32
    return jnp.where(first, pltpu.roll(tile, 96, 1), pltpu.roll(tile, 32, 1))


def layer_kernel(
    tok_in, cot_in, one_in, two_in, three_in, gains_in, qid_in, kid_in, freq_in,
    mixed_out, input_out, grad_one, grad_two, grad_three, gains_out,
    got_x, got_g, got_gain, w1, w2, w3, d1, d2, d3,
    core1, core2, core3, xa1, xa2, xa3, xb1, xb2, xb3, ya1, ya2, ya3, yb1, yb2, yb3,
    zl1, zl2, zl3, zr1, zr2, zr3,
    x_all, cos_t, sin_t, bias, n1, hat1, stat, qs, ks, vs, probs, att, mid, hat2, n2,
    tail_in, tail_down, hid, hid_tail, gel, gel_up, gel_t, gel_up_t, cot_pad, d_gate, d_tail,
    mid_grad, branch_pad, att_grad, d_proj, n1_grad,
    halo_out, halo_left, halo_right, mixed_send, mixed_got, input_send, input_got,
    gain_part, gain_z, gain_sum, gain_all,
    tok_s, tok_r, tok_rl, tok_rr, cot_s, cot_r, gn_s, gn_r,
    az_s, az_r, ax_s, ax_r, ay_s, ay_r, ac_s, ac_r,
    rc_s, rc_r, rx_s, rx_r, ry_s, ry_r, rz_s, rz_r,
    ha_s, ha_r, mx_s, mx_r, ig_s, ig_r, gz_s, gz_r, gp_s, gp_r,
    *, start_of,
):
    row = lax.axis_index("row")
    z = lax.axis_index("col")
    core = row % 2
    xc = (row // 2) % 2
    yc = row // 4
    rx = row + 2 - 4 * xc
    ry = row + 4 - 8 * yc
    rxy = ry + 2 - 4 * xc
    rc = row + 1 - 2 * core
    packs = (one_in, two_in, three_in)
    ws = (w1, w2, w3)
    ds_ = (d1, d2, d3)
    sent = []

    def go(link):
        link.start()
        sent.append(link)

    barrier = pltpu.get_barrier_semaphore()

    def greet(r, c):
        pl.semaphore_signal(barrier, inc=1, device_id={"row": r, "col": c}, device_id_type=MESH)

    for step in range(1, 8):
        greet((row + step) % 8, z)
    for step in range(1, 4):
        greet(row, (z + step) % 4)
    up, down = row < 7, row > 0
    low_end, high_end = (z == 0) & down, (z == 3) & up
    pl.when(down)(lambda: greet(row - 1, 3))
    pl.when(up)(lambda: greet(row + 1, 0))

    @pl.when(low_end)
    def _():
        for c in range(4):
            greet(row - 1, c)

    @pl.when(high_end)
    def _():
        for c in range(4):
            greet(row + 1, c)

    peers = 10 + jnp.minimum(row, 1) + jnp.minimum(7 - row, 1)
    peers += 4 * jnp.maximum(1 - z, 0) * jnp.minimum(row, 1)
    peers += 4 * jnp.maximum(z - 2, 0) * jnp.minimum(7 - row, 1)
    pl.semaphore_wait(barrier, peers)

    def window(c):
        low, high = max(0, 128 * c - 32), min(512, 128 * c + 160)
        return low, high - low, low - (128 * c - 32)

    for c in range(4):
        low, size, to = window(c)
        go(Link(tok_in.at[pl.ds(low, size), :], at_rows(got_x, z, to, size),
                tok_s.at[c], tok_r.at[z], row, c, z != c))
    go(Link(tok_in.at[pl.ds(0, 32), :], at_rows(got_x, z, 160, 32),
            tok_s.at[4], tok_rr.at[z], row - 1, 3, down))
    go(Link(tok_in.at[pl.ds(480, 32), :], at_rows(got_x, z, 0, 32),
            tok_s.at[5], tok_rl.at[z], row + 1, 0, up))
    for step in range(1, 4):
        c = (z + step) % 4
        go(Link(gains_in, got_gain.at[z], gn_s.at[step], gn_r.at[z], row, c))

    order = (z, 1 + z % 2, 2 - 2 * (z % 2) + z // 2, 3 - 3 * (z // 2))

    def near(i, c, r, part):
        size, cut = ROWS[i], SPLIT[i]
        start, count = {"all": (0, size), "a": (0, cut), "b": (cut, size - cut)}[part]
        return at_rows(ws[i], c, pl.multiple_of(r * size + start, 16), count)

    def gather_link(i, c, r, part, sem_s, sem_r, to_row, to_col, when=None):
        ref = near(i, c, r, part)
        return Link(ref, ref, sem_s, sem_r, to_row, to_col, when)

    def gather_first(i, j):
        c = order[j]
        if j == 0:
            go(gather_link(i, c, row, "all", az_s.at[i, 0, c], az_r.at[i, c], row, z + 1, z < 3))
            go(gather_link(i, c, row, "all", az_s.at[i, 1, c], az_r.at[i, c], row, z - 1, z > 0))
        else:
            arrived(near(i, c, row, "all"), az_r.at[i, c], row, z)
            go(gather_link(i, c, row, "all", az_s.at[i, 0, c], az_r.at[i, c], row, z + 1,
                           (c < z) & (z < 3)))
            go(gather_link(i, c, row, "all", az_s.at[i, 1, c], az_r.at[i, c], row, z - 1,
                           (c > z) & (z > 0)))
        go(gather_link(i, c, row, "a", ax_s.at[i, c, 0], ax_r.at[i, c, 0], rx, z))
        go(gather_link(i, c, row, "b", ay_s.at[i, c, 0], ay_r.at[i, c, 0], ry, z))
        go(gather_link(i, c, row, "b", ax_s.at[i, c, 1], ax_r.at[i, c, 1], rx, z))
        go(gather_link(i, c, row, "a", ay_s.at[i, c, 1], ay_r.at[i, c, 1], ry, z))
        go(gather_link(i, c, row, "all", ac_s.at[i, c, 0], ac_r.at[i, c, 0], rc, z))

    def gather_second(i, j):
        c = order[j]
        arrived(near(i, c, rx, "a"), ax_r.at[i, c, 0], rx, z)
        go(gather_link(i, c, rx, "a", ay_s.at[i, c, 2], ay_r.at[i, c, 2], ry, z))
        arrived(near(i, c, ry, "b"), ay_r.at[i, c, 0], ry, z)
        go(gather_link(i, c, ry, "b", ax_s.at[i, c, 2], ax_r.at[i, c, 2], rx, z))

    def gather_third(i, j):
        c = order[j]
        arrived(near(i, c, rx, "b"), ax_r.at[i, c, 1], rx, z)
        go(gather_link(i, c, rx, "all", ac_s.at[i, c, 1], ac_r.at[i, c, 1], rc, z))
        arrived(near(i, c, ry, "a"), ay_r.at[i, c, 1], ry, z)
        go(gather_link(i, c, ry, "all", ac_s.at[i, c, 2], ac_r.at[i, c, 2], rc, z))
        arrived(near(i, c, rxy, "a"), ay_r.at[i, c, 2], ry, z)
        arrived(near(i, c, rxy, "b"), ax_r.at[i, c, 2], rx, z)
        go(gather_link(i, c, rxy, "all", ac_s.at[i, c, 3], ac_r.at[i, c, 3], rc, z))

    def gather_done(i):
        for c in range(4):
            for n, r in enumerate((row, rx, ry, rxy)):
                arrived(near(i, c, r + 1 - 2 * core, "all"), ac_r.at[i, c, n], rc, z)

    for i in range(3):
        w = ws[i]
        w[z, pl.ds(pl.multiple_of(row * ROWS[i], 16), ROWS[i]), :] = packs[i][...]
    items = [(i, j) for i in range(3) for j in range(4)]

    def gather_step(t):
        if t < 12:
            gather_first(*items[t])
        if t == 0:
            for step in range(1, 4):
                c = (z + step) % 4
                go(Link(cot_in.at[pl.ds(pl.multiple_of(c * 128, 128), 128), :], got_g.at[z],
                        cot_s.at[step], cot_r.at[z], row, c))
        if 1 <= t < 13:
            gather_second(*items[t - 1])
        if 2 <= t < 14:
            gather_third(*items[t - 2])

    def take_tokens():
        for c in range(4):
            low, size, to = window(c)

            @pl.when(z == c)
            def _():
                got_x[c, to : to + size, :] = tok_in[low : low + size, :]
                for other in range(4):
                    if other != c:
                        arrived(at_rows(got_x, other, to, size), tok_r.at[other], row, other)

        @pl.when(low_end)
        def _():
            for other in range(4):
                arrived(at_rows(got_x, other, 0, 32), tok_rl.at[other], row - 1, other)

        @pl.when(high_end)
        def _():
            for other in range(4):
                arrived(at_rows(got_x, other, 160, 32), tok_rr.at[other], row + 1, other)

        @pl.when((z == 0) & (row == 0))
        def _():
            got_x[:, 0:32, :] = jnp.zeros((4, 32, 384), BF)

        @pl.when((z == 3) & (row == 7))
        def _():
            got_x[:, 160:192, :] = jnp.zeros((4, 32, 384), BF)

        got_gain[pl.ds(z, 1)] = gains_in[...][None]
        for step in range(1, 4):
            c = (z + step) % 4
            arrived(got_gain.at[c], gn_r.at[c], row, c)
        at = 0
        for low, high, lane in ((32, 160, 0), (32, 160, 192), (0, 32, 0), (0, 32, 192),
                                (160, 192, 0), (160, 192, 192)):
            x_all[at : at + high - low, :] = jnp.concatenate(
                [got_x[c, low:high, lane : lane + 192].astype(F32) for c in range(4)], axis=1)
            at += high - low

    def gain_row(which):
        return jnp.concatenate([got_gain[c, which : which + 1, 0:192] for c in range(4)], axis=1)

    def tables():
        spot = lax.broadcasted_iota(jnp.int32, (EXT, 128), 0)
        halo = spot - 256
        place = jnp.where(
            spot < 128, 2 * spot, jnp.where(
                spot < 256, 2 * spot - 255, jnp.where(
                    halo < 32, 2 * halo - 64, jnp.where(
                        halo < 64, 2 * halo - 127, jnp.where(
                            halo < 96, 2 * halo + 128, 2 * halo + 65)))))
        first, length = start_of(row, z)
        place = (place + first + length) % length
        angle = place.astype(F32) * freq_in[0:1, :]
        cos_t[...] = jnp.cos(angle)
        turn = jnp.where((lane_iota((EXT, 128)) % 64) < 32, -1.0, 1.0)
        sin_t[...] = jnp.sin(angle) * turn
        qrow = lax.broadcasted_iota(jnp.int32, (OWN, EXT), 0)
        qplace = jnp.where(qrow < 128, 2 * qrow, 2 * qrow - 255)
        kcol = lane_iota((OWN, EXT))
        khalo = kcol - 256
        kplace = jnp.where(
            kcol < 128, 2 * kcol, jnp.where(
                kcol < 256, 2 * kcol - 255, jnp.where(
                    khalo < 32, 2 * khalo - 64, jnp.where(
                        khalo < 64, 2 * khalo - 127, jnp.where(
                            khalo < 96, 2 * khalo + 128, 2 * khalo + 65)))))
        allowed = (jnp.abs(qplace - kplace) <= HALF) & (qid_in[...] == kid_in[...])
        bias[...] = jnp.where(allowed, 0.0, -1e30)

    def statistics(v):
        mu = jnp.mean(v, axis=1, keepdims=True)
        inv = lax.rsqrt(jnp.mean(v * v, axis=1, keepdims=True) - mu * mu + EPSILON)
        return (v - mu) * inv, inv

    def norm_one():
        hat, inv = statistics(x_all[0:OWN, :])
        hat1[...] = hat
        stat[0] = jnp.broadcast_to(inv, (OWN, 128))
        gain = gain_row(0)
        n1[0:OWN, :] = (hat * gain).astype(BF)
        hat, _ = statistics(x_all[OWN:EXT, :])
        n1[OWN:EXT, :] = (hat * gain).astype(BF)

    def take_cotangent():
        got_g[pl.ds(z, 1)] = cot_in[pl.ds(pl.multiple_of(z * 128, 128), 128), :][None]
        for step in range(1, 4):
            c = (z + step) % 4
            arrived(got_g.at[c], cot_r.at[c], row, c)
        pad = jnp.zeros((128, 64), BF)
        for c in range(4):
            for odd in range(2):
                cot_pad[128 * odd : 128 * odd + 128, 256 * c : 256 * c + 256] = jnp.concatenate(
                    [got_g[c, :, 192 * odd : 192 * odd + 192], pad], axis=1)

    low_lanes = lambda shape: lane_iota(shape) < 64

    def forward_heads(c):
        proj = dot(n1[...], w1[c, :, 0:640])
        cos, sin = cos_t[...], sin_t[...]
        rot = lambda tile, n: tile * cos[0:n] + swap_halves(tile) * sin[0:n]
        qs[c, 0] = (rot(proj[0:OWN, 0:128], OWN) * 0.125).astype(BF)
        ks[c, 0] = rot(proj[:, 128:256], EXT).astype(BF)
        vs[c, 0] = proj[:, 256:384].astype(BF)
        third = rot(proj[:, 384:512], EXT)
        low = low_lanes((EXT, 128))
        qs[c, 1] = jnp.where(low[0:OWN], third[0:OWN] * 0.125, 0.0).astype(BF)
        ks[c, 1] = jnp.where(low, pltpu.roll(third, 64, 1), 0.0).astype(BF)
        vs[c, 1] = jnp.where(low, proj[:, 512:640], 0.0).astype(BF)

        def head(h, q, k):
            scores = dot_nt(q, k) + bias[...]
            weight = jnp.exp(scores - jnp.max(scores, axis=1, keepdims=True))
            weight = weight * (1.0 / jnp.sum(weight, axis=1, keepdims=True))
            probs[3 * c + h] = weight
            return weight.astype(BF)

        zero = jnp.zeros((), BF)
        lowq, lowk = low_lanes((OWN, 128)), low
        q, k, v = qs[c, 0], ks[c, 0], vs[c, 0]
        both = dot(head(0, jnp.where(lowq, q, zero), k), jnp.where(lowk, v, zero))
        both += dot(head(1, jnp.where(lowq, zero, q), k), jnp.where(lowk, zero, v))
        att[:, 192 * c : 192 * c + 128] = both.astype(BF)
        one = dot(head(2, qs[c, 1], ks[c, 1]), vs[c, 1])
        att[:, 192 * c + 128 : 192 * c + 192] = one[:, 0:64].astype(BF)

    def forward_middle():
        for c in range(4):
            out = dot(att[...], w1[c, :, 512:768])
            mid[:, 192 * c : 192 * c + 192] = (
                x_all[0:OWN, 192 * c : 192 * c + 192] + out[:, 64:256])
        hat, inv = statistics(mid[...])
        hat2[...] = hat
        stat[1] = jnp.broadcast_to(inv, (OWN, 128))
        n2[...] = (hat * gain_row(1)).astype(BF)

    def gelu_parts(g):
        phi = 0.5 * (1.0 + lax.erf(g * 0.7071067811865476))
        return g * phi, phi + g * (jnp.exp(g * g * -0.5) * 0.3989422804014327)

    def forward_hidden(c):
        both = dot(n2[...], w2[c])
        value, slope = gelu_parts(both[:, 0:256])
        other = both[:, 256:512]
        gel[c] = value
        gel_up[c] = other * slope
        hid[c] = (value * other).astype(BF)

    def forward_tail():
        for c in range(4):
            for r in range(8):
                tail_in[96 * r : 96 * r + 96, 128 * c : 128 * c + 128] = (
                    w3[c, 144 * r : 144 * r + 96, 128:256])
                if r < 4:
                    tail_down[c, 32 * r : 32 * r + 32, :] = (
                        w3[c, 288 * r + 256 : 288 * r + 288, :])
        tails = dot(n2[...], tail_in[...])
        lanes = lane_iota((OWN, 128)) // 32
        packed = jnp.zeros((OWN, 128), F32)
        for c in range(4):
            tile = tails[:, 128 * c : 128 * c + 128]
            value, slope = gelu_parts(tile)
            other = pltpu.roll(tile, 96, 1)
            gel_t[c] = value
            gel_up_t[c] = other * slope
            moved = pltpu.roll(value * other, (32 * c + 64) % 128, 1)
            packed = jnp.where(lanes == c, moved, packed)
        hid_tail[...] = packed.astype(BF)

    def forward_mixed():
        for k in range(4):
            total = dot(hid_tail[...], tail_down[k])
            for c in range(4):
                total += dot(hid[c], w3[k, 288 * c : 288 * c + 256, :])
            out = (mid[:, 192 * k : 192 * k + 192] + total[:, 0:192]).astype(BF)
            mixed_send[k] = jnp.concatenate([out[0:128], out[128:256]], axis=1)
        for step in range(1, 4):
            c = (z + step) % 4
            go(Link(mixed_send.at[c], mixed_got.at[z], mx_s.at[step], mx_r.at[z], row, c))

    def backward_hidden(c):
        grad = dot_nt(cot_pad[:, 0:256], w3[0, 288 * c : 288 * c + 256, :])
        for k in range(1, 4):
            grad += dot_nt(cot_pad[:, 256 * k : 256 * k + 256], w3[k, 288 * c : 288 * c + 256, :])
        d_gate[c] = jnp.concatenate([grad * gel_up[c], grad * gel[c]], axis=1).astype(BF)

    def backward_tail():
        grad = dot_nt(cot_pad[:, 0:256], tail_down[0])
        for k in range(1, 4):
            grad += dot_nt(cot_pad[:, 256 * k : 256 * k + 256], tail_down[k])
        lanes = lane_iota((OWN, 128))
        for c in range(4):
            gate = pltpu.roll(grad, (64 - 32 * c) % 128, 1) * gel_up_t[c]
            other = pltpu.roll(grad, (96 - 32 * c) % 128, 1) * pltpu.roll(gel_t[c], 32, 1)
            d_tail[:, 128 * c : 128 * c + 128] = jnp.where(
                lanes >= 96, other, jnp.where(lanes >= 64, gate, 0.0)).astype(BF)

    def grad_down():
        for c in range(4):
            part = dot_tn(hid[c], cot_pad[...]).astype(BF)
            for k in range(4):
                d3[k, 288 * c : 288 * c + 256, :] = part[:, 256 * k : 256 * k + 256]
        part = dot_tn(hid_tail[...], cot_pad[...]).astype(BF)
        for c in range(4):
            for k in range(4):
                d3[k, 288 * c + 256 : 288 * c + 288, :] = (
                    part[32 * c : 32 * c + 32, 256 * k : 256 * k + 256])

    def grad_tail():
        part = dot_tn(n2[...], d_tail[...]).astype(BF)
        for c in range(4):
            for r in range(8):
                d3[c, 144 * r : 144 * r + 96, 128:256] = (
                    d3[c, 144 * r : 144 * r + 96, 128:256]
                    + part[96 * r : 96 * r + 96, 128 * c : 128 * c + 128])

    def grad_in(c):
        d2[c] = dot_tn(n2[...], d_gate[c]).astype(BF)

    def norm_back(grad, hat, inv, gain):
        e = grad * gain
        return inv * (e - jnp.mean(e, axis=1, keepdims=True)
                      - hat * jnp.mean(e * hat, axis=1, keepdims=True))

    def backward_middle():
        grad = dot_nt(d_tail[...], tail_in[...])
        for c in range(4):
            grad += dot_nt(d_gate[c], w2[c])
        hat = hat2[...]
        gain_part[1:2, :] = jnp.sum(grad * hat, axis=0, keepdims=True)
        back = norm_back(grad, hat, stat[1][:, 0:1], gain_row(1))
        pad = jnp.zeros((OWN, 64), BF)
        total = jnp.concatenate(
            [cot_pad[:, 256 * c : 256 * c + 192].astype(F32) for c in range(4)], axis=1) + back
        mid_grad[...] = total
        branch = total.astype(BF)
        for c in range(4):
            branch_pad[:, 256 * c : 256 * c + 256] = jnp.concatenate(
                [pad, branch[:, 192 * c : 192 * c + 192]], axis=1)
        grad = dot_nt(branch_pad[:, 0:256], w1[0, :, 512:768])
        for c in range(1, 4):
            grad += dot_nt(branch_pad[:, 256 * c : 256 * c + 256], w1[c, :, 512:768])
        att_grad[...] = grad.astype(BF)

    def grad_out():
        part = dot_tn(att[...], branch_pad[...]).astype(BF)
        for c in range(4):
            d1[c, :, 512:768] = part[:, 256 * c : 256 * c + 256]

    def backward_heads(c):
        zero = jnp.zeros((), BF)
        lowq, lowk = low_lanes((OWN, 128)), low_lanes((EXT, 128))

        def head(h, g, v):
            weight = probs[3 * c + h]
            prob_grad = dot_nt(g, v)
            inner = jnp.sum(weight * prob_grad, axis=1, keepdims=True)
            return (weight * (prob_grad - inner)).astype(BF), weight.astype(BF)

        q, k, v = qs[c, 0], ks[c, 0], vs[c, 0]
        g = att_grad[:, 192 * c : 192 * c + 128]
        g0, g1 = jnp.where(lowq, g, zero), jnp.where(lowq, zero, g)
        s0, p0 = head(0, g0, v)
        s1, p1 = head(1, g1, v)
        dq = dot(s0, jnp.where(lowk, k, zero)) + dot(s1, jnp.where(lowk, zero, k))
        dk = dot_tn(s0, jnp.where(lowq, q, zero)) + dot_tn(s1, jnp.where(lowq, zero, q))
        dv = dot_tn(p0, g0) + dot_tn(p1, g1)
        g2 = jnp.concatenate(
            [att_grad[:, 192 * c + 128 : 192 * c + 192], jnp.zeros((OWN, 64), BF)], axis=1)
        s2, p2 = head(2, g2, vs[c, 1])
        dq2 = dot(s2, ks[c, 1]) * 0.125
        dk2 = pltpu.roll(dot_tn(s2, qs[c, 1]), 64, 1)
        dv2 = dot_tn(p2, g2)
        cos, sin = cos_t[...], sin_t[...]
        back = lambda tile: tile * cos - swap_halves(tile) * sin
        none = jnp.zeros((EXT - OWN, 128), F32)
        dq = jnp.concatenate([dq * 0.125, none], axis=0)
        d_proj[c, :, 0:128] = back(dq).astype(BF)
        d_proj[c, :, 128:256] = back(dk).astype(BF)
        d_proj[c, :, 256:384] = dv.astype(BF)
        d_proj[c, :, 384:512] = back(jnp.concatenate([dq2, none], axis=0) + dk2).astype(BF)
        d_proj[c, :, 512:640] = dv2.astype(BF)

    def grad_qkv(c):
        part = dot_tn(n1[...], d_proj[c]).astype(BF)
        d1[c, :, 0:512] = part[:, 0:512]
        d1[c, :, 512:640] = d1[c, :, 512:640] + part[:, 512:640]

    def backward_first():
        grad = dot_nt(d_proj[0], w1[0, :, 0:640])
        for c in range(1, 4):
            grad += dot_nt(d_proj[c], w1[c, :, 0:640])
        n1_grad[...] = grad[0:OWN]
        halo_out[...] = grad[OWN:EXT].astype(BF)

    edge_low, edge_high = (z == 0) & (row == 0), (z == 3) & (row == 7)
    left_row = jnp.where(z == 0, row - 1, row)
    right_row = jnp.where(z == 3, row + 1, row)
    left_col, right_col = (z + 3) % 4, (z + 1) % 4

    def halo_send():
        go(Link(halo_out.at[pl.ds(0, 64), :], halo_right, ha_s.at[0], ha_r.at[1],
                left_row, left_col, jnp.logical_not(edge_low)))
        go(Link(halo_out.at[pl.ds(64, 64), :], halo_left, ha_s.at[1], ha_r.at[0],
                right_row, right_col, jnp.logical_not(edge_high)))

    def halo_take():
        @pl.when(jnp.logical_not(edge_low))
        def _():
            arrived(halo_left, ha_r.at[0], left_row, left_col)
            n1_grad[0:32, :] += halo_left[0:32, :].astype(F32)
            n1_grad[128:160, :] += halo_left[32:64, :].astype(F32)

        @pl.when(jnp.logical_not(edge_high))
        def _():
            arrived(halo_right, ha_r.at[1], right_row, right_col)
            n1_grad[96:128, :] += halo_right[0:32, :].astype(F32)
            n1_grad[224:256, :] += halo_right[32:64, :].astype(F32)

    def backward_last():
        grad, hat = n1_grad[...], hat1[...]
        gain_part[0:1, :] = jnp.sum(grad * hat, axis=0, keepdims=True)
        total = mid_grad[...] + norm_back(grad, hat, stat[0][:, 0:1], gain_row(0))
        out = total.astype(BF)
        for k in range(4):
            mine = out[:, 192 * k : 192 * k + 192]
            input_send[k] = jnp.concatenate([mine[0:128], mine[128:256]], axis=1)
        for step in range(1, 4):
            c = (z + step) % 4
            go(Link(input_send.at[c], input_got.at[z], ig_s.at[step], ig_r.at[z], row, c))
        for c in range(4):
            gain_part_c = gain_part[0:2, 192 * c : 192 * c + 192]
            gain_sum[c, 0:2, 0:192] = gain_part_c
        for step in range(1, 4):
            c = (z + step) % 4
            go(Link(gain_sum.at[c], gain_z.at[z], gz_s.at[step], gz_r.at[z], row, c))

    cores = (core1, core2, core3)
    xas, xbs, yas, ybs = (xa1, xa2, xa3), (xb1, xb2, xb3), (ya1, ya2, ya3), (yb1, yb2, yb3)
    zls, zrs = (zl1, zl2, zl3), (zr1, zr2, zr3)
    outs = (grad_one, grad_two, grad_three)

    def place(i, c, r, part):
        size, cut = ROWS[i], SPLIT[i]
        start, count = {"all": (0, size), "a": (0, cut), "b": (cut, size - cut)}[part]
        return c, pl.ds(pl.multiple_of(r * size + start, 16), count)

    def piece(i, c, r, part):
        lead, span = place(i, c, r, part)
        return ds_[i].at[lead, span, :]

    def add_into(i, c, r, part, value):
        lead, span = place(i, c, r, part)
        ds_[i][lead, span, :] = ds_[i][lead, span, :] + value

    def sum_first(i, j):
        c = order[3 - j]
        for n in range(4):
            go(Link(piece(i, c, 2 * n + 1 - core, "all"), cores[i].at[c, n],
                    rc_s.at[i, c, n], rc_r.at[i, c, n], rc, z))

    def sum_second(i, j):
        c = order[3 - j]
        for n in range(4):
            arrived(cores[i].at[c, n], rc_r.at[i, c, n], rc, z)
            add_into(i, c, 2 * n + core, "all", cores[i][c, n])
        for y in range(2):
            go(Link(piece(i, c, 4 * y + 2 * (1 - xc) + core, "a"), xas[i].at[c, y],
                    rx_s.at[i, c, y], rx_r.at[i, c, y], rx, z))
        for x in range(2):
            go(Link(piece(i, c, 4 * (1 - yc) + 2 * x + core, "b"), ybs[i].at[c, x],
                    ry_s.at[i, c, x], ry_r.at[i, c, x], ry, z))

    def sum_third(i, j):
        c = order[3 - j]
        for y in range(2):
            arrived(xas[i].at[c, y], rx_r.at[i, c, y], rx, z)
            add_into(i, c, 4 * y + 2 * xc + core, "a", xas[i][c, y])
        go(Link(piece(i, c, ry, "a"), yas[i].at[c], ry_s.at[i, c, 2], ry_r.at[i, c, 2], ry, z))
        for x in range(2):
            arrived(ybs[i].at[c, x], ry_r.at[i, c, x], ry, z)
            add_into(i, c, 4 * yc + 2 * x + core, "b", ybs[i][c, x])
        go(Link(piece(i, c, rx, "b"), xbs[i].at[c], rx_s.at[i, c, 2], rx_r.at[i, c, 2], rx, z))

    def sum_fourth(i, j):
        c = order[3 - j]
        arrived(yas[i].at[c], ry_r.at[i, c, 2], ry, z)
        add_into(i, c, row, "a", yas[i][c])
        arrived(xbs[i].at[c], rx_r.at[i, c, 2], rx, z)
        add_into(i, c, row, "b", xbs[i][c])

        @pl.when((c > z) & (z > 0))
        def _():
            arrived(zls[i].at[c], rz_r.at[i, 0, c], row, z - 1)
            add_into(i, c, row, "all", zls[i][c])

        @pl.when((c < z) & (z < 3))
        def _():
            arrived(zrs[i].at[c], rz_r.at[i, 1, c], row, z + 1)
            add_into(i, c, row, "all", zrs[i][c])

        go(Link(piece(i, c, row, "all"), zls[i].at[c], rz_s.at[i, 0, c], rz_r.at[i, 0, c],
                row, z + 1, c > z))
        go(Link(piece(i, c, row, "all"), zrs[i].at[c], rz_s.at[i, 1, c], rz_r.at[i, 1, c],
                row, z - 1, c < z))

    def sum_last(i):
        lead, span = place(i, z, row, "all")
        outs[i][...] = ds_[i][lead, span, :].astype(F32)

        @pl.when(z > 0)
        def _():
            arrived(zls[i].at[z], rz_r.at[i, 0, z], row, z - 1)
            outs[i][...] = outs[i][...] + zls[i][z].astype(F32)

        @pl.when(z < 3)
        def _():
            arrived(zrs[i].at[z], rz_r.at[i, 1, z], row, z + 1)
            outs[i][...] = outs[i][...] + zrs[i][z].astype(F32)

    def sum_step(t, queue):
        for lag, step in enumerate((sum_first, sum_second, sum_third, sum_fourth)):
            if 0 <= t - lag < len(queue):
                step(*queue[t - lag])

    def gains_first():
        gain_z[pl.ds(z, 1)] = gain_sum[pl.ds(z, 1)]
        for step in range(1, 4):
            c = (z + step) % 4
            arrived(gain_z.at[c], gz_r.at[c], row, c)
        gain_all[pl.ds(row, 1)] = (gain_z[0] + gain_z[1] + gain_z[2] + gain_z[3])[None]
        for step in range(1, 8):
            go(Link(gain_all.at[row], gain_all.at[row], gp_s.at[step], gp_r.at[row],
                    (row + step) % 8, z))

    def gains_last():
        for step in range(1, 8):
            r = (row + step) % 8
            arrived(gain_all.at[r], gp_r.at[r], r, z)
        total = gain_all[0]
        for r in range(1, 8):
            total = total + gain_all[r]
        gains_out[...] = total

    def finish(out_ref, send, got, sems):
        got[pl.ds(z, 1)] = send[pl.ds(z, 1)]
        for step in range(1, 4):
            c = (z + step) % 4
            arrived(got.at[c], sems.at[c], row, c)
        for c in range(4):
            out_ref[128 * c : 128 * c + 128, :] = got[c].astype(out_ref.dtype)

    gather_step(0)
    tables()
    take_tokens()
    norm_one()
    for t in range(1, 14):
        gather_step(t)
    gather_done(0)
    for c in range(4):
        forward_heads(c)
    forward_middle()
    gather_done(1)
    for c in range(4):
        forward_hidden(c)
    gather_done(2)
    forward_tail()
    take_cotangent()
    forward_mixed()
    for c in range(4):
        backward_hidden(c)
    backward_tail()
    grad_down()
    grad_tail()
    for c in range(4):
        grad_in(c)
    backward_middle()
    grad_out()
    for c in range(4):
        backward_heads(c)
        grad_qkv(c)
    backward_first()
    halo_send()
    queue = [(i, j) for i in (2, 1, 0) for j in range(4)]
    for t in range(5):
        sum_step(t, queue)
    halo_take()
    backward_last()
    for t in range(5, 8):
        sum_step(t, queue)
    gains_first()
    for t in range(8, 15):
        sum_step(t, queue)
    for i in (2, 1, 0):
        sum_last(i)
    gains_last()
    finish(mixed_out, mixed_send, mixed_got, mx_r)
    finish(input_out, input_send, input_got, ig_r)
    for link in sent:
        link.sent()


def fast_local(
    tokens, segment_ids, gain_one, qkv_weight, out_weight, gain_two, in_weight, down_weight,
    cotangent,
):
    rows_all = tokens.shape[1] * 2 * lax.axis_size("row")
    row, z = lax.axis_index("row"), lax.axis_index("col")
    length = min(SEQ_MAX, rows_all)

    def start_of(row, z):
        return (row * 4 + z) * OWN, length

    places = np.arange(rows_all + 2 * HALF, dtype=np.int32) - HALF
    ids = jnp.pad(segment_ids, HALF, constant_values=-1) + jnp.asarray(places // length) * 65536
    ids = lax.dynamic_slice_in_dim(ids, (row * 4 + z) * OWN, EXT).reshape(EXT // 2, 2).T
    ids = jnp.concatenate(
        [ids[0, 32:160], ids[1, 32:160], ids[0, :32], ids[1, :32], ids[0, 160:], ids[1, 160:]])
    frequency = 10000.0 ** (-(np.arange(HEAD_DIM // 2) * 2.0) / HEAD_DIM)
    frequency = jnp.asarray(np.tile(frequency.astype(np.float32), 4)[None, :].repeat(8, 0))
    q, k, v = (qkv_weight[:, s] for s in range(3))
    one = jnp.concatenate(
        [q[:, :128], k[:, :128], v[:, :128], q[:, 128:], k[:, 128:], v[:, 128:], out_weight], 1)
    two = jnp.concatenate([in_weight[:, 0, :256], in_weight[:, 1, :256]], 1)
    tail = jnp.concatenate([in_weight[:, 0, 256:], in_weight[:, 1, 256:]], 1)
    three = jnp.concatenate([down_weight, jnp.pad(tail, ((0, 48), (0, 0)))], 1)
    gains = jnp.pad(jnp.stack([gain_one, gain_two]), ((0, 6), (0, 64)))
    vmem, dma = pltpu.VMEM, pltpu.SemaphoreType.DMA
    shapes = [
        vmem((4, 192, 384), BF), vmem((4, 128, 384), BF), vmem((4, 8, 256), F32),
        vmem((4, 768, 768), BF), vmem((4, 768, 512), BF), vmem((4, 1152, 256), BF),
        vmem((4, 768, 768), BF), vmem((4, 768, 512), BF), vmem((4, 1152, 256), BF),
    ]
    shapes += [vmem((4, 4, ROWS[i], COLS[i]), BF) for i in range(3)]
    shapes += [vmem((4, 2, SPLIT[i], COLS[i]), BF) for i in range(3)]
    shapes += [vmem((4, ROWS[i] - SPLIT[i], COLS[i]), BF) for i in range(3)]
    shapes += [vmem((4, SPLIT[i], COLS[i]), BF) for i in range(3)]
    shapes += [vmem((4, 2, ROWS[i] - SPLIT[i], COLS[i]), BF) for i in range(3)]
    shapes += [vmem((4, ROWS[i], COLS[i]), BF) for i in range(3)] * 2
    shapes += [
        vmem((EXT, 768), F32), vmem((EXT, 128), F32), vmem((EXT, 128), F32),
        vmem((OWN, EXT), F32), vmem((EXT, 768), BF), vmem((OWN, 768), F32),
        vmem((2, OWN, 128), F32), vmem((4, 2, OWN, 128), BF), vmem((4, 2, EXT, 128), BF),
        vmem((4, 2, EXT, 128), BF), vmem((12, OWN, EXT), F32), vmem((OWN, 768), BF),
        vmem((OWN, 768), F32), vmem((OWN, 768), F32), vmem((OWN, 768), BF),
        vmem((768, 512), BF), vmem((4, 128, 256), BF), vmem((4, OWN, 256), BF),
        vmem((OWN, 128), BF), vmem((4, OWN, 256), F32), vmem((4, OWN, 256), F32),
        vmem((4, OWN, 128), F32), vmem((4, OWN, 128), F32), vmem((OWN, 1024), BF),
        vmem((4, OWN, 512), BF), vmem((OWN, 512), BF),
        vmem((OWN, 768), F32), vmem((OWN, 1024), BF), vmem((OWN, 768), BF),
        vmem((4, EXT, 640), BF), vmem((OWN, 768), F32),
        vmem((128, 768), BF), vmem((64, 768), BF), vmem((64, 768), BF),
        vmem((4, 128, 384), BF), vmem((4, 128, 384), BF),
        vmem((4, 128, 384), BF), vmem((4, 128, 384), BF),
        vmem((8, 768), F32), vmem((4, 8, 256), F32), vmem((4, 8, 256), F32),
        vmem((8, 8, 256), F32),
        dma((6,)), dma((4,)), dma((4,)), dma((4,)), dma((4,)), dma((4,)), dma((4,)), dma((4,)),
        dma((3, 2, 4)), dma((3, 4)), dma((3, 4, 3)), dma((3, 4, 3)), dma((3, 4, 3)),
        dma((3, 4, 3)), dma((3, 4, 4)), dma((3, 4, 4)),
        dma((3, 4, 4)), dma((3, 4, 4)), dma((3, 4, 3)), dma((3, 4, 3)), dma((3, 4, 3)),
        dma((3, 4, 3)), dma((3, 2, 4)), dma((3, 2, 4)),
        dma((2,)), dma((2,)), dma((4,)), dma((4,)), dma((4,)), dma((4,)), dma((4,)), dma((4,)),
        dma((8,)), dma((8,)),
    ]
    whole = pl.BlockSpec(memory_space=pltpu.VMEM)
    mixed, input_grad, one_g, two_g, three_g, gains_g = pl.pallas_call(
        functools.partial(layer_kernel, start_of=start_of),
        out_shape=(
            jax.ShapeDtypeStruct((512, 384), BF), jax.ShapeDtypeStruct((512, 384), F32),
            jax.ShapeDtypeStruct((96, 768), F32), jax.ShapeDtypeStruct((96, 512), F32),
            jax.ShapeDtypeStruct((144, 256), F32), jax.ShapeDtypeStruct((8, 256), F32),
        ),
        in_specs=[whole] * 9,
        out_specs=(whole,) * 6,
        scratch_shapes=shapes,
        compiler_params=pltpu.CompilerParams(
            collective_id=0, has_side_effects=True, vmem_limit_bytes=62 * 1024 * 1024),
    )(tokens[0], cotangent[0], one, two, three, gains, ids[:OWN, None], ids[None, :], frequency)
    qkv_grad = jnp.stack(
        [jnp.concatenate([one_g[:, 128 * s : 128 * s + 128],
                          one_g[:, 384 + 64 * s : 448 + 64 * s]], 1) for s in range(3)], 1)
    in_grad = jnp.stack(
        [jnp.concatenate([two_g[:, 256 * s : 256 * s + 256],
                          three_g[:96, 192 + 32 * s : 224 + 32 * s]], 1) for s in range(2)], 1)
    return (
        mixed[None], input_grad[None], gains_g[0, :192], qkv_grad, one_g[:, 576:],
        gains_g[1, :192], in_grad, three_g[:, :192],
    )


def solution(mesh):
    placed = (
        P("col", "row", None),
        P(),
        P("col"),
        P("row", None, "col"),
        P("row", "col"),
        P("col"),
        P("row", None, "col"),
        P("row", "col"),
        P("col", "row", None),
    )
    part = local
    if mesh.shape["row"] == 8 and mesh.shape["col"] == 4:
        part = fast_local
    return jax.shard_map(
        part,
        mesh=mesh,
        in_specs=placed,
        out_specs=(
            P("col", "row", None),
            P("col", "row", None),
            P("col"),
            P("row", None, "col"),
            P("row", "col"),
            P("col"),
            P("row", None, "col"),
            P("row", "col"),
        ),
        check_vma=False,
    )
```

```python
import functools

import jax
import jax.numpy as jnp
import numpy as np
from jax import lax
from jax.experimental import pallas as pl
from jax.experimental.pallas import tpu as pltpu
from jax.sharding import PartitionSpec as P

HEAD_DIM = 64
WINDOW = 128
SEQ_MAX = 4096


EPSILON = 1e-05


def with_halo(block, sides, width):
    for axis, dim in sides:
        count = lax.axis_size(axis)
        forward = [(i, i + 1) for i in range(count - 1)]
        backward = [(target, source) for source, target in forward]
        low = lax.ppermute(
            lax.slice_in_dim(block, block.shape[dim] - width, None, axis=dim), axis, forward
        )
        high = lax.ppermute(lax.slice_in_dim(block, 0, width, axis=dim), axis, backward)
        block = jnp.concatenate([low, block, high], axis=dim)
    return block


def rotate(values, cosine, sine_table):
    half_dim = values.shape[-1] // 2
    turned = jnp.concatenate([-values[..., half_dim:], values[..., :half_dim]], axis=-1)
    return values * cosine + turned * sine_table


def rotate_back(grad_rows, cosine, sine_table):
    half_dim = grad_rows.shape[-1] // 2
    turned = jnp.concatenate([-grad_rows[..., half_dim:], grad_rows[..., :half_dim]], axis=-1)
    return grad_rows * cosine - turned * sine_table


def spread(values):
    return lax.all_gather(values, "col", axis=1, tiled=True)


def collect(partial_rows):
    return lax.psum_scatter(partial_rows, "col", scatter_dimension=1, tiled=True)


def norm_forward(values, full_width):
    row_sums = lax.psum((jnp.sum(values, axis=1), jnp.sum(values * values, axis=1)), "col")
    mean_value = row_sums[0] / full_width
    variance = row_sums[1] / full_width - mean_value * mean_value
    inverse = lax.rsqrt(variance + EPSILON)
    return ((values - mean_value[:, None]) * inverse[:, None], inverse)


def norm_backward(grad_rows, scaled, inverse, gain_part, full_width):
    weighted = grad_rows * gain_part
    row_sums = lax.psum((jnp.sum(weighted, axis=1), jnp.sum(weighted * scaled, axis=1)), "col")
    input_part = inverse[:, None] * (
        weighted - row_sums[0][:, None] / full_width - scaled * (row_sums[1][:, None] / full_width)
    )
    return (input_part, jnp.sum(grad_rows * scaled, axis=0))


def geglu(gate_up):
    return jax.nn.gelu(gate_up[:, 0], approximate=False) * gate_up[:, 1]


def local(
    tokens,
    segment_ids,
    gain_one,
    qkv_weight,
    out_weight,
    gain_two,
    in_weight,
    down_weight,
    cotangent,
):
    pair_rows = tokens.shape[1]
    rows_here = pair_rows * 2
    tok_width = tokens.shape[2] // 2
    full_width = tok_width * lax.axis_size("col")
    heads_here = qkv_weight.shape[2] // HEAD_DIM
    head_width = heads_here * HEAD_DIM
    half_window = WINDOW // 2
    block_rows = min(512, rows_here)
    block_count = rows_here // block_rows
    key_span = block_rows + 2 * half_window
    score_scale = HEAD_DIM ** (-0.5)
    length = min(SEQ_MAX, rows_here * lax.axis_size("row"))
    first_row = lax.axis_index("row") * rows_here
    grad_rows = cotangent.reshape(rows_here, tok_width)
    qkv_full, out_full, in_full, down_full = (
        lax.all_gather(qkv_weight, "row", axis=0, tiled=True),
        lax.all_gather(out_weight, "row", axis=0, tiled=True),
        lax.all_gather(in_weight, "row", axis=0, tiled=True),
        lax.all_gather(down_weight, "row", axis=0, tiled=True),
    )
    global_rows = first_row + jnp.arange(rows_here, dtype=jnp.int32)
    places = (global_rows % length).astype(jnp.float32)
    frequencies = 10000.0 ** (-(jnp.arange(HEAD_DIM // 2, dtype=jnp.float32) * 2.0) / HEAD_DIM)
    angles = places[:, None] * frequencies[None, :]
    angles = jnp.concatenate([angles, angles], axis=1)[:, None, :]
    cosine = jnp.cos(angles)
    sine_table = jnp.sin(angles)
    query_ids = lax.dynamic_slice_in_dim(segment_ids, first_row, rows_here)
    padded_ids = jnp.pad(segment_ids, half_window, constant_values=-1)
    key_ids = lax.dynamic_slice_in_dim(padded_ids, first_row, rows_here + 2 * half_window)
    query_seqs = global_rows // length
    key_seqs = (
        first_row - half_window + jnp.arange(rows_here + 2 * half_window, dtype=jnp.int32)
    ) // length
    offsets = (
        jnp.arange(key_span, dtype=jnp.int32)[None, :]
        - half_window
        - jnp.arange(block_rows, dtype=jnp.int32)[:, None]
    )
    in_window = jnp.abs(offsets) <= half_window

    def block_scores(block_start, block_queries, block_keys):
        same_doc = (
            query_ids[block_start : block_start + block_rows, None]
            == key_ids[None, block_start : block_start + key_span]
        )
        same_seq = (
            query_seqs[block_start : block_start + block_rows, None]
            == key_seqs[None, block_start : block_start + key_span]
        )
        allowed = in_window & same_doc & same_seq
        scores = (
            jnp.einsum(
                "qhd,khd->hqk", block_queries, block_keys, preferred_element_type=jnp.float32
            )
            * score_scale
        )
        return jnp.where(allowed[None], scores, -1e30)

    token_values = tokens.reshape(rows_here, tok_width).astype(jnp.float32)
    scaled_one, inverse_one = norm_forward(token_values, full_width)
    normed_one_full = spread((scaled_one * gain_one).astype(jnp.bfloat16))
    projected = jnp.einsum(
        "td,dsf->tsf", normed_one_full, qkv_full, preferred_element_type=jnp.float32
    )
    projected = projected.reshape(rows_here, 3, heads_here, HEAD_DIM)
    queries = rotate(projected[:, 0], cosine, sine_table).astype(jnp.bfloat16)
    key_rows = rotate(projected[:, 1], cosine, sine_table).astype(jnp.bfloat16)
    value_rows = projected[:, 2].astype(jnp.bfloat16)
    key_value = jnp.concatenate(
        [key_rows.reshape(rows_here, head_width), value_rows.reshape(rows_here, head_width)], axis=1
    )
    padded_pair = with_halo(key_value, (("row", 0),), half_window)
    padded_keys = padded_pair[:, :head_width].reshape(
        rows_here + 2 * half_window, heads_here, HEAD_DIM
    )
    padded_values = padded_pair[:, head_width:].reshape(
        rows_here + 2 * half_window, heads_here, HEAD_DIM
    )
    output_blocks = []
    total_blocks = []
    for block_number in range(block_count):
        block_start = block_number * block_rows
        masked = block_scores(
            block_start,
            queries[block_start : block_start + block_rows],
            padded_keys[block_start : block_start + key_span],
        )
        largest = jnp.max(masked, axis=-1, keepdims=True)
        log_total = largest + jnp.log(jnp.sum(jnp.exp(masked - largest), axis=-1, keepdims=True))
        weights = jnp.exp(masked - log_total).astype(jnp.bfloat16)
        output_blocks.append(
            jnp.einsum(
                "hqk,khd->qhd",
                weights,
                padded_values[block_start : block_start + key_span],
                preferred_element_type=jnp.float32,
            )
        )
        total_blocks.append(log_total)
    attended = (
        jnp.concatenate(output_blocks, axis=0).reshape(rows_here, head_width).astype(jnp.bfloat16)
    )
    attended_full = spread(attended)
    middle = token_values + jnp.dot(attended_full, out_full, preferred_element_type=jnp.float32)
    scaled_two, inverse_two = norm_forward(middle, full_width)
    normed_two_full = spread((scaled_two * gain_two).astype(jnp.bfloat16))
    gate_up = jnp.einsum(
        "td,dsf->tsf", normed_two_full, in_full, preferred_element_type=jnp.float32
    )
    hidden_value, geglu_pull = jax.vjp(geglu, gate_up)
    hidden_full = spread(hidden_value.astype(jnp.bfloat16))
    mixed = (middle + jnp.dot(hidden_full, down_full, preferred_element_type=jnp.float32)).astype(
        jnp.bfloat16
    )
    qkv_back, out_back, in_back, down_back = (
        lax.all_gather(qkv_weight, "row", axis=0, tiled=True),
        lax.all_gather(out_weight, "row", axis=0, tiled=True),
        lax.all_gather(in_weight, "row", axis=0, tiled=True),
        lax.all_gather(down_weight, "row", axis=0, tiled=True),
    )
    down_part = jnp.einsum("tf,td->fd", hidden_full, grad_rows, preferred_element_type=jnp.float32)
    hidden_grad = collect(
        jnp.einsum("td,fd->tf", grad_rows, down_back, preferred_element_type=jnp.float32)
    )
    gate_up_grad = geglu_pull(hidden_grad)[0].astype(jnp.bfloat16)
    in_part = jnp.einsum(
        "td,tsf->dsf", normed_two_full, gate_up_grad, preferred_element_type=jnp.float32
    )
    normed_two_grad = collect(
        jnp.einsum("tsf,dsf->td", gate_up_grad, in_back, preferred_element_type=jnp.float32)
    )
    middle_norm_grad, gain_two_part = norm_backward(
        normed_two_grad, scaled_two, inverse_two, gain_two, full_width
    )
    middle_grad = grad_rows.astype(jnp.float32) + middle_norm_grad
    branch_grad = middle_grad.astype(jnp.bfloat16)
    out_part = jnp.einsum(
        "td,tf->df", attended_full, branch_grad, preferred_element_type=jnp.float32
    )
    attended_grad = collect(
        jnp.einsum("tf,df->td", branch_grad, out_back, preferred_element_type=jnp.float32)
    ).astype(jnp.bfloat16)
    attended_heads = attended_grad.reshape(rows_here, heads_here, HEAD_DIM)
    query_blocks = []
    key_grad_ext = jnp.zeros((rows_here + 2 * half_window, heads_here, HEAD_DIM), jnp.float32)
    value_grad_ext = jnp.zeros((rows_here + 2 * half_window, heads_here, HEAD_DIM), jnp.float32)
    for block_number in range(block_count):
        block_start = block_number * block_rows
        block_queries = queries[block_start : block_start + block_rows]
        block_keys = padded_keys[block_start : block_start + key_span]
        block_values = padded_values[block_start : block_start + key_span]
        block_grads = attended_heads[block_start : block_start + block_rows]
        masked = block_scores(block_start, block_queries, block_keys)
        probs = jnp.exp(masked - total_blocks[block_number])
        prob_grad = jnp.einsum(
            "qhd,khd->hqk", block_grads, block_values, preferred_element_type=jnp.float32
        )
        inner = jnp.sum(probs * prob_grad, axis=-1, keepdims=True)
        score_grad = (probs * (prob_grad - inner)).astype(jnp.bfloat16)
        query_blocks.append(
            jnp.einsum("hqk,khd->qhd", score_grad, block_keys, preferred_element_type=jnp.float32)
            * score_scale
        )
        key_grad_ext = key_grad_ext.at[block_start : block_start + key_span].add(
            jnp.einsum(
                "hqk,qhd->khd", score_grad, block_queries, preferred_element_type=jnp.float32
            )
            * score_scale
        )
        value_grad_ext = value_grad_ext.at[block_start : block_start + key_span].add(
            jnp.einsum(
                "hqk,qhd->khd",
                probs.astype(jnp.bfloat16),
                block_grads,
                preferred_element_type=jnp.float32,
            )
        )
    grad_pair = jnp.concatenate(
        [key_grad_ext.reshape(-1, head_width), value_grad_ext.reshape(-1, head_width)], axis=1
    )
    rim_rows = jnp.concatenate(
        [grad_pair[:half_window], grad_pair[rows_here + half_window :]], axis=0
    )
    beside_all = with_halo(rim_rows.astype(jnp.bfloat16), (("row", 0),), half_window).astype(
        rim_rows.dtype
    )
    own_grad = grad_pair[half_window : half_window + rows_here]
    own_grad = own_grad.at[:half_window].add(beside_all[:half_window])
    own_grad = own_grad.at[rows_here - half_window :].add(beside_all[3 * half_window :])
    key_grad = own_grad[:, :head_width].reshape(rows_here, heads_here, HEAD_DIM)
    value_grad = own_grad[:, head_width:].reshape(rows_here, heads_here, HEAD_DIM)
    query_grad = jnp.concatenate(query_blocks, axis=0)
    projected_grad = jnp.stack(
        [
            rotate_back(query_grad, cosine, sine_table),
            rotate_back(key_grad, cosine, sine_table),
            value_grad,
        ],
        axis=1,
    )
    projected_grad = projected_grad.reshape(rows_here, 3, head_width).astype(jnp.bfloat16)
    qkv_part = jnp.einsum(
        "td,tsf->dsf", normed_one_full, projected_grad, preferred_element_type=jnp.float32
    )
    normed_one_grad = collect(
        jnp.einsum("tsf,dsf->td", projected_grad, qkv_back, preferred_element_type=jnp.float32)
    )
    token_norm_grad, gain_one_part = norm_backward(
        normed_one_grad, scaled_one, inverse_one, gain_one, full_width
    )
    input_grad = middle_grad + token_norm_grad
    weight_grads = (
        lax.psum_scatter(qkv_part, "row", scatter_dimension=0, tiled=True),
        lax.psum_scatter(out_part, "row", scatter_dimension=0, tiled=True),
        lax.psum_scatter(in_part, "row", scatter_dimension=0, tiled=True),
        lax.psum_scatter(down_part, "row", scatter_dimension=0, tiled=True),
    )
    gain_grads = lax.psum((gain_one_part, gain_two_part), "row")
    mixed_out = mixed.reshape(1, pair_rows, 2 * tok_width)
    input_out = input_grad.reshape(1, pair_rows, 2 * tok_width)
    return (
        mixed_out,
        input_out,
        gain_grads[0],
        weight_grads[0],
        weight_grads[1],
        gain_grads[1],
        weight_grads[2],
        weight_grads[3],
    )


F32 = jnp.float32
BF = jnp.bfloat16
MESH = pl.DeviceIdType.MESH
ROWS = (96, 96, 144)
COLS = (768, 512, 256)
SPLIT = (48, 48, 64)
OWN = 256
EXT = 384
HALF = 64


def dot(a, b):
    return lax.dot_general(a, b, (((1,), (0,)), ((), ())), preferred_element_type=F32)


def dot_nt(a, b):
    return lax.dot_general(a, b, (((1,), (1,)), ((), ())), preferred_element_type=F32)


def dot_tn(a, b):
    return lax.dot_general(a, b, (((0,), (0,)), ((), ())), preferred_element_type=F32)


class Link:
    def __init__(self, src, dst, send, recv, row, col, when=None):
        self.args = (src, dst, send, recv)
        self.device = {"row": row, "col": col}
        self.when = when

    def make(self):
        src, dst, send, recv = self.args
        return pltpu.make_async_remote_copy(
            src_ref=src,
            dst_ref=dst,
            send_sem=send,
            recv_sem=recv,
            device_id=self.device,
            device_id_type=MESH,
        )

    def run(self, step):
        if self.when is None:
            step()
        else:
            pl.when(self.when)(step)

    def start(self):
        self.run(lambda: self.make().start())

    def sent(self):
        self.run(lambda: self.make().wait_send())


def arrived(dst, recv, row, col):
    pltpu.make_async_remote_copy(
        src_ref=dst,
        dst_ref=dst,
        send_sem=recv,
        recv_sem=recv,
        device_id={"row": row, "col": col},
        device_id_type=MESH,
    ).wait_recv()


def at_rows(ref, lead, start, size):
    return ref.at[lead, pl.ds(start, size), :]


def lane_iota(shape):
    return lax.broadcasted_iota(jnp.int32, shape, 1)


def swap_halves(tile):
    first = (lane_iota(tile.shape) % 64) < 32
    return jnp.where(first, pltpu.roll(tile, 96, 1), pltpu.roll(tile, 32, 1))


def layer_kernel(
    tok_in, cot_in, qkv_in, out_in, in_in, down_in, gain_one_in, gain_two_in, ids_in, freq_in,
    mixed_out, input_out, qkv_out, out_out, in_out, down_out, gain_one_out, gain_two_out,
    got_x, got_g, got_gain, w1, w2, w3, d1, d2, d3,
    core1, core2, core3, xa1, xa2, xa3, xb1, xb2, xb3, ya1, ya2, ya3, yb1, yb2, yb3,
    zl1, zl2, zl3, zr1, zr2, zr3,
    gains_in, own_ids, x_all, cos_t, sin_t, bias, n1, hat1, stat, qs, ks, vs, probs, att_c, att, mid, hat2, n2,
    tail_in, tail_down, hid, hid_tail, gel, gel_up, gel_t, gel_up_t, cot_pad, d_gate, d_tail,
    mid_grad, branch_pad, att_grad, d_proj, n1_grad,
    halo_out, halo_left, halo_right, mixed_send, mixed_got, input_send, input_got,
    gain_part, gain_z, gain_sum, gain_all, grad_one, grad_two, grad_three,
    tok_s, tok_r, tok_rl, tok_rr, cot_s, cot_r, gn_s, gn_r,
    az_s, az_r, ax_s, ax_r, ay_s, ay_r, ac_s, ac_r,
    rc_s, rc_r, rx_s, rx_r, ry_s, ry_r, rz_s, rz_r,
    io_s, ha_s, ha_r, mx_s, mx_r, ig_s, ig_r, gz_s, gz_r, gp_s, gp_r,
    *, start_of,
):
    row = lax.axis_index("row")
    z = lax.axis_index("col")
    core = row % 2
    xc = (row // 2) % 2
    yc = row // 4
    rx = row + 2 - 4 * xc
    ry = row + 4 - 8 * yc
    rxy = ry + 2 - 4 * xc
    rc = row + 1 - 2 * core
    ws = (w1, w2, w3)
    ds_ = (d1, d2, d3)
    sent = []

    def go(link):
        link.start()
        sent.append(link)

    barrier = pltpu.get_barrier_semaphore()

    def greet(r, c):
        pl.semaphore_signal(barrier, inc=1, device_id={"row": r, "col": c}, device_id_type=MESH)

    for step in range(1, 8):
        greet((row + step) % 8, z)
    for step in range(1, 4):
        greet(row, (z + step) % 4)
    up, down = row < 7, row > 0
    low_end, high_end = (z == 0) & down, (z == 3) & up
    pl.when(down)(lambda: greet(row - 1, 3))
    pl.when(up)(lambda: greet(row + 1, 0))

    @pl.when(low_end)
    def _():
        for c in range(4):
            greet(row - 1, c)

    @pl.when(high_end)
    def _():
        for c in range(4):
            greet(row + 1, c)

    peers = 10 + jnp.minimum(row, 1) + jnp.minimum(7 - row, 1)
    peers += 4 * jnp.maximum(1 - z, 0) * jnp.minimum(row, 1)
    peers += 4 * jnp.maximum(z - 2, 0) * jnp.minimum(7 - row, 1)
    def window(c):
        low, high = max(0, 128 * c - 32), min(512, 128 * c + 160)
        return low, high - low, low - (128 * c - 32)

    def send_tokens():
        for c in range(4):
            low, size, to = window(c)
            go(Link(tok_in.at[pl.ds(low, size), :], at_rows(got_x, z, to, size),
                    tok_s.at[c], tok_r.at[z], row, c, z != c))
        go(Link(tok_in.at[pl.ds(0, 32), :], at_rows(got_x, z, 160, 32),
                tok_s.at[4], tok_rr.at[z], row - 1, 3, down))
        go(Link(tok_in.at[pl.ds(480, 32), :], at_rows(got_x, z, 0, 32),
                tok_s.at[5], tok_rl.at[z], row + 1, 0, up))
        for step in range(1, 4):
            c = (z + step) % 4
            go(Link(gains_in, got_gain.at[z], gn_s.at[step], gn_r.at[z], row, c))

    def send_cotangent():
        for step in range(1, 4):
            c = (z + step) % 4
            go(Link(cot_in.at[pl.ds(pl.multiple_of(c * 128, 128), 128), :], got_g.at[z],
                    cot_s.at[step], cot_r.at[z], row, c))

    order = (z, 1 + z % 2, 2 - 2 * (z % 2) + z // 2, 3 - 3 * (z // 2))

    def near(i, c, r, part):
        size, cut = ROWS[i], SPLIT[i]
        start, count = {"all": (0, size), "a": (0, cut), "b": (cut, size - cut)}[part]
        return at_rows(ws[i], c, pl.multiple_of(r * size + start, 16), count)

    def gather_link(i, c, r, part, sem_s, sem_r, to_row, to_col, when=None):
        ref = near(i, c, r, part)
        return Link(ref, ref, sem_s, sem_r, to_row, to_col, when)

    def gather_first(i, j):
        c = order[j]
        if j == 0:
            go(gather_link(i, c, row, "all", az_s.at[i, 0, c], az_r.at[i, c], row, z + 1, z < 3))
            go(gather_link(i, c, row, "all", az_s.at[i, 1, c], az_r.at[i, c], row, z - 1, z > 0))
        else:
            arrived(near(i, c, row, "all"), az_r.at[i, c], row, z)
            go(gather_link(i, c, row, "all", az_s.at[i, 0, c], az_r.at[i, c], row, z + 1,
                           (c < z) & (z < 3)))
            go(gather_link(i, c, row, "all", az_s.at[i, 1, c], az_r.at[i, c], row, z - 1,
                           (c > z) & (z > 0)))
        go(gather_link(i, c, row, "a", ax_s.at[i, c, 0], ax_r.at[i, c, 0], rx, z))
        go(gather_link(i, c, row, "b", ay_s.at[i, c, 0], ay_r.at[i, c, 0], ry, z))
        go(gather_link(i, c, row, "b", ax_s.at[i, c, 1], ax_r.at[i, c, 1], rx, z))
        go(gather_link(i, c, row, "a", ay_s.at[i, c, 1], ay_r.at[i, c, 1], ry, z))
        go(gather_link(i, c, row, "all", ac_s.at[i, c, 0], ac_r.at[i, c, 0], rc, z))

    def gather_second(i, j):
        c = order[j]
        arrived(near(i, c, rx, "a"), ax_r.at[i, c, 0], rx, z)
        go(gather_link(i, c, rx, "a", ay_s.at[i, c, 2], ay_r.at[i, c, 2], ry, z))
        arrived(near(i, c, ry, "b"), ay_r.at[i, c, 0], ry, z)
        go(gather_link(i, c, ry, "b", ax_s.at[i, c, 2], ax_r.at[i, c, 2], rx, z))

    def gather_third(i, j):
        c = order[j]
        arrived(near(i, c, rx, "b"), ax_r.at[i, c, 1], rx, z)
        go(gather_link(i, c, rx, "all", ac_s.at[i, c, 1], ac_r.at[i, c, 1], rc, z))
        arrived(near(i, c, ry, "a"), ay_r.at[i, c, 1], ry, z)
        go(gather_link(i, c, ry, "all", ac_s.at[i, c, 2], ac_r.at[i, c, 2], rc, z))
        arrived(near(i, c, rxy, "a"), ay_r.at[i, c, 2], ry, z)
        arrived(near(i, c, rxy, "b"), ax_r.at[i, c, 2], rx, z)
        go(gather_link(i, c, rxy, "all", ac_s.at[i, c, 3], ac_r.at[i, c, 3], rc, z))

    def gather_done(i, j):
        for c in (order[j],):
            for n, r in enumerate((row, rx, ry, rxy)):
                arrived(near(i, c, r + 1 - 2 * core, "all"), ac_r.at[i, c, n], rc, z)

    def pack_own():
        r96 = pl.ds(pl.multiple_of(row * 96, 16), 96)
        r144 = pl.ds(pl.multiple_of(row * 144, 16), 144)
        q, k, v = qkv_in[0], qkv_in[1], qkv_in[2]
        gate, other = in_in[:, 0, :], in_in[:, 1, :]
        w1[z, r96, :] = jnp.concatenate(
            [q[:, :128], k[:, :128], v[:, :128], q[:, 128:], k[:, 128:], v[:, 128:],
             out_in[...]], axis=1)
        w2[z, r96, :] = jnp.concatenate([gate[:, :256], other[:, :256]], axis=1)
        tail = jnp.concatenate([gate[:, 256:], other[:, 256:]], axis=1)
        tail = jnp.concatenate([tail, jnp.zeros((48, 64), BF)], axis=0)
        w3[z, r144, :] = jnp.concatenate([down_in[...], tail], axis=1)
        gains_in[...] = jnp.zeros((8, 256), F32)
        gains_in[0:1, 0:192] = gain_one_in[...].reshape(1, 192)
        gains_in[1:2, 0:192] = gain_two_in[...].reshape(1, 192)

    items = ((0, 0), (1, 0), (0, 1), (2, 0), (0, 2), (1, 1), (0, 3), (1, 2), (1, 3), (2, 1),
             (2, 2), (2, 3))

    def gather_step(t):
        if t < 12:
            gather_first(*items[t])
        if t == 0:
            send_tokens()
        if t == 11:
            send_cotangent()
        if 2 <= t < 14:
            gather_second(*items[t - 2])
        if 3 <= t < 15:
            gather_third(*items[t - 3])

    def take_tokens():
        for c in range(4):
            low, size, to = window(c)

            @pl.when(z == c)
            def _():
                got_x[c, to : to + size, :] = tok_in[low : low + size, :]
                for other in range(4):
                    if other != c:
                        arrived(at_rows(got_x, other, to, size), tok_r.at[other], row, other)

        @pl.when(low_end)
        def _():
            for other in range(4):
                arrived(at_rows(got_x, other, 0, 32), tok_rl.at[other], row - 1, other)

        @pl.when(high_end)
        def _():
            for other in range(4):
                arrived(at_rows(got_x, other, 160, 32), tok_rr.at[other], row + 1, other)

        @pl.when((z == 0) & (row == 0))
        def _():
            got_x[:, 0:32, :] = jnp.zeros((4, 32, 384), BF)

        @pl.when((z == 3) & (row == 7))
        def _():
            got_x[:, 160:192, :] = jnp.zeros((4, 32, 384), BF)

        got_gain[pl.ds(z, 1)] = gains_in[...][None]
        for step in range(1, 4):
            c = (z + step) % 4
            arrived(got_gain.at[c], gn_r.at[c], row, c)
        at = 0
        for low, high, lane in ((32, 160, 0), (32, 160, 192), (0, 32, 0), (0, 32, 192),
                                (160, 192, 0), (160, 192, 192)):
            x_all[at : at + high - low, :] = jnp.concatenate(
                [got_x[c, low:high, lane : lane + 192].astype(F32) for c in range(4)], axis=1)
            at += high - low

    def gain_row(which):
        return jnp.concatenate([got_gain[c, which : which + 1, 0:192] for c in range(4)], axis=1)

    def window_ids(first, length):
        last = ids_in.shape[0] - 1
        spot = first // 128
        near_rows = [ids_in[pl.ds(jnp.clip(spot + n, 0, last), 1), :] for n in range(-1, 3)]
        base = near_rows[1][0:1, 0:1]
        rel = jnp.concatenate(near_rows, axis=0) - base
        rel = jnp.clip(rel, -200, 200).astype(BF)
        source = lax.broadcasted_iota(jnp.int32, (128, 128), 0)
        target = lane_iota((128, 128))
        pick = (source == jnp.where(target < 64, 2 * target, 2 * target - 127)).astype(BF)
        rel = jnp.concatenate([rel, jnp.zeros((4, 128), BF)], axis=0)
        rel = dot(rel, pick)
        keys = jnp.concatenate(
            [rel[1:2, :64], rel[2:3, :64], rel[1:2, 64:], rel[2:3, 64:], rel[0:1, 32:64],
             rel[0:1, 96:], rel[3:4, :32], rel[3:4, 64:96]], axis=1)
        lane = lane_iota((1, EXT))
        lost = (lane >= 256) & (lane < 320) & (first % length == 0)
        lost |= (lane >= 320) & ((first + OWN) % length == 0)
        keys = jnp.where(lost, 1000.0, keys)
        own_ids[...] = jnp.broadcast_to(keys[:, :OWN], (8, OWN))
        return keys, own_ids[...].T[:, 0:1]

    def tables():
        spot = lax.broadcasted_iota(jnp.int32, (EXT, 128), 0)
        halo = spot - 256
        place = jnp.where(
            spot < 128, 2 * spot, jnp.where(
                spot < 256, 2 * spot - 255, jnp.where(
                    halo < 32, 2 * halo - 64, jnp.where(
                        halo < 64, 2 * halo - 127, jnp.where(
                            halo < 96, 2 * halo + 128, 2 * halo + 65)))))
        first, length = start_of(row, z)
        place = (place + first + length) % length
        angle = place.astype(F32) * freq_in[0:1, :]
        cos_t[...] = jnp.cos(angle)
        turn = jnp.where((lane_iota((EXT, 128)) % 64) < 32, -1.0, 1.0)
        sin_t[...] = jnp.sin(angle) * turn
        key_ids, query_ids = window_ids(first, length)
        qrow = lax.broadcasted_iota(jnp.int32, (OWN, EXT), 0)
        qplace = jnp.where(qrow < 128, 2 * qrow, 2 * qrow - 255)
        kcol = lane_iota((OWN, EXT))
        khalo = kcol - 256
        kplace = jnp.where(
            kcol < 128, 2 * kcol, jnp.where(
                kcol < 256, 2 * kcol - 255, jnp.where(
                    khalo < 32, 2 * khalo - 64, jnp.where(
                        khalo < 64, 2 * khalo - 127, jnp.where(
                            khalo < 96, 2 * khalo + 128, 2 * khalo + 65)))))
        allowed = (jnp.abs(qplace - kplace) <= HALF) & (query_ids == key_ids)
        bias[...] = jnp.where(allowed, 0.0, -1e30)

    def statistics(v):
        mu = jnp.mean(v, axis=1, keepdims=True)
        inv = lax.rsqrt(jnp.mean(v * v, axis=1, keepdims=True) - mu * mu + EPSILON)
        return (v - mu) * inv, inv

    def norm_one():
        hat, inv = statistics(x_all[0:OWN, :])
        hat1[...] = hat
        stat[0] = jnp.broadcast_to(inv, (OWN, 128))
        gain = gain_row(0)
        n1[0:OWN, :] = (hat * gain).astype(BF)
        hat, _ = statistics(x_all[OWN:EXT, :])
        n1[OWN:EXT, :] = (hat * gain).astype(BF)

    def take_cotangent():
        got_g[pl.ds(z, 1)] = cot_in[pl.ds(pl.multiple_of(z * 128, 128), 128), :][None]
        for step in range(1, 4):
            c = (z + step) % 4
            arrived(got_g.at[c], cot_r.at[c], row, c)
        pad = jnp.zeros((128, 64), BF)
        for c in range(4):
            for odd in range(2):
                cot_pad[128 * odd : 128 * odd + 128, 256 * c : 256 * c + 256] = jnp.concatenate(
                    [got_g[c, :, 192 * odd : 192 * odd + 192], pad], axis=1)

    low_lanes = lambda shape: lane_iota(shape) < 64

    def forward_heads(c):
        proj = dot(n1[...], w1[c, :, 0:640])
        cos, sin = cos_t[...], sin_t[...]
        rot = lambda tile, n: tile * cos[0:n] + swap_halves(tile) * sin[0:n]
        qs[c, 0] = (rot(proj[0:OWN, 0:128], OWN) * 0.125).astype(BF)
        ks[c, 0] = rot(proj[:, 128:256], EXT).astype(BF)
        vs[c, 0] = proj[:, 256:384].astype(BF)
        third = rot(proj[:, 384:512], EXT)
        low = low_lanes((EXT, 128))
        qs[c, 1] = jnp.where(low[0:OWN], third[0:OWN] * 0.125, 0.0).astype(BF)
        ks[c, 1] = jnp.where(low, pltpu.roll(third, 64, 1), 0.0).astype(BF)
        vs[c, 1] = jnp.where(low, proj[:, 512:640], 0.0).astype(BF)

        def head(h, q, k):
            scores = dot_nt(q, k) + bias[...]
            weight = jnp.exp(scores - jnp.max(scores, axis=1, keepdims=True))
            weight = weight * (1.0 / jnp.sum(weight, axis=1, keepdims=True))
            probs[3 * c + h] = weight
            return weight.astype(BF)

        zero = jnp.zeros((), BF)
        lowq, lowk = low_lanes((OWN, 128)), low
        q, k, v = qs[c, 0], ks[c, 0], vs[c, 0]
        both = dot(head(0, jnp.where(lowq, q, zero), k), jnp.where(lowk, v, zero))
        both += dot(head(1, jnp.where(lowq, zero, q), k), jnp.where(lowk, zero, v))
        att_c[c, :, 0:128] = both.astype(BF)
        att_c[c, :, 128:256] = dot(head(2, qs[c, 1], ks[c, 1]), vs[c, 1]).astype(BF)

    def forward_middle():
        for c in range(4):
            att[:, 192 * c : 192 * c + 192] = att_c[c, :, 0:192]
        for c in range(4):
            out = dot(att[...], w1[c, :, 512:768])
            mid[:, 192 * c : 192 * c + 192] = (
                x_all[0:OWN, 192 * c : 192 * c + 192] + out[:, 64:256])
        hat, inv = statistics(mid[...])
        hat2[...] = hat
        stat[1] = jnp.broadcast_to(inv, (OWN, 128))
        n2[...] = (hat * gain_row(1)).astype(BF)

    def gelu_parts(g):
        phi = 0.5 * (1.0 + lax.erf(g * 0.7071067811865476))
        return g * phi, phi + g * (jnp.exp(g * g * -0.5) * 0.3989422804014327)

    def forward_hidden(c):
        both = dot(n2[...], w2[c])
        value, slope = gelu_parts(both[:, 0:256])
        other = both[:, 256:512]
        gel[c] = value
        gel_up[c] = other * slope
        hid[c] = (value * other).astype(BF)

    def forward_tail():
        for c in range(4):
            for r in range(8):
                tail_in[96 * r : 96 * r + 96, 128 * c : 128 * c + 128] = (
                    w3[c, 144 * r : 144 * r + 96, 128:256])
                if r < 4:
                    tail_down[c, 32 * r : 32 * r + 32, :] = (
                        w3[c, 288 * r + 256 : 288 * r + 288, :])
        tails = dot(n2[...], tail_in[...])
        lanes = lane_iota((OWN, 128)) // 32
        packed = jnp.zeros((OWN, 128), F32)
        for c in range(4):
            tile = tails[:, 128 * c : 128 * c + 128]
            value, slope = gelu_parts(tile)
            other = pltpu.roll(tile, 96, 1)
            gel_t[c] = value
            gel_up_t[c] = other * slope
            moved = pltpu.roll(value * other, (32 * c + 64) % 128, 1)
            packed = jnp.where(lanes == c, moved, packed)
        hid_tail[...] = packed.astype(BF)

    def forward_mixed():
        for k in range(4):
            total = dot(hid_tail[...], tail_down[k])
            for c in range(4):
                total += dot(hid[c], w3[k, 288 * c : 288 * c + 256, :])
            out = (mid[:, 192 * k : 192 * k + 192] + total[:, 0:192]).astype(BF)
            mixed_send[k] = jnp.concatenate([out[0:128], out[128:256]], axis=1)
        for step in range(1, 4):
            c = (z + step) % 4
            go(Link(mixed_send.at[c], mixed_got.at[z], mx_s.at[step], mx_r.at[z], row, c))

    def backward_hidden(c):
        grad = dot_nt(cot_pad[:, 0:256], w3[0, 288 * c : 288 * c + 256, :])
        for k in range(1, 4):
            grad += dot_nt(cot_pad[:, 256 * k : 256 * k + 256], w3[k, 288 * c : 288 * c + 256, :])
        d_gate[c] = jnp.concatenate([grad * gel_up[c], grad * gel[c]], axis=1).astype(BF)

    def backward_tail():
        grad = dot_nt(cot_pad[:, 0:256], tail_down[0])
        for k in range(1, 4):
            grad += dot_nt(cot_pad[:, 256 * k : 256 * k + 256], tail_down[k])
        lanes = lane_iota((OWN, 128))
        for c in range(4):
            gate = pltpu.roll(grad, (64 - 32 * c) % 128, 1) * gel_up_t[c]
            other = pltpu.roll(grad, (96 - 32 * c) % 128, 1) * pltpu.roll(gel_t[c], 32, 1)
            d_tail[:, 128 * c : 128 * c + 128] = jnp.where(
                lanes >= 96, other, jnp.where(lanes >= 64, gate, 0.0)).astype(BF)

    def grad_down():
        for c in range(4):
            part = dot_tn(hid[c], cot_pad[...]).astype(BF)
            for k in range(4):
                d3[k, 288 * c : 288 * c + 256, :] = part[:, 256 * k : 256 * k + 256]
        part = dot_tn(hid_tail[...], cot_pad[...]).astype(BF)
        for c in range(4):
            for k in range(4):
                d3[k, 288 * c + 256 : 288 * c + 288, :] = (
                    part[32 * c : 32 * c + 32, 256 * k : 256 * k + 256])

    def grad_tail():
        part = dot_tn(n2[...], d_tail[...]).astype(BF)
        for c in range(4):
            for r in range(8):
                d3[c, 144 * r : 144 * r + 96, 128:256] = (
                    d3[c, 144 * r : 144 * r + 96, 128:256]
                    + part[96 * r : 96 * r + 96, 128 * c : 128 * c + 128])

    def grad_in(c):
        d2[c] = dot_tn(n2[...], d_gate[c]).astype(BF)

    def norm_back(grad, hat, inv, gain):
        e = grad * gain
        return inv * (e - jnp.mean(e, axis=1, keepdims=True)
                      - hat * jnp.mean(e * hat, axis=1, keepdims=True))

    def backward_middle():
        grad = dot_nt(d_tail[...], tail_in[...])
        for c in range(4):
            grad += dot_nt(d_gate[c], w2[c])
        hat = hat2[...]
        gain_part[1:2, :] = jnp.sum(grad * hat, axis=0, keepdims=True)
        back = norm_back(grad, hat, stat[1][:, 0:1], gain_row(1))
        pad = jnp.zeros((OWN, 64), BF)
        total = jnp.concatenate(
            [cot_pad[:, 256 * c : 256 * c + 192].astype(F32) for c in range(4)], axis=1) + back
        mid_grad[...] = total
        branch = total.astype(BF)
        for c in range(4):
            branch_pad[:, 256 * c : 256 * c + 256] = jnp.concatenate(
                [pad, branch[:, 192 * c : 192 * c + 192]], axis=1)
        grad = dot_nt(branch_pad[:, 0:256], w1[0, :, 512:768])
        for c in range(1, 4):
            grad += dot_nt(branch_pad[:, 256 * c : 256 * c + 256], w1[c, :, 512:768])
        att_grad[...] = grad.astype(BF)

    def grad_out():
        part = dot_tn(att[...], branch_pad[...]).astype(BF)
        for c in range(4):
            d1[c, :, 512:768] = part[:, 256 * c : 256 * c + 256]

    def backward_heads(c):
        zero = jnp.zeros((), BF)
        lowq, lowk = low_lanes((OWN, 128)), low_lanes((EXT, 128))

        def head(h, g, v):
            weight = probs[3 * c + h]
            prob_grad = dot_nt(g, v)
            inner = jnp.sum(weight * prob_grad, axis=1, keepdims=True)
            return (weight * (prob_grad - inner)).astype(BF), weight.astype(BF)

        q, k, v = qs[c, 0], ks[c, 0], vs[c, 0]
        g = att_grad[:, 192 * c : 192 * c + 128]
        g0, g1 = jnp.where(lowq, g, zero), jnp.where(lowq, zero, g)
        s0, p0 = head(0, g0, v)
        s1, p1 = head(1, g1, v)
        dq = dot(s0, jnp.where(lowk, k, zero)) + dot(s1, jnp.where(lowk, zero, k))
        dk = dot_tn(s0, jnp.where(lowq, q, zero)) + dot_tn(s1, jnp.where(lowq, zero, q))
        dv = dot_tn(p0, g0) + dot_tn(p1, g1)
        g2 = jnp.concatenate(
            [att_grad[:, 192 * c + 128 : 192 * c + 192], jnp.zeros((OWN, 64), BF)], axis=1)
        s2, p2 = head(2, g2, vs[c, 1])
        dq2 = dot(s2, ks[c, 1]) * 0.125
        dk2 = pltpu.roll(dot_tn(s2, qs[c, 1]), 64, 1)
        dv2 = dot_tn(p2, g2)
        cos, sin = cos_t[...], sin_t[...]
        back = lambda tile: tile * cos - swap_halves(tile) * sin
        none = jnp.zeros((EXT - OWN, 128), F32)
        dq = jnp.concatenate([dq * 0.125, none], axis=0)
        d_proj[c, :, 0:128] = back(dq).astype(BF)
        d_proj[c, :, 128:256] = back(dk).astype(BF)
        d_proj[c, :, 256:384] = dv.astype(BF)
        d_proj[c, :, 384:512] = back(jnp.concatenate([dq2, none], axis=0) + dk2).astype(BF)
        d_proj[c, :, 512:640] = dv2.astype(BF)

    def grad_qkv(c):
        part = dot_tn(n1[...], d_proj[c]).astype(BF)
        d1[c, :, 0:512] = part[:, 0:512]
        d1[c, :, 512:640] = d1[c, :, 512:640] + part[:, 512:640]

    def backward_first():
        grad = dot_nt(d_proj[0], w1[0, :, 0:640])
        for c in range(1, 4):
            grad += dot_nt(d_proj[c], w1[c, :, 0:640])
        n1_grad[...] = grad[0:OWN]
        halo_out[...] = grad[OWN:EXT].astype(BF)

    edge_low, edge_high = (z == 0) & (row == 0), (z == 3) & (row == 7)
    left_row = jnp.where(z == 0, row - 1, row)
    right_row = jnp.where(z == 3, row + 1, row)
    left_col, right_col = (z + 3) % 4, (z + 1) % 4

    def halo_send():
        go(Link(halo_out.at[pl.ds(0, 64), :], halo_right, ha_s.at[0], ha_r.at[1],
                left_row, left_col, jnp.logical_not(edge_low)))
        go(Link(halo_out.at[pl.ds(64, 64), :], halo_left, ha_s.at[1], ha_r.at[0],
                right_row, right_col, jnp.logical_not(edge_high)))

    def halo_take():
        @pl.when(jnp.logical_not(edge_low))
        def _():
            arrived(halo_left, ha_r.at[0], left_row, left_col)
            n1_grad[0:32, :] += halo_left[0:32, :].astype(F32)
            n1_grad[128:160, :] += halo_left[32:64, :].astype(F32)

        @pl.when(jnp.logical_not(edge_high))
        def _():
            arrived(halo_right, ha_r.at[1], right_row, right_col)
            n1_grad[96:128, :] += halo_right[0:32, :].astype(F32)
            n1_grad[224:256, :] += halo_right[32:64, :].astype(F32)

    def backward_last():
        grad, hat = n1_grad[...], hat1[...]
        gain_part[0:1, :] = jnp.sum(grad * hat, axis=0, keepdims=True)
        total = mid_grad[...] + norm_back(grad, hat, stat[0][:, 0:1], gain_row(0))
        out = total.astype(BF)
        for k in range(4):
            mine = out[:, 192 * k : 192 * k + 192]
            input_send[k] = jnp.concatenate([mine[0:128], mine[128:256]], axis=1)
        for step in range(1, 4):
            c = (z + step) % 4
            go(Link(input_send.at[c], input_got.at[z], ig_s.at[step], ig_r.at[z], row, c))
        for c in range(4):
            gain_part_c = gain_part[0:2, 192 * c : 192 * c + 192]
            gain_sum[c, 0:2, 0:192] = gain_part_c
        for step in range(1, 4):
            c = (z + step) % 4
            go(Link(gain_sum.at[c], gain_z.at[z], gz_s.at[step], gz_r.at[z], row, c))

    cores = (core1, core2, core3)
    xas, xbs, yas, ybs = (xa1, xa2, xa3), (xb1, xb2, xb3), (ya1, ya2, ya3), (yb1, yb2, yb3)
    zls, zrs = (zl1, zl2, zl3), (zr1, zr2, zr3)
    outs = (grad_one, grad_two, grad_three)

    def unpack_outs():
        one, two, three = grad_one[...], grad_two[...], grad_three[...]
        for n in range(3):
            qkv_out[n] = jnp.concatenate(
                [one[:, 128 * n : 128 * n + 128], one[:, 384 + 64 * n : 448 + 64 * n]], axis=1)
        out_out[...] = one[:, 576:768]
        for n in range(2):
            in_out[:, n, :] = jnp.concatenate(
                [two[:, 256 * n : 256 * n + 256], three[0:96, 192 + 32 * n : 224 + 32 * n]],
                axis=1)
        down_out[...] = three[:, 0:192]


    def place(i, c, r, part):
        size, cut = ROWS[i], SPLIT[i]
        start, count = {"all": (0, size), "a": (0, cut), "b": (cut, size - cut)}[part]
        return c, pl.ds(pl.multiple_of(r * size + start, 16), count)

    def piece(i, c, r, part):
        lead, span = place(i, c, r, part)
        return ds_[i].at[lead, span, :]

    def add_into(i, c, r, part, value):
        lead, span = place(i, c, r, part)
        ds_[i][lead, span, :] = ds_[i][lead, span, :] + value

    def sum_first(i, j):
        c = order[3 - j]
        for n in range(4):
            go(Link(piece(i, c, 2 * n + 1 - core, "all"), cores[i].at[c, n],
                    rc_s.at[i, c, n], rc_r.at[i, c, n], rc, z))

    def sum_second(i, j):
        c = order[3 - j]
        for n in range(4):
            arrived(cores[i].at[c, n], rc_r.at[i, c, n], rc, z)
            add_into(i, c, 2 * n + core, "all", cores[i][c, n])
        for y in range(2):
            go(Link(piece(i, c, 4 * y + 2 * (1 - xc) + core, "a"), xas[i].at[c, y],
                    rx_s.at[i, c, y], rx_r.at[i, c, y], rx, z))
        for x in range(2):
            go(Link(piece(i, c, 4 * (1 - yc) + 2 * x + core, "b"), ybs[i].at[c, x],
                    ry_s.at[i, c, x], ry_r.at[i, c, x], ry, z))

    def sum_third(i, j):
        c = order[3 - j]
        for y in range(2):
            arrived(xas[i].at[c, y], rx_r.at[i, c, y], rx, z)
            add_into(i, c, 4 * y + 2 * xc + core, "a", xas[i][c, y])
        go(Link(piece(i, c, ry, "a"), yas[i].at[c], ry_s.at[i, c, 2], ry_r.at[i, c, 2], ry, z))
        for x in range(2):
            arrived(ybs[i].at[c, x], ry_r.at[i, c, x], ry, z)
            add_into(i, c, 4 * yc + 2 * x + core, "b", ybs[i][c, x])
        go(Link(piece(i, c, rx, "b"), xbs[i].at[c], rx_s.at[i, c, 2], rx_r.at[i, c, 2], rx, z))

    def sum_fourth(i, j):
        c = order[3 - j]
        arrived(yas[i].at[c], ry_r.at[i, c, 2], ry, z)
        add_into(i, c, row, "a", yas[i][c])
        arrived(xbs[i].at[c], rx_r.at[i, c, 2], rx, z)
        add_into(i, c, row, "b", xbs[i][c])

        @pl.when((c > z) & (z > 0))
        def _():
            arrived(zls[i].at[c], rz_r.at[i, 0, c], row, z - 1)
            add_into(i, c, row, "all", zls[i][c])

        @pl.when((c < z) & (z < 3))
        def _():
            arrived(zrs[i].at[c], rz_r.at[i, 1, c], row, z + 1)
            add_into(i, c, row, "all", zrs[i][c])

        go(Link(piece(i, c, row, "all"), zls[i].at[c], rz_s.at[i, 0, c], rz_r.at[i, 0, c],
                row, z + 1, c > z))
        go(Link(piece(i, c, row, "all"), zrs[i].at[c], rz_s.at[i, 1, c], rz_r.at[i, 1, c],
                row, z - 1, c < z))

    def sum_last(i):
        lead, span = place(i, z, row, "all")
        outs[i][...] = ds_[i][lead, span, :].astype(F32)

        @pl.when(z > 0)
        def _():
            arrived(zls[i].at[z], rz_r.at[i, 0, z], row, z - 1)
            outs[i][...] = outs[i][...] + zls[i][z].astype(F32)

        @pl.when(z < 3)
        def _():
            arrived(zrs[i].at[z], rz_r.at[i, 1, z], row, z + 1)
            outs[i][...] = outs[i][...] + zrs[i][z].astype(F32)

    def sum_step(t, queue):
        for lag, step in enumerate((sum_first, sum_second, sum_third, sum_fourth)):
            if 0 <= t - lag < len(queue):
                step(*queue[t - lag])

    def gains_first():
        gain_z[pl.ds(z, 1)] = gain_sum[pl.ds(z, 1)]
        for step in range(1, 4):
            c = (z + step) % 4
            arrived(gain_z.at[c], gz_r.at[c], row, c)
        gain_all[pl.ds(row, 1)] = (gain_z[0] + gain_z[1] + gain_z[2] + gain_z[3])[None]
        for step in range(1, 8):
            go(Link(gain_all.at[row], gain_all.at[row], gp_s.at[step], gp_r.at[row],
                    (row + step) % 8, z))

    def gains_last():
        for step in range(1, 8):
            r = (row + step) % 8
            arrived(gain_all.at[r], gp_r.at[r], r, z)
        total = gain_all[0]
        for r in range(1, 8):
            total = total + gain_all[r]
        gain_one_out[...] = total[0:1, 0:192].reshape(192)
        gain_two_out[...] = total[1:2, 0:192].reshape(192)

    def finish(out_ref, send, got, sems):
        got[pl.ds(z, 1)] = send[pl.ds(z, 1)]
        for step in range(1, 4):
            c = (z + step) % 4
            arrived(got.at[c], sems.at[c], row, c)
        for c in range(4):
            out_ref[128 * c : 128 * c + 128, :] = got[c].astype(out_ref.dtype)

    pack_own()
    pl.semaphore_wait(barrier, peers)
    gather_step(0)
    gather_step(1)
    tables()
    gather_step(2)
    gather_step(3)
    take_tokens()
    norm_one()
    for t in range(4, 15):
        gather_step(t)
        if t in (4, 6, 8, 10):
            j = (t - 4) // 2
            gather_done(0, j)
            forward_heads(order[j])
        if t == 11:
            forward_middle()
        if t in (12, 13):
            for j in (2 * t - 24, 2 * t - 23):
                gather_done(1, j)
                forward_hidden(order[j])
    for j in range(4):
        gather_done(2, j)
    forward_tail()
    take_cotangent()
    for c in range(4):
        backward_hidden(c)
    backward_tail()
    grad_down()
    grad_tail()
    for j in range(4):
        sum_first(2, j)
    for j in range(4):
        grad_in(order[3 - j])
        sum_first(1, j)
        sum_second(2, j)
    forward_mixed()
    backward_middle()
    sum_third(2, 0)
    sum_second(1, 0)
    grad_out()
    for j in range(4):
        backward_heads(j)
        if j < 3:
            sum_third(2, j + 1)
            sum_second(1, j + 1)
    for j in range(4):
        grad_qkv(order[3 - j])
        sum_first(0, j)
        sum_third(1, j)
        sum_fourth(2, j)
    backward_first()
    halo_send()
    sum_second(0, 0)
    sum_second(0, 1)
    halo_take()
    backward_last()
    sum_fourth(1, 0)
    sum_fourth(1, 1)
    sum_second(0, 2)
    sum_third(0, 0)
    sum_fourth(1, 2)
    sum_fourth(1, 3)
    gains_first()
    sum_second(0, 3)
    sum_third(0, 1)
    sum_fourth(0, 0)
    sum_third(0, 2)
    sum_fourth(0, 1)
    finish(mixed_out, mixed_send, mixed_got, mx_r)
    sum_third(0, 3)
    sum_fourth(0, 2)
    sum_fourth(0, 3)
    sum_last(2)
    sum_last(1)
    finish(input_out, input_send, input_got, ig_r)
    gains_last()
    sum_last(0)
    unpack_outs()
    for link in sent:
        link.sent()


def hand_over(*refs):
    for n in range(8):
        refs[8 + n][...] = refs[n][...]


def fast_local(
    tokens, segment_ids, gain_one, qkv_weight, out_weight, gain_two, in_weight, down_weight,
    cotangent,
):
    rows_all = tokens.shape[1] * 2 * lax.axis_size("row")
    length = min(SEQ_MAX, rows_all)

    def start_of(row, z):
        return (row * 4 + z) * OWN, length

    frequency = 10000.0 ** (-(np.arange(HEAD_DIM // 2) * 2.0) / HEAD_DIM)
    frequency = jnp.asarray(np.tile(frequency.astype(np.float32), 4)[None, :].repeat(8, 0))
    vmem, dma = pltpu.VMEM, pltpu.SemaphoreType.DMA
    shapes = [
        vmem((4, 192, 384), BF), vmem((4, 128, 384), BF), vmem((4, 8, 256), F32),
        vmem((4, 768, 768), BF), vmem((4, 768, 512), BF), vmem((4, 1152, 256), BF),
        vmem((4, 768, 768), BF), vmem((4, 768, 512), BF), vmem((4, 1152, 256), BF),
    ]
    shapes += [vmem((4, 4, ROWS[i], COLS[i]), BF) for i in range(3)]
    shapes += [vmem((4, 2, SPLIT[i], COLS[i]), BF) for i in range(3)]
    shapes += [vmem((4, ROWS[i] - SPLIT[i], COLS[i]), BF) for i in range(3)]
    shapes += [vmem((4, SPLIT[i], COLS[i]), BF) for i in range(3)]
    shapes += [vmem((4, 2, ROWS[i] - SPLIT[i], COLS[i]), BF) for i in range(3)]
    shapes += [vmem((4, ROWS[i], COLS[i]), BF) for i in range(3)] * 2
    shapes += [
        vmem((8, 256), F32), vmem((8, OWN), F32),
        vmem((EXT, 768), F32), vmem((EXT, 128), F32), vmem((EXT, 128), F32),
        vmem((OWN, EXT), F32), vmem((EXT, 768), BF), vmem((OWN, 768), F32),
        vmem((2, OWN, 128), F32), vmem((4, 2, OWN, 128), BF), vmem((4, 2, EXT, 128), BF),
        vmem((4, 2, EXT, 128), BF), vmem((12, OWN, EXT), F32),
        vmem((4, OWN, 256), BF), vmem((OWN, 768), BF),
        vmem((OWN, 768), F32), vmem((OWN, 768), F32), vmem((OWN, 768), BF),
        vmem((768, 512), BF), vmem((4, 128, 256), BF), vmem((4, OWN, 256), BF),
        vmem((OWN, 128), BF), vmem((4, OWN, 256), F32), vmem((4, OWN, 256), F32),
        vmem((4, OWN, 128), F32), vmem((4, OWN, 128), F32), vmem((OWN, 1024), BF),
        vmem((4, OWN, 512), BF), vmem((OWN, 512), BF),
        vmem((OWN, 768), F32), vmem((OWN, 1024), BF), vmem((OWN, 768), BF),
        vmem((4, EXT, 640), BF), vmem((OWN, 768), F32),
        vmem((128, 768), BF), vmem((64, 768), BF), vmem((64, 768), BF),
        vmem((4, 128, 384), BF), vmem((4, 128, 384), BF),
        vmem((4, 128, 384), BF), vmem((4, 128, 384), BF),
        vmem((8, 768), F32), vmem((4, 8, 256), F32), vmem((4, 8, 256), F32),
        vmem((8, 8, 256), F32), vmem((96, 768), F32), vmem((96, 512), F32), vmem((144, 256), F32),
        dma((6,)), dma((4,)), dma((4,)), dma((4,)), dma((4,)), dma((4,)), dma((4,)), dma((4,)),
        dma((3, 2, 4)), dma((3, 4)), dma((3, 4, 3)), dma((3, 4, 3)), dma((3, 4, 3)),
        dma((3, 4, 3)), dma((3, 4, 4)), dma((3, 4, 4)),
        dma((3, 4, 4)), dma((3, 4, 4)), dma((3, 4, 3)), dma((3, 4, 3)), dma((3, 4, 3)),
        dma((3, 4, 3)), dma((3, 2, 4)), dma((3, 2, 4)),
        dma((8,)), dma((2,)), dma((2,)), dma((4,)), dma((4,)), dma((4,)), dma((4,)), dma((4,)),
        dma((4,)), dma((8,)), dma((8,)),
    ]
    whole = pl.BlockSpec(memory_space=pltpu.VMEM)
    results = (
        jax.ShapeDtypeStruct((512, 384), BF), jax.ShapeDtypeStruct((512, 384), F32),
        jax.ShapeDtypeStruct((3, 96, 192), F32), jax.ShapeDtypeStruct((96, 192), F32),
        jax.ShapeDtypeStruct((96, 2, 288), F32), jax.ShapeDtypeStruct((144, 192), F32),
        jax.ShapeDtypeStruct((192,), F32), jax.ShapeDtypeStruct((192,), F32),
    )
    outs = pl.pallas_call(
        functools.partial(layer_kernel, start_of=start_of),
        out_shape=results,
        in_specs=[whole] * 10,
        out_specs=(whole,) * 8,
        scratch_shapes=shapes,
        compiler_params=pltpu.CompilerParams(
            collective_id=0, has_side_effects=True, vmem_limit_bytes=62 * 1024 * 1024),
    )(tokens[0], cotangent[0], qkv_weight.transpose(1, 0, 2), out_weight, in_weight, down_weight,
      gain_one, gain_two, segment_ids.reshape(-1, 128), frequency)
    mixed, input_grad, qkv_grad, out_grad, in_grad, down_grad, one_grad, two_grad = pl.pallas_call(
        hand_over,
        out_shape=results,
        in_specs=[whole] * 8,
        out_specs=(whole,) * 8,
    )(*outs)
    return (
        mixed[None], input_grad[None], one_grad, qkv_grad.transpose(1, 0, 2), out_grad,
        two_grad, in_grad, down_grad,
    )


def solution(mesh):
    placed = (
        P("col", "row", None),
        P(),
        P("col"),
        P("row", None, "col"),
        P("row", "col"),
        P("col"),
        P("row", None, "col"),
        P("row", "col"),
        P("col", "row", None),
    )
    part = local
    if mesh.shape["row"] == 8 and mesh.shape["col"] == 4:
        part = fast_local
    return jax.shard_map(
        part,
        mesh=mesh,
        in_specs=placed,
        out_specs=(
            P("col", "row", None),
            P("col", "row", None),
            P("col"),
            P("row", None, "col"),
            P("row", "col"),
            P("col"),
            P("row", None, "col"),
            P("row", "col"),
        ),
        check_vma=False,
    )
```

```python
import functools

import jax
import jax.numpy as jnp
import numpy as np
from jax import lax
from jax.experimental import pallas as pl
from jax.experimental.pallas import tpu as pltpu
from jax.sharding import PartitionSpec as P

HEAD_DIM = 64
WINDOW = 128
SEQ_MAX = 4096


EPSILON = 1e-05


def with_halo(block, sides, width):
    for axis, dim in sides:
        count = lax.axis_size(axis)
        forward = [(i, i + 1) for i in range(count - 1)]
        backward = [(target, source) for source, target in forward]
        low = lax.ppermute(
            lax.slice_in_dim(block, block.shape[dim] - width, None, axis=dim), axis, forward
        )
        high = lax.ppermute(lax.slice_in_dim(block, 0, width, axis=dim), axis, backward)
        block = jnp.concatenate([low, block, high], axis=dim)
    return block


def rotate(values, cosine, sine_table):
    half_dim = values.shape[-1] // 2
    turned = jnp.concatenate([-values[..., half_dim:], values[..., :half_dim]], axis=-1)
    return values * cosine + turned * sine_table


def rotate_back(grad_rows, cosine, sine_table):
    half_dim = grad_rows.shape[-1] // 2
    turned = jnp.concatenate([-grad_rows[..., half_dim:], grad_rows[..., :half_dim]], axis=-1)
    return grad_rows * cosine - turned * sine_table


def spread(values):
    return lax.all_gather(values, "col", axis=1, tiled=True)


def collect(partial_rows):
    return lax.psum_scatter(partial_rows, "col", scatter_dimension=1, tiled=True)


def norm_forward(values, full_width):
    row_sums = lax.psum((jnp.sum(values, axis=1), jnp.sum(values * values, axis=1)), "col")
    mean_value = row_sums[0] / full_width
    variance = row_sums[1] / full_width - mean_value * mean_value
    inverse = lax.rsqrt(variance + EPSILON)
    return ((values - mean_value[:, None]) * inverse[:, None], inverse)


def norm_backward(grad_rows, scaled, inverse, gain_part, full_width):
    weighted = grad_rows * gain_part
    row_sums = lax.psum((jnp.sum(weighted, axis=1), jnp.sum(weighted * scaled, axis=1)), "col")
    input_part = inverse[:, None] * (
        weighted - row_sums[0][:, None] / full_width - scaled * (row_sums[1][:, None] / full_width)
    )
    return (input_part, jnp.sum(grad_rows * scaled, axis=0))


def geglu(gate_up):
    return jax.nn.gelu(gate_up[:, 0], approximate=False) * gate_up[:, 1]


def local(
    tokens,
    segment_ids,
    gain_one,
    qkv_weight,
    out_weight,
    gain_two,
    in_weight,
    down_weight,
    cotangent,
):
    pair_rows = tokens.shape[1]
    rows_here = pair_rows * 2
    tok_width = tokens.shape[2] // 2
    full_width = tok_width * lax.axis_size("col")
    heads_here = qkv_weight.shape[2] // HEAD_DIM
    head_width = heads_here * HEAD_DIM
    half_window = WINDOW // 2
    block_rows = min(512, rows_here)
    block_count = rows_here // block_rows
    key_span = block_rows + 2 * half_window
    score_scale = HEAD_DIM ** (-0.5)
    length = min(SEQ_MAX, rows_here * lax.axis_size("row"))
    first_row = lax.axis_index("row") * rows_here
    grad_rows = cotangent.reshape(rows_here, tok_width)
    qkv_full, out_full, in_full, down_full = (
        lax.all_gather(qkv_weight, "row", axis=0, tiled=True),
        lax.all_gather(out_weight, "row", axis=0, tiled=True),
        lax.all_gather(in_weight, "row", axis=0, tiled=True),
        lax.all_gather(down_weight, "row", axis=0, tiled=True),
    )
    global_rows = first_row + jnp.arange(rows_here, dtype=jnp.int32)
    places = (global_rows % length).astype(jnp.float32)
    frequencies = 10000.0 ** (-(jnp.arange(HEAD_DIM // 2, dtype=jnp.float32) * 2.0) / HEAD_DIM)
    angles = places[:, None] * frequencies[None, :]
    angles = jnp.concatenate([angles, angles], axis=1)[:, None, :]
    cosine = jnp.cos(angles)
    sine_table = jnp.sin(angles)
    query_ids = lax.dynamic_slice_in_dim(segment_ids, first_row, rows_here)
    padded_ids = jnp.pad(segment_ids, half_window, constant_values=-1)
    key_ids = lax.dynamic_slice_in_dim(padded_ids, first_row, rows_here + 2 * half_window)
    query_seqs = global_rows // length
    key_seqs = (
        first_row - half_window + jnp.arange(rows_here + 2 * half_window, dtype=jnp.int32)
    ) // length
    offsets = (
        jnp.arange(key_span, dtype=jnp.int32)[None, :]
        - half_window
        - jnp.arange(block_rows, dtype=jnp.int32)[:, None]
    )
    in_window = jnp.abs(offsets) <= half_window

    def block_scores(block_start, block_queries, block_keys):
        same_doc = (
            query_ids[block_start : block_start + block_rows, None]
            == key_ids[None, block_start : block_start + key_span]
        )
        same_seq = (
            query_seqs[block_start : block_start + block_rows, None]
            == key_seqs[None, block_start : block_start + key_span]
        )
        allowed = in_window & same_doc & same_seq
        scores = (
            jnp.einsum(
                "qhd,khd->hqk", block_queries, block_keys, preferred_element_type=jnp.float32
            )
            * score_scale
        )
        return jnp.where(allowed[None], scores, -1e30)

    token_values = tokens.reshape(rows_here, tok_width).astype(jnp.float32)
    scaled_one, inverse_one = norm_forward(token_values, full_width)
    normed_one_full = spread((scaled_one * gain_one).astype(jnp.bfloat16))
    projected = jnp.einsum(
        "td,dsf->tsf", normed_one_full, qkv_full, preferred_element_type=jnp.float32
    )
    projected = projected.reshape(rows_here, 3, heads_here, HEAD_DIM)
    queries = rotate(projected[:, 0], cosine, sine_table).astype(jnp.bfloat16)
    key_rows = rotate(projected[:, 1], cosine, sine_table).astype(jnp.bfloat16)
    value_rows = projected[:, 2].astype(jnp.bfloat16)
    key_value = jnp.concatenate(
        [key_rows.reshape(rows_here, head_width), value_rows.reshape(rows_here, head_width)], axis=1
    )
    padded_pair = with_halo(key_value, (("row", 0),), half_window)
    padded_keys = padded_pair[:, :head_width].reshape(
        rows_here + 2 * half_window, heads_here, HEAD_DIM
    )
    padded_values = padded_pair[:, head_width:].reshape(
        rows_here + 2 * half_window, heads_here, HEAD_DIM
    )
    output_blocks = []
    total_blocks = []
    for block_number in range(block_count):
        block_start = block_number * block_rows
        masked = block_scores(
            block_start,
            queries[block_start : block_start + block_rows],
            padded_keys[block_start : block_start + key_span],
        )
        largest = jnp.max(masked, axis=-1, keepdims=True)
        log_total = largest + jnp.log(jnp.sum(jnp.exp(masked - largest), axis=-1, keepdims=True))
        weights = jnp.exp(masked - log_total).astype(jnp.bfloat16)
        output_blocks.append(
            jnp.einsum(
                "hqk,khd->qhd",
                weights,
                padded_values[block_start : block_start + key_span],
                preferred_element_type=jnp.float32,
            )
        )
        total_blocks.append(log_total)
    attended = (
        jnp.concatenate(output_blocks, axis=0).reshape(rows_here, head_width).astype(jnp.bfloat16)
    )
    attended_full = spread(attended)
    middle = token_values + jnp.dot(attended_full, out_full, preferred_element_type=jnp.float32)
    scaled_two, inverse_two = norm_forward(middle, full_width)
    normed_two_full = spread((scaled_two * gain_two).astype(jnp.bfloat16))
    gate_up = jnp.einsum(
        "td,dsf->tsf", normed_two_full, in_full, preferred_element_type=jnp.float32
    )
    hidden_value, geglu_pull = jax.vjp(geglu, gate_up)
    hidden_full = spread(hidden_value.astype(jnp.bfloat16))
    mixed = (middle + jnp.dot(hidden_full, down_full, preferred_element_type=jnp.float32)).astype(
        jnp.bfloat16
    )
    qkv_back, out_back, in_back, down_back = (
        lax.all_gather(qkv_weight, "row", axis=0, tiled=True),
        lax.all_gather(out_weight, "row", axis=0, tiled=True),
        lax.all_gather(in_weight, "row", axis=0, tiled=True),
        lax.all_gather(down_weight, "row", axis=0, tiled=True),
    )
    down_part = jnp.einsum("tf,td->fd", hidden_full, grad_rows, preferred_element_type=jnp.float32)
    hidden_grad = collect(
        jnp.einsum("td,fd->tf", grad_rows, down_back, preferred_element_type=jnp.float32)
    )
    gate_up_grad = geglu_pull(hidden_grad)[0].astype(jnp.bfloat16)
    in_part = jnp.einsum(
        "td,tsf->dsf", normed_two_full, gate_up_grad, preferred_element_type=jnp.float32
    )
    normed_two_grad = collect(
        jnp.einsum("tsf,dsf->td", gate_up_grad, in_back, preferred_element_type=jnp.float32)
    )
    middle_norm_grad, gain_two_part = norm_backward(
        normed_two_grad, scaled_two, inverse_two, gain_two, full_width
    )
    middle_grad = grad_rows.astype(jnp.float32) + middle_norm_grad
    branch_grad = middle_grad.astype(jnp.bfloat16)
    out_part = jnp.einsum(
        "td,tf->df", attended_full, branch_grad, preferred_element_type=jnp.float32
    )
    attended_grad = collect(
        jnp.einsum("tf,df->td", branch_grad, out_back, preferred_element_type=jnp.float32)
    ).astype(jnp.bfloat16)
    attended_heads = attended_grad.reshape(rows_here, heads_here, HEAD_DIM)
    query_blocks = []
    key_grad_ext = jnp.zeros((rows_here + 2 * half_window, heads_here, HEAD_DIM), jnp.float32)
    value_grad_ext = jnp.zeros((rows_here + 2 * half_window, heads_here, HEAD_DIM), jnp.float32)
    for block_number in range(block_count):
        block_start = block_number * block_rows
        block_queries = queries[block_start : block_start + block_rows]
        block_keys = padded_keys[block_start : block_start + key_span]
        block_values = padded_values[block_start : block_start + key_span]
        block_grads = attended_heads[block_start : block_start + block_rows]
        masked = block_scores(block_start, block_queries, block_keys)
        probs = jnp.exp(masked - total_blocks[block_number])
        prob_grad = jnp.einsum(
            "qhd,khd->hqk", block_grads, block_values, preferred_element_type=jnp.float32
        )
        inner = jnp.sum(probs * prob_grad, axis=-1, keepdims=True)
        score_grad = (probs * (prob_grad - inner)).astype(jnp.bfloat16)
        query_blocks.append(
            jnp.einsum("hqk,khd->qhd", score_grad, block_keys, preferred_element_type=jnp.float32)
            * score_scale
        )
        key_grad_ext = key_grad_ext.at[block_start : block_start + key_span].add(
            jnp.einsum(
                "hqk,qhd->khd", score_grad, block_queries, preferred_element_type=jnp.float32
            )
            * score_scale
        )
        value_grad_ext = value_grad_ext.at[block_start : block_start + key_span].add(
            jnp.einsum(
                "hqk,qhd->khd",
                probs.astype(jnp.bfloat16),
                block_grads,
                preferred_element_type=jnp.float32,
            )
        )
    grad_pair = jnp.concatenate(
        [key_grad_ext.reshape(-1, head_width), value_grad_ext.reshape(-1, head_width)], axis=1
    )
    rim_rows = jnp.concatenate(
        [grad_pair[:half_window], grad_pair[rows_here + half_window :]], axis=0
    )
    beside_all = with_halo(rim_rows.astype(jnp.bfloat16), (("row", 0),), half_window).astype(
        rim_rows.dtype
    )
    own_grad = grad_pair[half_window : half_window + rows_here]
    own_grad = own_grad.at[:half_window].add(beside_all[:half_window])
    own_grad = own_grad.at[rows_here - half_window :].add(beside_all[3 * half_window :])
    key_grad = own_grad[:, :head_width].reshape(rows_here, heads_here, HEAD_DIM)
    value_grad = own_grad[:, head_width:].reshape(rows_here, heads_here, HEAD_DIM)
    query_grad = jnp.concatenate(query_blocks, axis=0)
    projected_grad = jnp.stack(
        [
            rotate_back(query_grad, cosine, sine_table),
            rotate_back(key_grad, cosine, sine_table),
            value_grad,
        ],
        axis=1,
    )
    projected_grad = projected_grad.reshape(rows_here, 3, head_width).astype(jnp.bfloat16)
    qkv_part = jnp.einsum(
        "td,tsf->dsf", normed_one_full, projected_grad, preferred_element_type=jnp.float32
    )
    normed_one_grad = collect(
        jnp.einsum("tsf,dsf->td", projected_grad, qkv_back, preferred_element_type=jnp.float32)
    )
    token_norm_grad, gain_one_part = norm_backward(
        normed_one_grad, scaled_one, inverse_one, gain_one, full_width
    )
    input_grad = middle_grad + token_norm_grad
    weight_grads = (
        lax.psum_scatter(qkv_part, "row", scatter_dimension=0, tiled=True),
        lax.psum_scatter(out_part, "row", scatter_dimension=0, tiled=True),
        lax.psum_scatter(in_part, "row", scatter_dimension=0, tiled=True),
        lax.psum_scatter(down_part, "row", scatter_dimension=0, tiled=True),
    )
    gain_grads = lax.psum((gain_one_part, gain_two_part), "row")
    mixed_out = mixed.reshape(1, pair_rows, 2 * tok_width)
    input_out = input_grad.reshape(1, pair_rows, 2 * tok_width)
    return (
        mixed_out,
        input_out,
        gain_grads[0],
        weight_grads[0],
        weight_grads[1],
        gain_grads[1],
        weight_grads[2],
        weight_grads[3],
    )


F32 = jnp.float32
BF = jnp.bfloat16
MESH = pl.DeviceIdType.MESH
ROWS = (96, 96, 144)
COLS = (768, 512, 256)
SPLIT = (48, 48, 64)
OWN = 256
EXT = 384
HALF = 64


def dot(a, b):
    return lax.dot_general(a, b, (((1,), (0,)), ((), ())), preferred_element_type=F32)


def dot_nt(a, b):
    return lax.dot_general(a, b, (((1,), (1,)), ((), ())), preferred_element_type=F32)


def dot_tn(a, b):
    return lax.dot_general(a, b, (((0,), (0,)), ((), ())), preferred_element_type=F32)


SCHEDULE = (
    ("gather_z", 0, 0), ("gather_z", 1, 0), ("gather_xy", 1, 0), ("gather_xy", 0, 0),
    ("gather_z", 0, 1), ("gather_xy", 0, 1), ("gather_z", 1, 1), ("gather_xy", 1, 1),
    ("gather_z", 2, 0), ("tables",), ("gather_xy", 2, 0), ("gather_z", 0, 2),
    ("gather_second_x", 1, 1), ("gather_xy", 0, 2), ("gather_z", 2, 1), ("gather_z", 1, 2),
    ("gather_z", 2, 2), ("send_tokens",), ("gather_xy", 1, 2), ("gather_xy", 2, 1),
    ("gather_second_y", 0, 1), ("gather_second_x", 0, 2), ("gather_second_y", 1, 0),
    ("gather_second_x", 0, 1), ("gather_second_y", 0, 2), ("gather_second_y", 2, 0),
    ("gather_second_x", 2, 0), ("gather_z", 0, 3), ("gather_xy", 0, 3), ("gather_z", 2, 3),
    ("gather_second_x", 1, 0), ("gather_z", 1, 3), ("gather_second_y", 1, 1),
    ("gather_third", 2, 0), ("gather_second_y", 2, 1), ("gather_second_x", 2, 1),
    ("gather_second_y", 0, 3), ("gather_third", 0, 1), ("gather_third", 0, 2),
    ("gather_done", 2, 0), ("gather_done", 0, 1), ("gather_second_x", 0, 3), ("send_cotangent",),
    ("gather_third", 1, 0), ("gather_xy", 2, 3), ("gather_third", 1, 1), ("take_tokens",),
    ("gather_second_x", 1, 2), ("gather_second_y", 0, 0), ("gather_second_x", 0, 0),
    ("gather_third", 2, 1), ("norm_one",), ("gather_third", 0, 3), ("forward_heads", 1),
    ("gather_xy", 1, 3), ("gather_xy", 2, 2), ("gather_done", 0, 2), ("gather_second_y", 1, 2),
    ("gather_done", 0, 3), ("forward_heads", 3), ("gather_third", 0, 0), ("gather_done", 2, 1),
    ("gather_second_y", 2, 3), ("forward_heads", 2), ("gather_second_x", 2, 3),
    ("gather_done", 1, 0), ("gather_done", 0, 0), ("gather_second_x", 1, 3),
    ("gather_done", 1, 1), ("gather_second_y", 1, 3), ("gather_second_x", 2, 2),
    ("forward_heads", 0), ("gather_third", 1, 2), ("gather_second_y", 2, 2), ("forward_middle",),
    ("gather_third", 2, 3), ("forward_hidden", 1), ("forward_hidden", 0), ("gather_third", 1, 3),
    ("gather_done", 1, 2), ("take_cotangent",), ("gather_done", 2, 3), ("gather_third", 2, 2),
    ("forward_hidden", 2), ("gather_done", 1, 3), ("forward_hidden", 3), ("gather_done", 2, 2),
    ("forward_tail",), ("backward_tail",), ("grad_down",), ("grad_tail",), ("backward_hidden", 3),
    ("backward_hidden", 0), ("sum_first", 2, 1), ("backward_hidden", 2), ("backward_hidden", 1),
    ("sum_first", 2, 0), ("sum_first", 2, 2), ("grad_in", 3), ("grad_in", 1), ("grad_in", 0),
    ("sum_first", 1, 0), ("sum_first", 2, 3), ("sum_first", 1, 1), ("sum_second", 2, 0),
    ("sum_second", 2, 1), ("sum_second", 2, 2), ("backward_middle",), ("sum_second", 1, 0),
    ("sum_second", 2, 3), ("forward_mixed",), ("sum_second", 1, 1), ("grad_in", 2),
    ("sum_first", 1, 2), ("backward_heads", 3), ("backward_heads", 1), ("sum_second", 1, 2),
    ("backward_heads", 0), ("backward_heads", 2), ("backward_first",), ("halo_send",),
    ("sum_third_x", 1, 0), ("grad_out",), ("grad_qkv", 0), ("sum_third_y", 1, 0),
    ("sum_first", 0, 0), ("sum_third_x", 2, 0), ("grad_qkv", 1), ("sum_third_x", 2, 1),
    ("sum_third_y", 2, 0), ("sum_first", 0, 1), ("sum_second", 0, 0), ("halo_take",),
    ("backward_last",), ("sum_third_x", 1, 1), ("sum_second", 0, 1), ("sum_third_y", 1, 1),
    ("sum_third_x", 0, 0), ("sum_first", 1, 3), ("sum_third_y", 2, 1), ("sum_third_x", 1, 2),
    ("sum_third_x", 2, 3), ("grad_qkv", 2), ("sum_third_y", 0, 0), ("sum_third_y", 2, 2),
    ("sum_third_x", 2, 2), ("sum_first", 0, 2), ("sum_third_y", 1, 2), ("sum_fourth", 2, 0),
    ("sum_second", 0, 2), ("sum_fourth", 1, 0), ("finish", "mx"), ("sum_third_x", 0, 1),
    ("grad_qkv", 3), ("sum_first", 0, 3), ("sum_third_y", 0, 1), ("sum_fourth", 2, 1),
    ("sum_second", 1, 3), ("sum_fourth", 0, 0), ("sum_fourth", 1, 1), ("sum_second", 0, 3),
    ("sum_third_y", 0, 2), ("sum_fourth", 2, 2), ("sum_third_x", 0, 2), ("sum_third_y", 2, 3),
    ("sum_fourth", 0, 1), ("finish", "ig"), ("sum_fourth", 1, 2), ("sum_third_y", 1, 3),
    ("sum_third_y", 0, 3), ("sum_third_x", 0, 3), ("sum_third_x", 1, 3), ("gains_first",),
    ("sum_fourth", 0, 2), ("sum_fourth", 1, 3), ("sum_fourth", 0, 3), ("sum_fourth", 2, 3),
    ("gains_last",), ("sum_last", 1), ("sum_last", 2), ("sum_last", 0), ("unpack_outs",),
)


class Link:
    def __init__(self, src, dst, send, recv, row, col, when=None):
        self.args = (src, dst, send, recv)
        self.device = {"row": row, "col": col}
        self.when = when

    def make(self):
        src, dst, send, recv = self.args
        return pltpu.make_async_remote_copy(
            src_ref=src,
            dst_ref=dst,
            send_sem=send,
            recv_sem=recv,
            device_id=self.device,
            device_id_type=MESH,
        )

    def run(self, step):
        if self.when is None:
            step()
        else:
            pl.when(self.when)(step)

    def start(self):
        self.run(lambda: self.make().start())

    def sent(self):
        self.run(lambda: self.make().wait_send())


def arrived(dst, recv, row, col):
    pltpu.make_async_remote_copy(
        src_ref=dst,
        dst_ref=dst,
        send_sem=recv,
        recv_sem=recv,
        device_id={"row": row, "col": col},
        device_id_type=MESH,
    ).wait_recv()


def at_rows(ref, lead, start, size):
    return ref.at[lead, pl.ds(start, size), :]


def lane_iota(shape):
    return lax.broadcasted_iota(jnp.int32, shape, 1)


def swap_halves(tile):
    first = (lane_iota(tile.shape) % 64) < 32
    return jnp.where(first, pltpu.roll(tile, 96, 1), pltpu.roll(tile, 32, 1))


def layer_kernel(
    tok_in, cot_in, qkv_in, out_in, in_in, down_in, gain_one_in, gain_two_in, ids_in, freq_in,
    mixed_out, input_out, qkv_out, out_out, in_out, down_out, gain_one_out, gain_two_out,
    got_x, got_g, got_gain, w1, w2, w3, d1, d2, d3,
    core1, core2, core3, xa1, xa2, xa3, xb1, xb2, xb3, ya1, ya2, ya3, yb1, yb2, yb3,
    zl1, zl2, zl3, zr1, zr2, zr3,
    gains_in, own_ids, x_all, cos_t, sin_t, bias, n1, hat1, stat, qs, ks, vs, probs, att_c, att, mid, hat2, n2,
    tail_in, tail_down, hid, hid_tail, gel, gel_up, gel_t, gel_up_t, cot_pad, d_gate, d_tail,
    mid_grad, branch_pad, att_grad, d_proj, n1_grad,
    halo_out, halo_left, halo_right, mixed_send, mixed_got, input_send, input_got,
    gain_part, gain_z, gain_sum, gain_all, grad_one, grad_two, grad_three,
    tok_s, tok_r, tok_rl, tok_rr, cot_s, cot_r, gn_s, gn_r,
    az_s, az_r, ax_s, ax_r, ay_s, ay_r, ac_s, ac_r,
    rc_s, rc_r, rx_s, rx_r, ry_s, ry_r, rz_s, rz_r,
    io_s, ha_s, ha_r, mx_s, mx_r, ig_s, ig_r, gz_s, gz_r, gp_s, gp_r,
    *, start_of,
):
    row = lax.axis_index("row")
    z = lax.axis_index("col")
    core = row % 2
    xc = (row // 2) % 2
    yc = row // 4
    rx = row + 2 - 4 * xc
    ry = row + 4 - 8 * yc
    rxy = ry + 2 - 4 * xc
    rc = row + 1 - 2 * core
    ws = (w1, w2, w3)
    ds_ = (d1, d2, d3)
    sent = []

    def go(link):
        link.start()
        sent.append(link)

    barrier = pltpu.get_barrier_semaphore()

    def greet(r, c):
        pl.semaphore_signal(barrier, inc=1, device_id={"row": r, "col": c}, device_id_type=MESH)

    for step in range(1, 8):
        greet((row + step) % 8, z)
    for step in range(1, 4):
        greet(row, (z + step) % 4)
    up, down = row < 7, row > 0
    low_end, high_end = (z == 0) & down, (z == 3) & up
    pl.when(down)(lambda: greet(row - 1, 3))
    pl.when(up)(lambda: greet(row + 1, 0))

    @pl.when(low_end)
    def _():
        for c in range(4):
            greet(row - 1, c)

    @pl.when(high_end)
    def _():
        for c in range(4):
            greet(row + 1, c)

    peers = 10 + jnp.minimum(row, 1) + jnp.minimum(7 - row, 1)
    peers += 4 * jnp.maximum(1 - z, 0) * jnp.minimum(row, 1)
    peers += 4 * jnp.maximum(z - 2, 0) * jnp.minimum(7 - row, 1)
    def window(c):
        low, high = max(0, 128 * c - 32), min(512, 128 * c + 160)
        return low, high - low, low - (128 * c - 32)

    def send_tokens():
        for c in range(4):
            low, size, to = window(c)
            go(Link(tok_in.at[pl.ds(low, size), :], at_rows(got_x, z, to, size),
                    tok_s.at[c], tok_r.at[z], row, c, z != c))
        go(Link(tok_in.at[pl.ds(0, 32), :], at_rows(got_x, z, 160, 32),
                tok_s.at[4], tok_rr.at[z], row - 1, 3, down))
        go(Link(tok_in.at[pl.ds(480, 32), :], at_rows(got_x, z, 0, 32),
                tok_s.at[5], tok_rl.at[z], row + 1, 0, up))
        for step in range(1, 4):
            c = (z + step) % 4
            go(Link(gains_in, got_gain.at[z], gn_s.at[step], gn_r.at[z], row, c))

    def send_cotangent():
        for step in range(1, 4):
            c = (z + step) % 4
            go(Link(cot_in.at[pl.ds(pl.multiple_of(c * 128, 128), 128), :], got_g.at[z],
                    cot_s.at[step], cot_r.at[z], row, c))

    order = (z, 1 + z % 2, 2 - 2 * (z % 2) + z // 2, 3 - 3 * (z // 2))

    def near(i, c, r, part):
        size, cut = ROWS[i], SPLIT[i]
        start, count = {"all": (0, size), "a": (0, cut), "b": (cut, size - cut)}[part]
        return at_rows(ws[i], c, pl.multiple_of(r * size + start, 16), count)

    def gather_link(i, c, r, part, sem_s, sem_r, to_row, to_col, when=None):
        ref = near(i, c, r, part)
        return Link(ref, ref, sem_s, sem_r, to_row, to_col, when)

    def gather_z(i, j):
        c = order[j]
        if j == 0:
            go(gather_link(i, c, row, "all", az_s.at[i, 0, c], az_r.at[i, c], row, z + 1, z < 3))
            go(gather_link(i, c, row, "all", az_s.at[i, 1, c], az_r.at[i, c], row, z - 1, z > 0))
        else:
            arrived(near(i, c, row, "all"), az_r.at[i, c], row, z)
            go(gather_link(i, c, row, "all", az_s.at[i, 0, c], az_r.at[i, c], row, z + 1,
                           (c < z) & (z < 3)))
            go(gather_link(i, c, row, "all", az_s.at[i, 1, c], az_r.at[i, c], row, z - 1,
                           (c > z) & (z > 0)))

    def gather_xy(i, j):
        c = order[j]
        go(gather_link(i, c, row, "a", ax_s.at[i, c, 0], ax_r.at[i, c, 0], rx, z))
        go(gather_link(i, c, row, "b", ay_s.at[i, c, 0], ay_r.at[i, c, 0], ry, z))
        go(gather_link(i, c, row, "b", ax_s.at[i, c, 1], ax_r.at[i, c, 1], rx, z))
        go(gather_link(i, c, row, "a", ay_s.at[i, c, 1], ay_r.at[i, c, 1], ry, z))
        go(gather_link(i, c, row, "all", ac_s.at[i, c, 0], ac_r.at[i, c, 0], rc, z))

    def gather_second_x(i, j):
        c = order[j]
        arrived(near(i, c, rx, "a"), ax_r.at[i, c, 0], rx, z)
        go(gather_link(i, c, rx, "a", ay_s.at[i, c, 2], ay_r.at[i, c, 2], ry, z))

    def gather_second_y(i, j):
        c = order[j]
        arrived(near(i, c, ry, "b"), ay_r.at[i, c, 0], ry, z)
        go(gather_link(i, c, ry, "b", ax_s.at[i, c, 2], ax_r.at[i, c, 2], rx, z))

    def gather_third(i, j):
        c = order[j]
        arrived(near(i, c, rx, "b"), ax_r.at[i, c, 1], rx, z)
        go(gather_link(i, c, rx, "all", ac_s.at[i, c, 1], ac_r.at[i, c, 1], rc, z))
        arrived(near(i, c, ry, "a"), ay_r.at[i, c, 1], ry, z)
        go(gather_link(i, c, ry, "all", ac_s.at[i, c, 2], ac_r.at[i, c, 2], rc, z))
        arrived(near(i, c, rxy, "a"), ay_r.at[i, c, 2], ry, z)
        arrived(near(i, c, rxy, "b"), ax_r.at[i, c, 2], rx, z)
        go(gather_link(i, c, rxy, "all", ac_s.at[i, c, 3], ac_r.at[i, c, 3], rc, z))

    def gather_done(i, j):
        for c in (order[j],):
            for n, r in enumerate((row, rx, ry, rxy)):
                arrived(near(i, c, r + 1 - 2 * core, "all"), ac_r.at[i, c, n], rc, z)

    def pack_own():
        r96 = pl.ds(pl.multiple_of(row * 96, 16), 96)
        r144 = pl.ds(pl.multiple_of(row * 144, 16), 144)
        q, k, v = qkv_in[0], qkv_in[1], qkv_in[2]
        gate, other = in_in[:, 0, :], in_in[:, 1, :]
        w1[z, r96, :] = jnp.concatenate(
            [q[:, :128], k[:, :128], v[:, :128], q[:, 128:], k[:, 128:], v[:, 128:],
             out_in[...]], axis=1)
        w2[z, r96, :] = jnp.concatenate([gate[:, :256], other[:, :256]], axis=1)
        tail = jnp.concatenate([gate[:, 256:], other[:, 256:]], axis=1)
        tail = jnp.concatenate([tail, jnp.zeros((48, 64), BF)], axis=0)
        w3[z, r144, :] = jnp.concatenate([down_in[...], tail], axis=1)
        gains_in[...] = jnp.zeros((8, 256), F32)
        gains_in[0:1, 0:192] = gain_one_in[...].reshape(1, 192)
        gains_in[1:2, 0:192] = gain_two_in[...].reshape(1, 192)

    def take_tokens():
        for c in range(4):
            low, size, to = window(c)

            @pl.when(z == c)
            def _():
                got_x[c, to : to + size, :] = tok_in[low : low + size, :]
                for other in range(4):
                    if other != c:
                        arrived(at_rows(got_x, other, to, size), tok_r.at[other], row, other)

        @pl.when(low_end)
        def _():
            for other in range(4):
                arrived(at_rows(got_x, other, 0, 32), tok_rl.at[other], row - 1, other)

        @pl.when(high_end)
        def _():
            for other in range(4):
                arrived(at_rows(got_x, other, 160, 32), tok_rr.at[other], row + 1, other)

        @pl.when((z == 0) & (row == 0))
        def _():
            got_x[:, 0:32, :] = jnp.zeros((4, 32, 384), BF)

        @pl.when((z == 3) & (row == 7))
        def _():
            got_x[:, 160:192, :] = jnp.zeros((4, 32, 384), BF)

        got_gain[pl.ds(z, 1)] = gains_in[...][None]
        for step in range(1, 4):
            c = (z + step) % 4
            arrived(got_gain.at[c], gn_r.at[c], row, c)
        at = 0
        for low, high, lane in ((32, 160, 0), (32, 160, 192), (0, 32, 0), (0, 32, 192),
                                (160, 192, 0), (160, 192, 192)):
            x_all[at : at + high - low, :] = jnp.concatenate(
                [got_x[c, low:high, lane : lane + 192].astype(F32) for c in range(4)], axis=1)
            at += high - low

    def gain_row(which):
        return jnp.concatenate([got_gain[c, which : which + 1, 0:192] for c in range(4)], axis=1)

    def window_ids(first, length):
        last = ids_in.shape[0] - 1
        spot = first // 128
        near_rows = [ids_in[pl.ds(jnp.clip(spot + n, 0, last), 1), :] for n in range(-1, 3)]
        base = near_rows[1][0:1, 0:1]
        rel = jnp.concatenate(near_rows, axis=0) - base
        rel = jnp.clip(rel, -200, 200).astype(BF)
        source = lax.broadcasted_iota(jnp.int32, (128, 128), 0)
        target = lane_iota((128, 128))
        pick = (source == jnp.where(target < 64, 2 * target, 2 * target - 127)).astype(BF)
        rel = jnp.concatenate([rel, jnp.zeros((4, 128), BF)], axis=0)
        rel = dot(rel, pick)
        keys = jnp.concatenate(
            [rel[1:2, :64], rel[2:3, :64], rel[1:2, 64:], rel[2:3, 64:], rel[0:1, 32:64],
             rel[0:1, 96:], rel[3:4, :32], rel[3:4, 64:96]], axis=1)
        lane = lane_iota((1, EXT))
        lost = (lane >= 256) & (lane < 320) & (first % length == 0)
        lost |= (lane >= 320) & ((first + OWN) % length == 0)
        keys = jnp.where(lost, 1000.0, keys)
        own_ids[...] = jnp.broadcast_to(keys[:, :OWN], (8, OWN))
        return keys, own_ids[...].T[:, 0:1]

    def tables():
        spot = lax.broadcasted_iota(jnp.int32, (EXT, 128), 0)
        halo = spot - 256
        place = jnp.where(
            spot < 128, 2 * spot, jnp.where(
                spot < 256, 2 * spot - 255, jnp.where(
                    halo < 32, 2 * halo - 64, jnp.where(
                        halo < 64, 2 * halo - 127, jnp.where(
                            halo < 96, 2 * halo + 128, 2 * halo + 65)))))
        first, length = start_of(row, z)
        place = (place + first + length) % length
        angle = place.astype(F32) * freq_in[0:1, :]
        cos_t[...] = jnp.cos(angle)
        turn = jnp.where((lane_iota((EXT, 128)) % 64) < 32, -1.0, 1.0)
        sin_t[...] = jnp.sin(angle) * turn
        key_ids, query_ids = window_ids(first, length)
        qrow = lax.broadcasted_iota(jnp.int32, (OWN, EXT), 0)
        qplace = jnp.where(qrow < 128, 2 * qrow, 2 * qrow - 255)
        kcol = lane_iota((OWN, EXT))
        khalo = kcol - 256
        kplace = jnp.where(
            kcol < 128, 2 * kcol, jnp.where(
                kcol < 256, 2 * kcol - 255, jnp.where(
                    khalo < 32, 2 * khalo - 64, jnp.where(
                        khalo < 64, 2 * khalo - 127, jnp.where(
                            khalo < 96, 2 * khalo + 128, 2 * khalo + 65)))))
        allowed = (jnp.abs(qplace - kplace) <= HALF) & (query_ids == key_ids)
        bias[...] = jnp.where(allowed, 0.0, -1e30)

    def statistics(v):
        mu = jnp.mean(v, axis=1, keepdims=True)
        inv = lax.rsqrt(jnp.mean(v * v, axis=1, keepdims=True) - mu * mu + EPSILON)
        return (v - mu) * inv, inv

    def norm_one():
        hat, inv = statistics(x_all[0:OWN, :])
        hat1[...] = hat
        stat[0] = jnp.broadcast_to(inv, (OWN, 128))
        gain = gain_row(0)
        n1[0:OWN, :] = (hat * gain).astype(BF)
        hat, _ = statistics(x_all[OWN:EXT, :])
        n1[OWN:EXT, :] = (hat * gain).astype(BF)

    def take_cotangent():
        got_g[pl.ds(z, 1)] = cot_in[pl.ds(pl.multiple_of(z * 128, 128), 128), :][None]
        for step in range(1, 4):
            c = (z + step) % 4
            arrived(got_g.at[c], cot_r.at[c], row, c)
        pad = jnp.zeros((128, 64), BF)
        for c in range(4):
            for odd in range(2):
                cot_pad[128 * odd : 128 * odd + 128, 256 * c : 256 * c + 256] = jnp.concatenate(
                    [got_g[c, :, 192 * odd : 192 * odd + 192], pad], axis=1)

    low_lanes = lambda shape: lane_iota(shape) < 64

    def forward_heads(j):
        c = order[j]
        proj = dot(n1[...], w1[c, :, 0:640])
        cos, sin = cos_t[...], sin_t[...]
        rot = lambda tile, n: tile * cos[0:n] + swap_halves(tile) * sin[0:n]
        qs[c, 0] = (rot(proj[0:OWN, 0:128], OWN) * 0.125).astype(BF)
        ks[c, 0] = rot(proj[:, 128:256], EXT).astype(BF)
        vs[c, 0] = proj[:, 256:384].astype(BF)
        third = rot(proj[:, 384:512], EXT)
        low = low_lanes((EXT, 128))
        qs[c, 1] = jnp.where(low[0:OWN], third[0:OWN] * 0.125, 0.0).astype(BF)
        ks[c, 1] = jnp.where(low, pltpu.roll(third, 64, 1), 0.0).astype(BF)
        vs[c, 1] = jnp.where(low, proj[:, 512:640], 0.0).astype(BF)

        def head(h, q, k):
            scores = dot_nt(q, k) + bias[...]
            weight = jnp.exp(scores - jnp.max(scores, axis=1, keepdims=True))
            weight = weight * (1.0 / jnp.sum(weight, axis=1, keepdims=True))
            probs[3 * c + h] = weight
            return weight.astype(BF)

        zero = jnp.zeros((), BF)
        lowq, lowk = low_lanes((OWN, 128)), low
        q, k, v = qs[c, 0], ks[c, 0], vs[c, 0]
        both = dot(head(0, jnp.where(lowq, q, zero), k), jnp.where(lowk, v, zero))
        both += dot(head(1, jnp.where(lowq, zero, q), k), jnp.where(lowk, zero, v))
        att_c[c, :, 0:128] = both.astype(BF)
        att_c[c, :, 128:256] = dot(head(2, qs[c, 1], ks[c, 1]), vs[c, 1]).astype(BF)

    def forward_middle():
        for c in range(4):
            att[:, 192 * c : 192 * c + 192] = att_c[c, :, 0:192]
        for c in range(4):
            out = dot(att[...], w1[c, :, 512:768])
            mid[:, 192 * c : 192 * c + 192] = (
                x_all[0:OWN, 192 * c : 192 * c + 192] + out[:, 64:256])
        hat, inv = statistics(mid[...])
        hat2[...] = hat
        stat[1] = jnp.broadcast_to(inv, (OWN, 128))
        n2[...] = (hat * gain_row(1)).astype(BF)

    def gelu_parts(g):
        phi = 0.5 * (1.0 + lax.erf(g * 0.7071067811865476))
        return g * phi, phi + g * (jnp.exp(g * g * -0.5) * 0.3989422804014327)

    def forward_hidden(j):
        c = order[j]
        both = dot(n2[...], w2[c])
        value, slope = gelu_parts(both[:, 0:256])
        other = both[:, 256:512]
        gel[c] = value
        gel_up[c] = other * slope
        hid[c] = (value * other).astype(BF)

    def forward_tail():
        for c in range(4):
            for r in range(8):
                tail_in[96 * r : 96 * r + 96, 128 * c : 128 * c + 128] = (
                    w3[c, 144 * r : 144 * r + 96, 128:256])
                if r < 4:
                    tail_down[c, 32 * r : 32 * r + 32, :] = (
                        w3[c, 288 * r + 256 : 288 * r + 288, :])
        tails = dot(n2[...], tail_in[...])
        lanes = lane_iota((OWN, 128)) // 32
        packed = jnp.zeros((OWN, 128), F32)
        for c in range(4):
            tile = tails[:, 128 * c : 128 * c + 128]
            value, slope = gelu_parts(tile)
            other = pltpu.roll(tile, 96, 1)
            gel_t[c] = value
            gel_up_t[c] = other * slope
            moved = pltpu.roll(value * other, (32 * c + 64) % 128, 1)
            packed = jnp.where(lanes == c, moved, packed)
        hid_tail[...] = packed.astype(BF)

    def forward_mixed():
        for k in range(4):
            total = dot(hid_tail[...], tail_down[k])
            for c in range(4):
                total += dot(hid[c], w3[k, 288 * c : 288 * c + 256, :])
            out = (mid[:, 192 * k : 192 * k + 192] + total[:, 0:192]).astype(BF)
            mixed_send[k] = jnp.concatenate([out[0:128], out[128:256]], axis=1)
        for step in range(1, 4):
            c = (z + step) % 4
            go(Link(mixed_send.at[c], mixed_got.at[z], mx_s.at[step], mx_r.at[z], row, c))

    def backward_hidden(c):
        grad = dot_nt(cot_pad[:, 0:256], w3[0, 288 * c : 288 * c + 256, :])
        for k in range(1, 4):
            grad += dot_nt(cot_pad[:, 256 * k : 256 * k + 256], w3[k, 288 * c : 288 * c + 256, :])
        d_gate[c] = jnp.concatenate([grad * gel_up[c], grad * gel[c]], axis=1).astype(BF)

    def backward_tail():
        grad = dot_nt(cot_pad[:, 0:256], tail_down[0])
        for k in range(1, 4):
            grad += dot_nt(cot_pad[:, 256 * k : 256 * k + 256], tail_down[k])
        lanes = lane_iota((OWN, 128))
        for c in range(4):
            gate = pltpu.roll(grad, (64 - 32 * c) % 128, 1) * gel_up_t[c]
            other = pltpu.roll(grad, (96 - 32 * c) % 128, 1) * pltpu.roll(gel_t[c], 32, 1)
            d_tail[:, 128 * c : 128 * c + 128] = jnp.where(
                lanes >= 96, other, jnp.where(lanes >= 64, gate, 0.0)).astype(BF)

    def grad_down():
        for c in range(4):
            part = dot_tn(hid[c], cot_pad[...]).astype(BF)
            for k in range(4):
                d3[k, 288 * c : 288 * c + 256, :] = part[:, 256 * k : 256 * k + 256]
        part = dot_tn(hid_tail[...], cot_pad[...]).astype(BF)
        for c in range(4):
            for k in range(4):
                d3[k, 288 * c + 256 : 288 * c + 288, :] = (
                    part[32 * c : 32 * c + 32, 256 * k : 256 * k + 256])

    def grad_tail():
        part = dot_tn(n2[...], d_tail[...]).astype(BF)
        for c in range(4):
            for r in range(8):
                d3[c, 144 * r : 144 * r + 96, 128:256] = (
                    d3[c, 144 * r : 144 * r + 96, 128:256]
                    + part[96 * r : 96 * r + 96, 128 * c : 128 * c + 128])

    def grad_in(j):
        c = order[3 - j]
        d2[c] = dot_tn(n2[...], d_gate[c]).astype(BF)

    def norm_back(grad, hat, inv, gain):
        e = grad * gain
        return inv * (e - jnp.mean(e, axis=1, keepdims=True)
                      - hat * jnp.mean(e * hat, axis=1, keepdims=True))

    def backward_middle():
        grad = dot_nt(d_tail[...], tail_in[...])
        for c in range(4):
            grad += dot_nt(d_gate[c], w2[c])
        hat = hat2[...]
        gain_part[1:2, :] = jnp.sum(grad * hat, axis=0, keepdims=True)
        back = norm_back(grad, hat, stat[1][:, 0:1], gain_row(1))
        pad = jnp.zeros((OWN, 64), BF)
        total = jnp.concatenate(
            [cot_pad[:, 256 * c : 256 * c + 192].astype(F32) for c in range(4)], axis=1) + back
        mid_grad[...] = total
        branch = total.astype(BF)
        for c in range(4):
            branch_pad[:, 256 * c : 256 * c + 256] = jnp.concatenate(
                [pad, branch[:, 192 * c : 192 * c + 192]], axis=1)
        grad = dot_nt(branch_pad[:, 0:256], w1[0, :, 512:768])
        for c in range(1, 4):
            grad += dot_nt(branch_pad[:, 256 * c : 256 * c + 256], w1[c, :, 512:768])
        grad = grad.astype(BF)
        for c in range(4):
            att_grad[c] = jnp.concatenate([grad[:, 192 * c : 192 * c + 192], pad], axis=1)

    def grad_out():
        part = dot_tn(att[...], branch_pad[...]).astype(BF)
        for c in range(4):
            d1[c, :, 512:768] = part[:, 256 * c : 256 * c + 256]

    def backward_heads(j):
        c = order[3 - j]
        zero = jnp.zeros((), BF)
        lowq, lowk = low_lanes((OWN, 128)), low_lanes((EXT, 128))

        def head(h, g, v):
            weight = probs[3 * c + h]
            prob_grad = dot_nt(g, v)
            inner = jnp.sum(weight * prob_grad, axis=1, keepdims=True)
            return (weight * (prob_grad - inner)).astype(BF), weight.astype(BF)

        q, k, v = qs[c, 0], ks[c, 0], vs[c, 0]
        g = att_grad[c, :, 0:128]
        g0, g1 = jnp.where(lowq, g, zero), jnp.where(lowq, zero, g)
        s0, p0 = head(0, g0, v)
        s1, p1 = head(1, g1, v)
        dq = dot(s0, jnp.where(lowk, k, zero)) + dot(s1, jnp.where(lowk, zero, k))
        dk = dot_tn(s0, jnp.where(lowq, q, zero)) + dot_tn(s1, jnp.where(lowq, zero, q))
        dv = dot_tn(p0, g0) + dot_tn(p1, g1)
        g2 = att_grad[c, :, 128:256]
        s2, p2 = head(2, g2, vs[c, 1])
        dq2 = dot(s2, ks[c, 1]) * 0.125
        dk2 = pltpu.roll(dot_tn(s2, qs[c, 1]), 64, 1)
        dv2 = dot_tn(p2, g2)
        cos, sin = cos_t[...], sin_t[...]
        back = lambda tile: tile * cos - swap_halves(tile) * sin
        none = jnp.zeros((EXT - OWN, 128), F32)
        dq = jnp.concatenate([dq * 0.125, none], axis=0)
        d_proj[c, :, 0:128] = back(dq).astype(BF)
        d_proj[c, :, 128:256] = back(dk).astype(BF)
        d_proj[c, :, 256:384] = dv.astype(BF)
        d_proj[c, :, 384:512] = back(jnp.concatenate([dq2, none], axis=0) + dk2).astype(BF)
        d_proj[c, :, 512:640] = dv2.astype(BF)

    def grad_qkv(j):
        c = order[3 - j]
        part = dot_tn(n1[...], d_proj[c]).astype(BF)
        d1[c, :, 0:512] = part[:, 0:512]
        d1[c, :, 512:640] = d1[c, :, 512:640] + part[:, 512:640]

    def backward_first():
        grad = dot_nt(d_proj[0], w1[0, :, 0:640])
        for c in range(1, 4):
            grad += dot_nt(d_proj[c], w1[c, :, 0:640])
        n1_grad[...] = grad[0:OWN]
        halo_out[...] = grad[OWN:EXT].astype(BF)

    edge_low, edge_high = (z == 0) & (row == 0), (z == 3) & (row == 7)
    left_row = jnp.where(z == 0, row - 1, row)
    right_row = jnp.where(z == 3, row + 1, row)
    left_col, right_col = (z + 3) % 4, (z + 1) % 4

    def halo_send():
        go(Link(halo_out.at[pl.ds(0, 64), :], halo_right, ha_s.at[0], ha_r.at[1],
                left_row, left_col, jnp.logical_not(edge_low)))
        go(Link(halo_out.at[pl.ds(64, 64), :], halo_left, ha_s.at[1], ha_r.at[0],
                right_row, right_col, jnp.logical_not(edge_high)))

    def halo_take():
        @pl.when(jnp.logical_not(edge_low))
        def _():
            arrived(halo_left, ha_r.at[0], left_row, left_col)
            n1_grad[0:32, :] += halo_left[0:32, :].astype(F32)
            n1_grad[128:160, :] += halo_left[32:64, :].astype(F32)

        @pl.when(jnp.logical_not(edge_high))
        def _():
            arrived(halo_right, ha_r.at[1], right_row, right_col)
            n1_grad[96:128, :] += halo_right[0:32, :].astype(F32)
            n1_grad[224:256, :] += halo_right[32:64, :].astype(F32)

    def backward_last():
        grad, hat = n1_grad[...], hat1[...]
        gain_part[0:1, :] = jnp.sum(grad * hat, axis=0, keepdims=True)
        total = mid_grad[...] + norm_back(grad, hat, stat[0][:, 0:1], gain_row(0))
        out = total.astype(BF)
        for k in range(4):
            mine = out[:, 192 * k : 192 * k + 192]
            input_send[k] = jnp.concatenate([mine[0:128], mine[128:256]], axis=1)
        for step in range(1, 4):
            c = (z + step) % 4
            go(Link(input_send.at[c], input_got.at[z], ig_s.at[step], ig_r.at[z], row, c))
        for c in range(4):
            gain_part_c = gain_part[0:2, 192 * c : 192 * c + 192]
            gain_sum[c, 0:2, 0:192] = gain_part_c
        for step in range(1, 4):
            c = (z + step) % 4
            go(Link(gain_sum.at[c], gain_z.at[z], gz_s.at[step], gz_r.at[z], row, c))

    cores = (core1, core2, core3)
    xas, xbs, yas, ybs = (xa1, xa2, xa3), (xb1, xb2, xb3), (ya1, ya2, ya3), (yb1, yb2, yb3)
    zls, zrs = (zl1, zl2, zl3), (zr1, zr2, zr3)
    outs = (grad_one, grad_two, grad_three)

    def unpack_outs():
        one, two, three = grad_one[...], grad_two[...], grad_three[...]
        for n in range(3):
            qkv_out[n] = jnp.concatenate(
                [one[:, 128 * n : 128 * n + 128], one[:, 384 + 64 * n : 448 + 64 * n]], axis=1)
        out_out[...] = one[:, 576:768]
        for n in range(2):
            in_out[:, n, :] = jnp.concatenate(
                [two[:, 256 * n : 256 * n + 256], three[0:96, 192 + 32 * n : 224 + 32 * n]],
                axis=1)
        down_out[...] = three[:, 0:192]


    def place(i, c, r, part):
        size, cut = ROWS[i], SPLIT[i]
        start, count = {"all": (0, size), "a": (0, cut), "b": (cut, size - cut)}[part]
        return c, pl.ds(pl.multiple_of(r * size + start, 16), count)

    def piece(i, c, r, part):
        lead, span = place(i, c, r, part)
        return ds_[i].at[lead, span, :]

    def add_into(i, c, r, part, value):
        lead, span = place(i, c, r, part)
        ds_[i][lead, span, :] = ds_[i][lead, span, :] + value

    def sum_first(i, j):
        c = order[3 - j]
        for n in range(4):
            go(Link(piece(i, c, 2 * n + 1 - core, "all"), cores[i].at[c, n],
                    rc_s.at[i, c, n], rc_r.at[i, c, n], rc, z))

    def sum_second(i, j):
        c = order[3 - j]
        for n in range(4):
            arrived(cores[i].at[c, n], rc_r.at[i, c, n], rc, z)
            add_into(i, c, 2 * n + core, "all", cores[i][c, n])
        for y in range(2):
            go(Link(piece(i, c, 4 * y + 2 * (1 - xc) + core, "a"), xas[i].at[c, y],
                    rx_s.at[i, c, y], rx_r.at[i, c, y], rx, z))
        for x in range(2):
            go(Link(piece(i, c, 4 * (1 - yc) + 2 * x + core, "b"), ybs[i].at[c, x],
                    ry_s.at[i, c, x], ry_r.at[i, c, x], ry, z))

    def sum_third_x(i, j):
        c = order[3 - j]
        for y in range(2):
            arrived(xas[i].at[c, y], rx_r.at[i, c, y], rx, z)
            add_into(i, c, 4 * y + 2 * xc + core, "a", xas[i][c, y])
        go(Link(piece(i, c, ry, "a"), yas[i].at[c], ry_s.at[i, c, 2], ry_r.at[i, c, 2], ry, z))

    def sum_third_y(i, j):
        c = order[3 - j]
        for x in range(2):
            arrived(ybs[i].at[c, x], ry_r.at[i, c, x], ry, z)
            add_into(i, c, 4 * yc + 2 * x + core, "b", ybs[i][c, x])
        go(Link(piece(i, c, rx, "b"), xbs[i].at[c], rx_s.at[i, c, 2], rx_r.at[i, c, 2], rx, z))

    def sum_fourth(i, j):
        c = order[3 - j]
        arrived(yas[i].at[c], ry_r.at[i, c, 2], ry, z)
        add_into(i, c, row, "a", yas[i][c])
        arrived(xbs[i].at[c], rx_r.at[i, c, 2], rx, z)
        add_into(i, c, row, "b", xbs[i][c])

        @pl.when((c > z) & (z > 0))
        def _():
            arrived(zls[i].at[c], rz_r.at[i, 0, c], row, z - 1)
            add_into(i, c, row, "all", zls[i][c])

        @pl.when((c < z) & (z < 3))
        def _():
            arrived(zrs[i].at[c], rz_r.at[i, 1, c], row, z + 1)
            add_into(i, c, row, "all", zrs[i][c])

        go(Link(piece(i, c, row, "all"), zls[i].at[c], rz_s.at[i, 0, c], rz_r.at[i, 0, c],
                row, z + 1, c > z))
        go(Link(piece(i, c, row, "all"), zrs[i].at[c], rz_s.at[i, 1, c], rz_r.at[i, 1, c],
                row, z - 1, c < z))

    def sum_last(i):
        lead, span = place(i, z, row, "all")
        outs[i][...] = ds_[i][lead, span, :].astype(F32)

        @pl.when(z > 0)
        def _():
            arrived(zls[i].at[z], rz_r.at[i, 0, z], row, z - 1)
            outs[i][...] = outs[i][...] + zls[i][z].astype(F32)

        @pl.when(z < 3)
        def _():
            arrived(zrs[i].at[z], rz_r.at[i, 1, z], row, z + 1)
            outs[i][...] = outs[i][...] + zrs[i][z].astype(F32)

    def gains_first():
        gain_z[pl.ds(z, 1)] = gain_sum[pl.ds(z, 1)]
        for step in range(1, 4):
            c = (z + step) % 4
            arrived(gain_z.at[c], gz_r.at[c], row, c)
        gain_all[pl.ds(row, 1)] = (gain_z[0] + gain_z[1] + gain_z[2] + gain_z[3])[None]
        for step in range(1, 8):
            go(Link(gain_all.at[row], gain_all.at[row], gp_s.at[step], gp_r.at[row],
                    (row + step) % 8, z))

    def gains_last():
        for step in range(1, 8):
            r = (row + step) % 8
            arrived(gain_all.at[r], gp_r.at[r], r, z)
        total = gain_all[0]
        for r in range(1, 8):
            total = total + gain_all[r]
        gain_one_out[...] = total[0:1, 0:192].reshape(192)
        gain_two_out[...] = total[1:2, 0:192].reshape(192)

    def finish(which):
        out_ref, send, got, sems = {
            "mx": (mixed_out, mixed_send, mixed_got, mx_r),
            "ig": (input_out, input_send, input_got, ig_r),
        }[which]
        got[pl.ds(z, 1)] = send[pl.ds(z, 1)]
        for step in range(1, 4):
            c = (z + step) % 4
            arrived(got.at[c], sems.at[c], row, c)
        for c in range(4):
            out_ref[128 * c : 128 * c + 128, :] = got[c].astype(out_ref.dtype)

    pack_own()
    pl.semaphore_wait(barrier, peers)
    steps = {step.__name__: step for step in (
        send_tokens, send_cotangent, take_tokens, take_cotangent, tables, norm_one, gather_z,
        gather_xy, gather_second_x, gather_second_y, gather_third, gather_done, forward_heads,
        forward_middle, forward_hidden, forward_tail, forward_mixed, backward_hidden,
        backward_tail, grad_down, grad_tail, grad_in, backward_middle, grad_out, backward_heads,
        grad_qkv, backward_first, halo_send, halo_take, backward_last, sum_first, sum_second,
        sum_third_x, sum_third_y, sum_fourth, sum_last, gains_first, gains_last, finish,
        unpack_outs,
    )}
    for name, *where in SCHEDULE:
        steps[name](*where)
    for link in sent:
        link.sent()


def hand_over(*refs):
    for n in range(8):
        refs[8 + n][...] = refs[n][...]


def fast_local(
    tokens, segment_ids, gain_one, qkv_weight, out_weight, gain_two, in_weight, down_weight,
    cotangent,
):
    rows_all = tokens.shape[1] * 2 * lax.axis_size("row")
    length = min(SEQ_MAX, rows_all)

    def start_of(row, z):
        return (row * 4 + z) * OWN, length

    frequency = 10000.0 ** (-(np.arange(HEAD_DIM // 2) * 2.0) / HEAD_DIM)
    frequency = jnp.asarray(np.tile(frequency.astype(np.float32), 4)[None, :].repeat(8, 0))
    vmem, dma = pltpu.VMEM, pltpu.SemaphoreType.DMA
    shapes = [
        vmem((4, 192, 384), BF), vmem((4, 128, 384), BF), vmem((4, 8, 256), F32),
        vmem((4, 768, 768), BF), vmem((4, 768, 512), BF), vmem((4, 1152, 256), BF),
        vmem((4, 768, 768), BF), vmem((4, 768, 512), BF), vmem((4, 1152, 256), BF),
    ]
    shapes += [vmem((4, 4, ROWS[i], COLS[i]), BF) for i in range(3)]
    shapes += [vmem((4, 2, SPLIT[i], COLS[i]), BF) for i in range(3)]
    shapes += [vmem((4, ROWS[i] - SPLIT[i], COLS[i]), BF) for i in range(3)]
    shapes += [vmem((4, SPLIT[i], COLS[i]), BF) for i in range(3)]
    shapes += [vmem((4, 2, ROWS[i] - SPLIT[i], COLS[i]), BF) for i in range(3)]
    shapes += [vmem((4, ROWS[i], COLS[i]), BF) for i in range(3)] * 2
    shapes += [
        vmem((8, 256), F32), vmem((8, OWN), F32),
        vmem((EXT, 768), F32), vmem((EXT, 128), F32), vmem((EXT, 128), F32),
        vmem((OWN, EXT), F32), vmem((EXT, 768), BF), vmem((OWN, 768), F32),
        vmem((2, OWN, 128), F32), vmem((4, 2, OWN, 128), BF), vmem((4, 2, EXT, 128), BF),
        vmem((4, 2, EXT, 128), BF), vmem((12, OWN, EXT), F32),
        vmem((4, OWN, 256), BF), vmem((OWN, 768), BF),
        vmem((OWN, 768), F32), vmem((OWN, 768), F32), vmem((OWN, 768), BF),
        vmem((768, 512), BF), vmem((4, 128, 256), BF), vmem((4, OWN, 256), BF),
        vmem((OWN, 128), BF), vmem((4, OWN, 256), F32), vmem((4, OWN, 256), F32),
        vmem((4, OWN, 128), F32), vmem((4, OWN, 128), F32), vmem((OWN, 1024), BF),
        vmem((4, OWN, 512), BF), vmem((OWN, 512), BF),
        vmem((OWN, 768), F32), vmem((OWN, 1024), BF), vmem((4, OWN, 256), BF),
        vmem((4, EXT, 640), BF), vmem((OWN, 768), F32),
        vmem((128, 768), BF), vmem((64, 768), BF), vmem((64, 768), BF),
        vmem((4, 128, 384), BF), vmem((4, 128, 384), BF),
        vmem((4, 128, 384), BF), vmem((4, 128, 384), BF),
        vmem((8, 768), F32), vmem((4, 8, 256), F32), vmem((4, 8, 256), F32),
        vmem((8, 8, 256), F32), vmem((96, 768), F32), vmem((96, 512), F32), vmem((144, 256), F32),
        dma((6,)), dma((4,)), dma((4,)), dma((4,)), dma((4,)), dma((4,)), dma((4,)), dma((4,)),
        dma((3, 2, 4)), dma((3, 4)), dma((3, 4, 3)), dma((3, 4, 3)), dma((3, 4, 3)),
        dma((3, 4, 3)), dma((3, 4, 4)), dma((3, 4, 4)),
        dma((3, 4, 4)), dma((3, 4, 4)), dma((3, 4, 3)), dma((3, 4, 3)), dma((3, 4, 3)),
        dma((3, 4, 3)), dma((3, 2, 4)), dma((3, 2, 4)),
        dma((8,)), dma((2,)), dma((2,)), dma((4,)), dma((4,)), dma((4,)), dma((4,)), dma((4,)),
        dma((4,)), dma((8,)), dma((8,)),
    ]
    whole = pl.BlockSpec(memory_space=pltpu.VMEM)
    results = (
        jax.ShapeDtypeStruct((512, 384), BF), jax.ShapeDtypeStruct((512, 384), F32),
        jax.ShapeDtypeStruct((3, 96, 192), F32), jax.ShapeDtypeStruct((96, 192), F32),
        jax.ShapeDtypeStruct((96, 2, 288), F32), jax.ShapeDtypeStruct((144, 192), F32),
        jax.ShapeDtypeStruct((192,), F32), jax.ShapeDtypeStruct((192,), F32),
    )
    outs = pl.pallas_call(
        functools.partial(layer_kernel, start_of=start_of),
        out_shape=results,
        in_specs=[whole] * 10,
        out_specs=(whole,) * 8,
        scratch_shapes=shapes,
        compiler_params=pltpu.CompilerParams(
            collective_id=0, has_side_effects=True, vmem_limit_bytes=62 * 1024 * 1024),
    )(tokens[0], cotangent[0], qkv_weight.transpose(1, 0, 2), out_weight, in_weight, down_weight,
      gain_one, gain_two, segment_ids.reshape(-1, 128), frequency)
    mixed, input_grad, qkv_grad, out_grad, in_grad, down_grad, one_grad, two_grad = pl.pallas_call(
        hand_over,
        out_shape=results,
        in_specs=[whole] * 8,
        out_specs=(whole,) * 8,
    )(*outs)
    return (
        mixed[None], input_grad[None], one_grad, qkv_grad.transpose(1, 0, 2), out_grad,
        two_grad, in_grad, down_grad,
    )


def solution(mesh):
    placed = (
        P("col", "row", None),
        P(),
        P("col"),
        P("row", None, "col"),
        P("row", "col"),
        P("col"),
        P("row", None, "col"),
        P("row", "col"),
        P("col", "row", None),
    )
    part = local
    if mesh.shape["row"] == 8 and mesh.shape["col"] == 4:
        part = fast_local
    return jax.shard_map(
        part,
        mesh=mesh,
        in_specs=placed,
        out_specs=(
            P("col", "row", None),
            P("col", "row", None),
            P("col"),
            P("row", None, "col"),
            P("row", "col"),
            P("col"),
            P("row", None, "col"),
            P("row", "col"),
        ),
        check_vma=False,
    )
```

```python
import functools

import jax
import jax.numpy as jnp
import numpy as np
from jax import lax
from jax.experimental import pallas as pl
from jax.experimental.pallas import tpu as pltpu
from jax.sharding import PartitionSpec as P

HEAD_DIM = 64
WINDOW = 128
SEQ_MAX = 4096


EPSILON = 1e-05


def with_halo(block, sides, width):
    for axis, dim in sides:
        count = lax.axis_size(axis)
        forward = [(i, i + 1) for i in range(count - 1)]
        backward = [(target, source) for source, target in forward]
        low = lax.ppermute(
            lax.slice_in_dim(block, block.shape[dim] - width, None, axis=dim), axis, forward
        )
        high = lax.ppermute(lax.slice_in_dim(block, 0, width, axis=dim), axis, backward)
        block = jnp.concatenate([low, block, high], axis=dim)
    return block


def rotate(values, cosine, sine_table):
    half_dim = values.shape[-1] // 2
    turned = jnp.concatenate([-values[..., half_dim:], values[..., :half_dim]], axis=-1)
    return values * cosine + turned * sine_table


def rotate_back(grad_rows, cosine, sine_table):
    half_dim = grad_rows.shape[-1] // 2
    turned = jnp.concatenate([-grad_rows[..., half_dim:], grad_rows[..., :half_dim]], axis=-1)
    return grad_rows * cosine - turned * sine_table


def spread(values):
    return lax.all_gather(values, "col", axis=1, tiled=True)


def collect(partial_rows):
    return lax.psum_scatter(partial_rows, "col", scatter_dimension=1, tiled=True)


def norm_forward(values, full_width):
    row_sums = lax.psum((jnp.sum(values, axis=1), jnp.sum(values * values, axis=1)), "col")
    mean_value = row_sums[0] / full_width
    variance = row_sums[1] / full_width - mean_value * mean_value
    inverse = lax.rsqrt(variance + EPSILON)
    return ((values - mean_value[:, None]) * inverse[:, None], inverse)


def norm_backward(grad_rows, scaled, inverse, gain_part, full_width):
    weighted = grad_rows * gain_part
    row_sums = lax.psum((jnp.sum(weighted, axis=1), jnp.sum(weighted * scaled, axis=1)), "col")
    input_part = inverse[:, None] * (
        weighted - row_sums[0][:, None] / full_width - scaled * (row_sums[1][:, None] / full_width)
    )
    return (input_part, jnp.sum(grad_rows * scaled, axis=0))


def geglu(gate_up):
    return jax.nn.gelu(gate_up[:, 0], approximate=False) * gate_up[:, 1]


def local(
    tokens,
    segment_ids,
    gain_one,
    qkv_weight,
    out_weight,
    gain_two,
    in_weight,
    down_weight,
    cotangent,
):
    pair_rows = tokens.shape[1]
    rows_here = pair_rows * 2
    tok_width = tokens.shape[2] // 2
    full_width = tok_width * lax.axis_size("col")
    heads_here = qkv_weight.shape[2] // HEAD_DIM
    head_width = heads_here * HEAD_DIM
    half_window = WINDOW // 2
    block_rows = min(512, rows_here)
    block_count = rows_here // block_rows
    key_span = block_rows + 2 * half_window
    score_scale = HEAD_DIM ** (-0.5)
    length = min(SEQ_MAX, rows_here * lax.axis_size("row"))
    first_row = lax.axis_index("row") * rows_here
    grad_rows = cotangent.reshape(rows_here, tok_width)
    qkv_full, out_full, in_full, down_full = (
        lax.all_gather(qkv_weight, "row", axis=0, tiled=True),
        lax.all_gather(out_weight, "row", axis=0, tiled=True),
        lax.all_gather(in_weight, "row", axis=0, tiled=True),
        lax.all_gather(down_weight, "row", axis=0, tiled=True),
    )
    global_rows = first_row + jnp.arange(rows_here, dtype=jnp.int32)
    places = (global_rows % length).astype(jnp.float32)
    frequencies = 10000.0 ** (-(jnp.arange(HEAD_DIM // 2, dtype=jnp.float32) * 2.0) / HEAD_DIM)
    angles = places[:, None] * frequencies[None, :]
    angles = jnp.concatenate([angles, angles], axis=1)[:, None, :]
    cosine = jnp.cos(angles)
    sine_table = jnp.sin(angles)
    query_ids = lax.dynamic_slice_in_dim(segment_ids, first_row, rows_here)
    padded_ids = jnp.pad(segment_ids, half_window, constant_values=-1)
    key_ids = lax.dynamic_slice_in_dim(padded_ids, first_row, rows_here + 2 * half_window)
    query_seqs = global_rows // length
    key_seqs = (
        first_row - half_window + jnp.arange(rows_here + 2 * half_window, dtype=jnp.int32)
    ) // length
    offsets = (
        jnp.arange(key_span, dtype=jnp.int32)[None, :]
        - half_window
        - jnp.arange(block_rows, dtype=jnp.int32)[:, None]
    )
    in_window = jnp.abs(offsets) <= half_window

    def block_scores(block_start, block_queries, block_keys):
        same_doc = (
            query_ids[block_start : block_start + block_rows, None]
            == key_ids[None, block_start : block_start + key_span]
        )
        same_seq = (
            query_seqs[block_start : block_start + block_rows, None]
            == key_seqs[None, block_start : block_start + key_span]
        )
        allowed = in_window & same_doc & same_seq
        scores = (
            jnp.einsum(
                "qhd,khd->hqk", block_queries, block_keys, preferred_element_type=jnp.float32
            )
            * score_scale
        )
        return jnp.where(allowed[None], scores, -1e30)

    token_values = tokens.reshape(rows_here, tok_width).astype(jnp.float32)
    scaled_one, inverse_one = norm_forward(token_values, full_width)
    normed_one_full = spread((scaled_one * gain_one).astype(jnp.bfloat16))
    projected = jnp.einsum(
        "td,dsf->tsf", normed_one_full, qkv_full, preferred_element_type=jnp.float32
    )
    projected = projected.reshape(rows_here, 3, heads_here, HEAD_DIM)
    queries = rotate(projected[:, 0], cosine, sine_table).astype(jnp.bfloat16)
    key_rows = rotate(projected[:, 1], cosine, sine_table).astype(jnp.bfloat16)
    value_rows = projected[:, 2].astype(jnp.bfloat16)
    key_value = jnp.concatenate(
        [key_rows.reshape(rows_here, head_width), value_rows.reshape(rows_here, head_width)], axis=1
    )
    padded_pair = with_halo(key_value, (("row", 0),), half_window)
    padded_keys = padded_pair[:, :head_width].reshape(
        rows_here + 2 * half_window, heads_here, HEAD_DIM
    )
    padded_values = padded_pair[:, head_width:].reshape(
        rows_here + 2 * half_window, heads_here, HEAD_DIM
    )
    output_blocks = []
    total_blocks = []
    for block_number in range(block_count):
        block_start = block_number * block_rows
        masked = block_scores(
            block_start,
            queries[block_start : block_start + block_rows],
            padded_keys[block_start : block_start + key_span],
        )
        largest = jnp.max(masked, axis=-1, keepdims=True)
        log_total = largest + jnp.log(jnp.sum(jnp.exp(masked - largest), axis=-1, keepdims=True))
        weights = jnp.exp(masked - log_total).astype(jnp.bfloat16)
        output_blocks.append(
            jnp.einsum(
                "hqk,khd->qhd",
                weights,
                padded_values[block_start : block_start + key_span],
                preferred_element_type=jnp.float32,
            )
        )
        total_blocks.append(log_total)
    attended = (
        jnp.concatenate(output_blocks, axis=0).reshape(rows_here, head_width).astype(jnp.bfloat16)
    )
    attended_full = spread(attended)
    middle = token_values + jnp.dot(attended_full, out_full, preferred_element_type=jnp.float32)
    scaled_two, inverse_two = norm_forward(middle, full_width)
    normed_two_full = spread((scaled_two * gain_two).astype(jnp.bfloat16))
    gate_up = jnp.einsum(
        "td,dsf->tsf", normed_two_full, in_full, preferred_element_type=jnp.float32
    )
    hidden_value, geglu_pull = jax.vjp(geglu, gate_up)
    hidden_full = spread(hidden_value.astype(jnp.bfloat16))
    mixed = (middle + jnp.dot(hidden_full, down_full, preferred_element_type=jnp.float32)).astype(
        jnp.bfloat16
    )
    qkv_back, out_back, in_back, down_back = (
        lax.all_gather(qkv_weight, "row", axis=0, tiled=True),
        lax.all_gather(out_weight, "row", axis=0, tiled=True),
        lax.all_gather(in_weight, "row", axis=0, tiled=True),
        lax.all_gather(down_weight, "row", axis=0, tiled=True),
    )
    down_part = jnp.einsum("tf,td->fd", hidden_full, grad_rows, preferred_element_type=jnp.float32)
    hidden_grad = collect(
        jnp.einsum("td,fd->tf", grad_rows, down_back, preferred_element_type=jnp.float32)
    )
    gate_up_grad = geglu_pull(hidden_grad)[0].astype(jnp.bfloat16)
    in_part = jnp.einsum(
        "td,tsf->dsf", normed_two_full, gate_up_grad, preferred_element_type=jnp.float32
    )
    normed_two_grad = collect(
        jnp.einsum("tsf,dsf->td", gate_up_grad, in_back, preferred_element_type=jnp.float32)
    )
    middle_norm_grad, gain_two_part = norm_backward(
        normed_two_grad, scaled_two, inverse_two, gain_two, full_width
    )
    middle_grad = grad_rows.astype(jnp.float32) + middle_norm_grad
    branch_grad = middle_grad.astype(jnp.bfloat16)
    out_part = jnp.einsum(
        "td,tf->df", attended_full, branch_grad, preferred_element_type=jnp.float32
    )
    attended_grad = collect(
        jnp.einsum("tf,df->td", branch_grad, out_back, preferred_element_type=jnp.float32)
    ).astype(jnp.bfloat16)
    attended_heads = attended_grad.reshape(rows_here, heads_here, HEAD_DIM)
    query_blocks = []
    key_grad_ext = jnp.zeros((rows_here + 2 * half_window, heads_here, HEAD_DIM), jnp.float32)
    value_grad_ext = jnp.zeros((rows_here + 2 * half_window, heads_here, HEAD_DIM), jnp.float32)
    for block_number in range(block_count):
        block_start = block_number * block_rows
        block_queries = queries[block_start : block_start + block_rows]
        block_keys = padded_keys[block_start : block_start + key_span]
        block_values = padded_values[block_start : block_start + key_span]
        block_grads = attended_heads[block_start : block_start + block_rows]
        masked = block_scores(block_start, block_queries, block_keys)
        probs = jnp.exp(masked - total_blocks[block_number])
        prob_grad = jnp.einsum(
            "qhd,khd->hqk", block_grads, block_values, preferred_element_type=jnp.float32
        )
        inner = jnp.sum(probs * prob_grad, axis=-1, keepdims=True)
        score_grad = (probs * (prob_grad - inner)).astype(jnp.bfloat16)
        query_blocks.append(
            jnp.einsum("hqk,khd->qhd", score_grad, block_keys, preferred_element_type=jnp.float32)
            * score_scale
        )
        key_grad_ext = key_grad_ext.at[block_start : block_start + key_span].add(
            jnp.einsum(
                "hqk,qhd->khd", score_grad, block_queries, preferred_element_type=jnp.float32
            )
            * score_scale
        )
        value_grad_ext = value_grad_ext.at[block_start : block_start + key_span].add(
            jnp.einsum(
                "hqk,qhd->khd",
                probs.astype(jnp.bfloat16),
                block_grads,
                preferred_element_type=jnp.float32,
            )
        )
    grad_pair = jnp.concatenate(
        [key_grad_ext.reshape(-1, head_width), value_grad_ext.reshape(-1, head_width)], axis=1
    )
    rim_rows = jnp.concatenate(
        [grad_pair[:half_window], grad_pair[rows_here + half_window :]], axis=0
    )
    beside_all = with_halo(rim_rows.astype(jnp.bfloat16), (("row", 0),), half_window).astype(
        rim_rows.dtype
    )
    own_grad = grad_pair[half_window : half_window + rows_here]
    own_grad = own_grad.at[:half_window].add(beside_all[:half_window])
    own_grad = own_grad.at[rows_here - half_window :].add(beside_all[3 * half_window :])
    key_grad = own_grad[:, :head_width].reshape(rows_here, heads_here, HEAD_DIM)
    value_grad = own_grad[:, head_width:].reshape(rows_here, heads_here, HEAD_DIM)
    query_grad = jnp.concatenate(query_blocks, axis=0)
    projected_grad = jnp.stack(
        [
            rotate_back(query_grad, cosine, sine_table),
            rotate_back(key_grad, cosine, sine_table),
            value_grad,
        ],
        axis=1,
    )
    projected_grad = projected_grad.reshape(rows_here, 3, head_width).astype(jnp.bfloat16)
    qkv_part = jnp.einsum(
        "td,tsf->dsf", normed_one_full, projected_grad, preferred_element_type=jnp.float32
    )
    normed_one_grad = collect(
        jnp.einsum("tsf,dsf->td", projected_grad, qkv_back, preferred_element_type=jnp.float32)
    )
    token_norm_grad, gain_one_part = norm_backward(
        normed_one_grad, scaled_one, inverse_one, gain_one, full_width
    )
    input_grad = middle_grad + token_norm_grad
    weight_grads = (
        lax.psum_scatter(qkv_part, "row", scatter_dimension=0, tiled=True),
        lax.psum_scatter(out_part, "row", scatter_dimension=0, tiled=True),
        lax.psum_scatter(in_part, "row", scatter_dimension=0, tiled=True),
        lax.psum_scatter(down_part, "row", scatter_dimension=0, tiled=True),
    )
    gain_grads = lax.psum((gain_one_part, gain_two_part), "row")
    mixed_out = mixed.reshape(1, pair_rows, 2 * tok_width)
    input_out = input_grad.reshape(1, pair_rows, 2 * tok_width)
    return (
        mixed_out,
        input_out,
        gain_grads[0],
        weight_grads[0],
        weight_grads[1],
        gain_grads[1],
        weight_grads[2],
        weight_grads[3],
    )


F32 = jnp.float32
BF = jnp.bfloat16
MESH = pl.DeviceIdType.MESH
ROWS = (96, 96, 144)
COLS = (768, 512, 256)
SPLIT = (48, 48, 64)
OWN = 256
EXT = 384
HALF = 64


def dot(a, b):
    return lax.dot_general(a, b, (((1,), (0,)), ((), ())), preferred_element_type=F32)


def dot_nt(a, b):
    return lax.dot_general(a, b, (((1,), (1,)), ((), ())), preferred_element_type=F32)


def dot_tn(a, b):
    return lax.dot_general(a, b, (((0,), (0,)), ((), ())), preferred_element_type=F32)


class Link:
    def __init__(self, way, src, dst, recv, row, col, when=None):
        self.way, self.src, self.dst, self.recv = way, src, dst, recv
        self.device = {"row": row, "col": col}
        self.when = when
        self.send = None

    def run(self, step):
        def body():
            copy = pltpu.make_async_remote_copy(
                src_ref=self.src,
                dst_ref=self.dst,
                send_sem=self.send,
                recv_sem=self.recv,
                device_id=self.device,
                device_id_type=MESH,
            )
            step(copy)

        if self.when is None:
            body()
        else:
            pl.when(self.when)(body)


class Ways:
    def __init__(self, **rings):
        self.rings = rings
        self.used = {way: [] for way in rings}

    def go(self, link):
        used, ring = self.used[link.way], self.rings[link.way]
        slot = len(used) % ring.shape[0]
        if len(used) >= ring.shape[0]:
            used[-ring.shape[0]].run(lambda copy: copy.wait_send())
        link.send = ring.at[slot]
        used.append(link)
        link.run(lambda copy: copy.start())

    def drain(self):
        for way, ring in self.rings.items():
            for link in self.used[way][-ring.shape[0] :]:
                link.run(lambda copy: copy.wait_send())


def arrived(ref, recv, row, col):
    pltpu.make_async_remote_copy(
        src_ref=ref,
        dst_ref=ref,
        send_sem=recv,
        recv_sem=recv,
        device_id={"row": row, "col": col},
        device_id_type=MESH,
    ).wait_recv()


def at_rows(ref, lead, start, size):
    return ref.at[lead, pl.ds(start, size), :]


def lane_iota(shape):
    return lax.broadcasted_iota(jnp.int32, shape, 1)


def swap_halves(tile):
    first = (lane_iota(tile.shape) % 64) < 32
    return jnp.where(first, pltpu.roll(tile, 96, 1), pltpu.roll(tile, 32, 1))


def layer_kernel(
    tok_in, cot_in, qkv_in, out_in, in_in, down_in, gain_one_in, gain_two_in, ids_in, freq_in,
    mixed_out, input_out, qkv_out, out_out, in_out, down_out, gain_one_out, gain_two_out,
    got_x, got_g, got_gain, w1, w2, w3, d1, d2, d3,
    core1, core2, core3, xa1, xa2, xa3, xb1, xb2, xb3, ya1, ya2, ya3, yb1, yb2, yb3,
    zb1, zb2, zb3,
    gains_in, own_ids, x_all, cos_t, sin_t, bias, n1, hat1, stat, qs, ks, vs, probs, att_c, att, mid, hat2, n2,
    tail_in, tail_down, hid, hid_tail, gel, gel_up, gel_t, gel_up_t, cot_pad, d_gate, d_tail,
    mid_grad, branch_pad, att_grad, d_proj, n1_grad,
    halo_out, halo_left, halo_right, mixed_send, mixed_got, input_send, input_got,
    relay_tok, relay_cot, relay_mixed, relay_input, gain_part, gain_z, gain_sum, gain_all, grad_one, grad_two, grad_three,
    way_x, way_y, way_z, way_c, io,
    hop_r, tok_r, tok_rl, tok_rr, cot_r, gn_r, az_r, ax_r, ay_r, ac_r,
    rc_r, rx_r, ry_r, rz_r, ha_r, mx_r, ig_r, gz_r, gp_r,
    *, start_of,
):
    row = lax.axis_index("row")
    z = lax.axis_index("col")
    core = row % 2
    xc = (row // 2) % 2
    yc = row // 4
    rx = row + 2 - 4 * xc
    ry = row + 4 - 8 * yc
    rxy = ry + 2 - 4 * xc
    rc = row + 1 - 2 * core
    ws = (w1, w2, w3)
    ds_ = (d1, d2, d3)
    ways = Ways(x=way_x, y=way_y, z=way_z, c=way_c)
    go = ways.go

    barrier = pltpu.get_barrier_semaphore()

    def greet(r, c):
        pl.semaphore_signal(barrier, inc=1, device_id={"row": r, "col": c}, device_id_type=MESH)

    for step in range(1, 8):
        greet((row + step) % 8, z)
    for step in range(1, 4):
        greet(row, (z + step) % 4)
    up, down = row < 7, row > 0
    low_end, high_end = (z == 0) & down, (z == 3) & up
    pl.when(down)(lambda: greet(row - 1, 3))
    pl.when(up)(lambda: greet(row + 1, 0))

    @pl.when(low_end)
    def _():
        for c in range(4):
            greet(row - 1, c)

    @pl.when(high_end)
    def _():
        for c in range(4):
            greet(row + 1, c)

    peers = 10 + jnp.minimum(row, 1) + jnp.minimum(7 - row, 1)
    peers += 4 * jnp.maximum(1 - z, 0) * jnp.minimum(row, 1)
    peers += 4 * jnp.maximum(z - 2, 0) * jnp.minimum(7 - row, 1)
    def window(c):
        low, high = max(0, 128 * c - 32), min(512, 128 * c + 160)
        return low, high - low, low - (128 * c - 32)

    slots = {(2, 1): 0, (3, 1): 1, (3, 2): 2}

    def hop_tok(d, k):
        for c in range(4):
            for way, sign in enumerate((1, -1)):
                s = c - sign * d
                if 0 <= s <= 3:
                    low, size, to = window(c)
                    here = s + sign * k
                    final = k == d - 1

                    @pl.when(z == here)
                    def _():
                        if k > 0:
                            slot = slots[d, k]
                            arrived(relay_tok.at[way, slot, pl.ds(0, size), :],
                                    hop_r.at[0, way, slot], row, here)

                    src = tok_in.at[pl.ds(low, size), :]
                    if k > 0:
                        src = relay_tok.at[way, slots[d, k], pl.ds(0, size), :]
                    if final:
                        dst, recv = got_x.at[s, pl.ds(to, size), :], tok_r.at[0]
                    else:
                        slot = slots[d, k + 1]
                        dst = relay_tok.at[way, slot, pl.ds(0, size), :]
                        recv = hop_r.at[0, way, slot]
                    go(Link("z", src, dst, recv, row, here + sign, z == here))

    def hop(kind, relay, first, last, recv_last, d, k):
        for way, sign in enumerate((1, -1)):
            s, c = z - sign * k, z - sign * k + sign * d
            sends = (s >= 0) & (c <= 3) if sign == 1 else (s <= 3) & (c >= 0)
            src = first(jnp.clip(c, 0, 3))
            if k > 0:
                slot = slots[d, k]
                src = relay.at[way, slot]
                pl.when(sends)(
                    lambda: arrived(relay.at[way, slot], hop_r.at[kind, way, slot], row, z))
            if k == d - 1:
                dst, recv = last(jnp.clip(s, 0, 3)), recv_last.at[0]
            else:
                slot_on = slots[d, k + 1]
                dst, recv = relay.at[way, slot_on], hop_r.at[kind, way, slot_on]
            go(Link("z", src, dst, recv, row, z + sign, sends))

    def lines(ref, c):
        return ref.at[pl.ds(pl.multiple_of(c * 128, 128), 128), :]

    def hop_cot(d, k):
        hop(1, relay_cot, lambda c: lines(cot_in, c), lambda s: got_g.at[s], cot_r, d, k)

    def hop_mixed(d, k):
        hop(2, relay_mixed, lambda c: mixed_send.at[c], lambda s: lines(mixed_got, s), mx_r, d, k)

    def hop_input(d, k):
        hop(3, relay_input, lambda c: input_send.at[c], lambda s: lines(input_got, s), ig_r, d, k)

    def send_gains_in():
        go(Link("z", tok_in.at[pl.ds(0, 32), :], at_rows(got_x, z, 160, 32),
                tok_rr.at[0], row - 1, 3, down))
        go(Link("z", tok_in.at[pl.ds(480, 32), :], at_rows(got_x, z, 0, 32),
                tok_rl.at[0], row + 1, 0, up))
        for step in range(1, 4):
            go(Link("z", gains_in, got_gain.at[z], gn_r.at[0], row, (z + step) % 4))

    def send_gain():
        for step in range(1, 4):
            c = (z + step) % 4
            go(Link("z", gain_sum.at[c], gain_z.at[z], gz_r.at[0], row, c))

    order = (z, 1 + z % 2, 2 - 2 * (z % 2) + z // 2, 3 - 3 * (z // 2))

    def near(i, c, r, part):
        size, cut = ROWS[i], SPLIT[i]
        start, count = {"all": (0, size), "a": (0, cut), "b": (cut, size - cut)}[part]
        return at_rows(ws[i], c, pl.multiple_of(r * size + start, 16), count)

    def gather_link(way, i, c, r, part, recv, to_row, to_col, when=None):
        ref = near(i, c, r, part)
        go(Link(way, ref, ref, recv, to_row, to_col, when))

    def gather_z(i, j):
        c = order[j]
        if j > 0:
            arrived(near(i, c, row, "all"), az_r.at[i, c], row, z)
        right = z < 3 if j == 0 else (c < z) & (z < 3)
        left = z > 0 if j == 0 else (c > z) & (z > 0)
        gather_link("z", i, c, row, "all", az_r.at[i, c], row, z + 1, right)
        gather_link("z", i, c, row, "all", az_r.at[i, c], row, z - 1, left)

    def gather_xy(i, j):
        c = order[j]
        gather_link("x", i, c, row, "a", ax_r.at[i, c, 0], rx, z)
        gather_link("y", i, c, row, "b", ay_r.at[i, c, 0], ry, z)
        gather_link("x", i, c, row, "b", ax_r.at[i, c, 1], rx, z)
        gather_link("y", i, c, row, "a", ay_r.at[i, c, 1], ry, z)
        gather_link("c", i, c, row, "all", ac_r.at[i, c], rc, z)

    def gather_second_x(i, j):
        c = order[j]
        arrived(near(i, c, rx, "a"), ax_r.at[i, c, 0], rx, z)
        gather_link("y", i, c, rx, "a", ay_r.at[i, c, 1], ry, z)

    def gather_second_y(i, j):
        c = order[j]
        arrived(near(i, c, ry, "b"), ay_r.at[i, c, 0], ry, z)
        gather_link("x", i, c, ry, "b", ax_r.at[i, c, 1], rx, z)

    def first_rows(i, c, count):
        return ws[i].at[c, pl.ds(0, count), :]

    def gather_third(i, j):
        c = order[j]
        arrived(first_rows(i, c, 2 * (ROWS[i] - SPLIT[i])), ax_r.at[i, c, 1], rx, z)
        arrived(first_rows(i, c, 2 * SPLIT[i]), ay_r.at[i, c, 1], ry, z)
        for r in (rx, ry, rxy):
            gather_link("c", i, c, r, "all", ac_r.at[i, c], rc, z)

    def gather_done(i, j):
        c = order[j]
        arrived(first_rows(i, c, 4 * ROWS[i]), ac_r.at[i, c], rc, z)

    def pack_own():
        r96 = pl.ds(pl.multiple_of(row * 96, 16), 96)
        r144 = pl.ds(pl.multiple_of(row * 144, 16), 144)
        q, k, v = qkv_in[0], qkv_in[1], qkv_in[2]
        gate, other = in_in[:, 0, :], in_in[:, 1, :]
        w1[z, r96, :] = jnp.concatenate(
            [q[:, :128], k[:, :128], v[:, :128], q[:, 128:], k[:, 128:], v[:, 128:],
             out_in[...]], axis=1)
        w2[z, r96, :] = jnp.concatenate([gate[:, :256], other[:, :256]], axis=1)
        tail = jnp.concatenate([gate[:, 256:], other[:, 256:]], axis=1)
        tail = jnp.concatenate([tail, jnp.zeros((48, 64), BF)], axis=0)
        w3[z, r144, :] = jnp.concatenate([down_in[...], tail], axis=1)
        gains_in[...] = jnp.zeros((8, 256), F32)
        gains_in[0:1, 0:192] = gain_one_in[...].reshape(1, 192)
        gains_in[1:2, 0:192] = gain_two_in[...].reshape(1, 192)

    def own_tokens(step):
        for c in range(4):
            low, size, to = window(c)

            @pl.when(z == c)
            def _():
                step(pltpu.make_async_copy(
                    tok_in.at[pl.ds(low, size), :], got_x.at[c, pl.ds(to, size), :], io.at[0]))

        step(pltpu.make_async_copy(lines(cot_in, z), got_g.at[z], io.at[1]))

    def take_tokens():
        own_tokens(lambda copy: copy.wait())
        for c in range(4):
            low, size, to = window(c)

            @pl.when(z == c)
            def _():
                arrived(got_x.at[pl.ds(0, 3), pl.ds(to, size), :], tok_r.at[0], row, c)

        @pl.when(low_end)
        def _():
            arrived(got_x.at[:, pl.ds(0, 32), :], tok_rl.at[0], row - 1, 0)

        @pl.when(high_end)
        def _():
            arrived(got_x.at[:, pl.ds(160, 32), :], tok_rr.at[0], row + 1, 0)

        @pl.when((z == 0) & (row == 0))
        def _():
            got_x[:, 0:32, :] = jnp.zeros((4, 32, 384), BF)

        @pl.when((z == 3) & (row == 7))
        def _():
            got_x[:, 160:192, :] = jnp.zeros((4, 32, 384), BF)

        got_gain[pl.ds(z, 1)] = gains_in[...][None]
        arrived(got_gain.at[pl.ds(0, 3)], gn_r.at[0], row, z)
        at = 0
        for low, high, lane in ((32, 160, 0), (32, 160, 192), (0, 32, 0), (0, 32, 192),
                                (160, 192, 0), (160, 192, 192)):
            x_all[at : at + high - low, :] = jnp.concatenate(
                [got_x[c, low:high, lane : lane + 192].astype(F32) for c in range(4)], axis=1)
            at += high - low

    def gain_row(which):
        return jnp.concatenate([got_gain[c, which : which + 1, 0:192] for c in range(4)], axis=1)

    def window_ids(first, length):
        last = ids_in.shape[0] - 1
        spot = first // 128
        near_rows = [ids_in[pl.ds(jnp.clip(spot + n, 0, last), 1), :] for n in range(-1, 3)]
        base = near_rows[1][0:1, 0:1]
        rel = jnp.concatenate(near_rows, axis=0) - base
        rel = jnp.clip(rel, -200, 200).astype(BF)
        source = lax.broadcasted_iota(jnp.int32, (128, 128), 0)
        target = lane_iota((128, 128))
        pick = (source == jnp.where(target < 64, 2 * target, 2 * target - 127)).astype(BF)
        rel = jnp.concatenate([rel, jnp.zeros((4, 128), BF)], axis=0)
        rel = dot(rel, pick)
        keys = jnp.concatenate(
            [rel[1:2, :64], rel[2:3, :64], rel[1:2, 64:], rel[2:3, 64:], rel[0:1, 32:64],
             rel[0:1, 96:], rel[3:4, :32], rel[3:4, 64:96]], axis=1)
        lane = lane_iota((1, EXT))
        lost = (lane >= 256) & (lane < 320) & (first % length == 0)
        lost |= (lane >= 320) & ((first + OWN) % length == 0)
        keys = jnp.where(lost, 1000.0, keys)
        own_ids[...] = jnp.broadcast_to(keys[:, :OWN], (8, OWN))
        return keys, own_ids[...].T[:, 0:1]

    def tables():
        spot = lax.broadcasted_iota(jnp.int32, (EXT, 128), 0)
        halo = spot - 256
        place = jnp.where(
            spot < 128, 2 * spot, jnp.where(
                spot < 256, 2 * spot - 255, jnp.where(
                    halo < 32, 2 * halo - 64, jnp.where(
                        halo < 64, 2 * halo - 127, jnp.where(
                            halo < 96, 2 * halo + 128, 2 * halo + 65)))))
        first, length = start_of(row, z)
        place = (place + first + length) % length
        angle = place.astype(F32) * freq_in[0:1, :]
        cos_t[...] = jnp.cos(angle)
        turn = jnp.where((lane_iota((EXT, 128)) % 64) < 32, -1.0, 1.0)
        sin_t[...] = jnp.sin(angle) * turn
        key_ids, query_ids = window_ids(first, length)
        qrow = lax.broadcasted_iota(jnp.int32, (OWN, EXT), 0)
        qplace = jnp.where(qrow < 128, 2 * qrow, 2 * qrow - 255)
        kcol = lane_iota((OWN, EXT))
        khalo = kcol - 256
        kplace = jnp.where(
            kcol < 128, 2 * kcol, jnp.where(
                kcol < 256, 2 * kcol - 255, jnp.where(
                    khalo < 32, 2 * khalo - 64, jnp.where(
                        khalo < 64, 2 * khalo - 127, jnp.where(
                            khalo < 96, 2 * khalo + 128, 2 * khalo + 65)))))
        allowed = (jnp.abs(qplace - kplace) <= HALF) & (query_ids == key_ids)
        bias[...] = jnp.where(allowed, 0.0, -1e30)

    def statistics(v):
        mu = jnp.mean(v, axis=1, keepdims=True)
        inv = lax.rsqrt(jnp.mean(v * v, axis=1, keepdims=True) - mu * mu + EPSILON)
        return (v - mu) * inv, inv

    def norm_one():
        hat, inv = statistics(x_all[0:OWN, :])
        hat1[...] = hat
        stat[0] = jnp.broadcast_to(inv, (OWN, 128))
        gain = gain_row(0)
        n1[0:OWN, :] = (hat * gain).astype(BF)
        hat, _ = statistics(x_all[OWN:EXT, :])
        n1[OWN:EXT, :] = (hat * gain).astype(BF)

    def take_cotangent():
        arrived(got_g.at[pl.ds(0, 3)], cot_r.at[0], row, z)
        pad = jnp.zeros((128, 64), BF)
        for c in range(4):
            for odd in range(2):
                cot_pad[128 * odd : 128 * odd + 128, 256 * c : 256 * c + 256] = jnp.concatenate(
                    [got_g[c, :, 192 * odd : 192 * odd + 192], pad], axis=1)

    low_lanes = lambda shape: lane_iota(shape) < 64

    def forward_heads(j):
        c = order[j]
        proj = dot(n1[...], w1[c, :, 0:640])
        cos, sin = cos_t[...], sin_t[...]
        rot = lambda tile, n: tile * cos[0:n] + swap_halves(tile) * sin[0:n]
        qs[c, 0] = (rot(proj[0:OWN, 0:128], OWN) * 0.125).astype(BF)
        ks[c, 0] = rot(proj[:, 128:256], EXT).astype(BF)
        vs[c, 0] = proj[:, 256:384].astype(BF)
        third = rot(proj[:, 384:512], EXT)
        low = low_lanes((EXT, 128))
        qs[c, 1] = jnp.where(low[0:OWN], third[0:OWN] * 0.125, 0.0).astype(BF)
        ks[c, 1] = jnp.where(low, pltpu.roll(third, 64, 1), 0.0).astype(BF)
        vs[c, 1] = jnp.where(low, proj[:, 512:640], 0.0).astype(BF)

        def head(h, q, k):
            scores = dot_nt(q, k) + bias[...]
            weight = jnp.exp(scores - jnp.max(scores, axis=1, keepdims=True))
            weight = weight * (1.0 / jnp.sum(weight, axis=1, keepdims=True))
            probs[3 * c + h] = weight
            return weight.astype(BF)

        zero = jnp.zeros((), BF)
        lowq, lowk = low_lanes((OWN, 128)), low
        q, k, v = qs[c, 0], ks[c, 0], vs[c, 0]
        both = dot(head(0, jnp.where(lowq, q, zero), k), jnp.where(lowk, v, zero))
        both += dot(head(1, jnp.where(lowq, zero, q), k), jnp.where(lowk, zero, v))
        att_c[c, :, 0:128] = both.astype(BF)
        att_c[c, :, 128:256] = dot(head(2, qs[c, 1], ks[c, 1]), vs[c, 1]).astype(BF)

    def forward_middle():
        for c in range(4):
            att[:, 192 * c : 192 * c + 192] = att_c[c, :, 0:192]
        for c in range(4):
            out = dot(att[...], w1[c, :, 512:768])
            mid[:, 192 * c : 192 * c + 192] = (
                x_all[0:OWN, 192 * c : 192 * c + 192] + out[:, 64:256])
        hat, inv = statistics(mid[...])
        hat2[...] = hat
        stat[1] = jnp.broadcast_to(inv, (OWN, 128))
        n2[...] = (hat * gain_row(1)).astype(BF)

    def gelu_parts(g):
        phi = 0.5 * (1.0 + lax.erf(g * 0.7071067811865476))
        return g * phi, phi + g * (jnp.exp(g * g * -0.5) * 0.3989422804014327)

    def forward_hidden(j):
        c = order[j]
        both = dot(n2[...], w2[c])
        value, slope = gelu_parts(both[:, 0:256])
        other = both[:, 256:512]
        gel[c] = value
        gel_up[c] = other * slope
        hid[c] = (value * other).astype(BF)

    def forward_tail():
        for c in range(4):
            for r in range(8):
                tail_in[96 * r : 96 * r + 96, 128 * c : 128 * c + 128] = (
                    w3[c, 144 * r : 144 * r + 96, 128:256])
                if r < 4:
                    tail_down[c, 32 * r : 32 * r + 32, :] = (
                        w3[c, 288 * r + 256 : 288 * r + 288, :])
        tails = dot(n2[...], tail_in[...])
        lanes = lane_iota((OWN, 128)) // 32
        packed = jnp.zeros((OWN, 128), F32)
        for c in range(4):
            tile = tails[:, 128 * c : 128 * c + 128]
            value, slope = gelu_parts(tile)
            other = pltpu.roll(tile, 96, 1)
            gel_t[c] = value
            gel_up_t[c] = other * slope
            moved = pltpu.roll(value * other, (32 * c + 64) % 128, 1)
            packed = jnp.where(lanes == c, moved, packed)
        hid_tail[...] = packed.astype(BF)

    def forward_mixed():
        for k in range(4):
            total = dot(hid_tail[...], tail_down[k])
            for c in range(4):
                total += dot(hid[c], w3[k, 288 * c : 288 * c + 256, :])
            out = (mid[:, 192 * k : 192 * k + 192] + total[:, 0:192]).astype(BF)
            mixed_send[k] = jnp.concatenate([out[0:128], out[128:256]], axis=1)

    def backward_hidden(c):
        grad = dot_nt(cot_pad[:, 0:256], w3[0, 288 * c : 288 * c + 256, :])
        for k in range(1, 4):
            grad += dot_nt(cot_pad[:, 256 * k : 256 * k + 256], w3[k, 288 * c : 288 * c + 256, :])
        d_gate[c] = jnp.concatenate([grad * gel_up[c], grad * gel[c]], axis=1).astype(BF)

    def backward_tail():
        grad = dot_nt(cot_pad[:, 0:256], tail_down[0])
        for k in range(1, 4):
            grad += dot_nt(cot_pad[:, 256 * k : 256 * k + 256], tail_down[k])
        lanes = lane_iota((OWN, 128))
        for c in range(4):
            gate = pltpu.roll(grad, (64 - 32 * c) % 128, 1) * gel_up_t[c]
            other = pltpu.roll(grad, (96 - 32 * c) % 128, 1) * pltpu.roll(gel_t[c], 32, 1)
            d_tail[:, 128 * c : 128 * c + 128] = jnp.where(
                lanes >= 96, other, jnp.where(lanes >= 64, gate, 0.0)).astype(BF)

    def grad_down():
        for c in range(4):
            part = dot_tn(hid[c], cot_pad[...]).astype(BF)
            for k in range(4):
                d3[k, 288 * c : 288 * c + 256, :] = part[:, 256 * k : 256 * k + 256]
        part = dot_tn(hid_tail[...], cot_pad[...]).astype(BF)
        for c in range(4):
            for k in range(4):
                d3[k, 288 * c + 256 : 288 * c + 288, :] = (
                    part[32 * c : 32 * c + 32, 256 * k : 256 * k + 256])

    def grad_tail():
        part = dot_tn(n2[...], d_tail[...]).astype(BF)
        for c in range(4):
            for r in range(8):
                d3[c, 144 * r : 144 * r + 96, 128:256] = (
                    d3[c, 144 * r : 144 * r + 96, 128:256]
                    + part[96 * r : 96 * r + 96, 128 * c : 128 * c + 128])

    def grad_in(j):
        c = order[3 - j]
        d2[c] = dot_tn(n2[...], d_gate[c]).astype(BF)

    def norm_back(grad, hat, inv, gain):
        e = grad * gain
        return inv * (e - jnp.mean(e, axis=1, keepdims=True)
                      - hat * jnp.mean(e * hat, axis=1, keepdims=True))

    def backward_middle():
        grad = dot_nt(d_tail[...], tail_in[...])
        for c in range(4):
            grad += dot_nt(d_gate[c], w2[c])
        hat = hat2[...]
        gain_part[1:2, :] = jnp.sum(grad * hat, axis=0, keepdims=True)
        back = norm_back(grad, hat, stat[1][:, 0:1], gain_row(1))
        pad = jnp.zeros((OWN, 64), BF)
        total = jnp.concatenate(
            [cot_pad[:, 256 * c : 256 * c + 192].astype(F32) for c in range(4)], axis=1) + back
        mid_grad[...] = total
        branch = total.astype(BF)
        for c in range(4):
            branch_pad[:, 256 * c : 256 * c + 256] = jnp.concatenate(
                [pad, branch[:, 192 * c : 192 * c + 192]], axis=1)
        grad = dot_nt(branch_pad[:, 0:256], w1[0, :, 512:768])
        for c in range(1, 4):
            grad += dot_nt(branch_pad[:, 256 * c : 256 * c + 256], w1[c, :, 512:768])
        grad = grad.astype(BF)
        for c in range(4):
            att_grad[c] = jnp.concatenate([grad[:, 192 * c : 192 * c + 192], pad], axis=1)

    def grad_out():
        part = dot_tn(att[...], branch_pad[...]).astype(BF)
        for c in range(4):
            d1[c, :, 512:768] = part[:, 256 * c : 256 * c + 256]

    def backward_heads(j):
        c = order[3 - j]
        zero = jnp.zeros((), BF)
        lowq, lowk = low_lanes((OWN, 128)), low_lanes((EXT, 128))

        def head(h, g, v):
            weight = probs[3 * c + h]
            prob_grad = dot_nt(g, v)
            inner = jnp.sum(weight * prob_grad, axis=1, keepdims=True)
            return (weight * (prob_grad - inner)).astype(BF), weight.astype(BF)

        q, k, v = qs[c, 0], ks[c, 0], vs[c, 0]
        g = att_grad[c, :, 0:128]
        g0, g1 = jnp.where(lowq, g, zero), jnp.where(lowq, zero, g)
        s0, p0 = head(0, g0, v)
        s1, p1 = head(1, g1, v)
        dq = dot(s0, jnp.where(lowk, k, zero)) + dot(s1, jnp.where(lowk, zero, k))
        dk = dot_tn(s0, jnp.where(lowq, q, zero)) + dot_tn(s1, jnp.where(lowq, zero, q))
        dv = dot_tn(p0, g0) + dot_tn(p1, g1)
        g2 = att_grad[c, :, 128:256]
        s2, p2 = head(2, g2, vs[c, 1])
        dq2 = dot(s2, ks[c, 1]) * 0.125
        dk2 = pltpu.roll(dot_tn(s2, qs[c, 1]), 64, 1)
        dv2 = dot_tn(p2, g2)
        cos, sin = cos_t[...], sin_t[...]
        back = lambda tile: tile * cos - swap_halves(tile) * sin
        none = jnp.zeros((EXT - OWN, 128), F32)
        dq = jnp.concatenate([dq * 0.125, none], axis=0)
        d_proj[c, :, 0:128] = back(dq).astype(BF)
        d_proj[c, :, 128:256] = back(dk).astype(BF)
        d_proj[c, :, 256:384] = dv.astype(BF)
        d_proj[c, :, 384:512] = back(jnp.concatenate([dq2, none], axis=0) + dk2).astype(BF)
        d_proj[c, :, 512:640] = dv2.astype(BF)

    def grad_qkv(j):
        c = order[3 - j]
        part = dot_tn(n1[...], d_proj[c]).astype(BF)
        d1[c, :, 0:512] = part[:, 0:512]
        d1[c, :, 512:640] = d1[c, :, 512:640] + part[:, 512:640]

    def backward_first():
        grad = dot_nt(d_proj[0], w1[0, :, 0:640])
        for c in range(1, 4):
            grad += dot_nt(d_proj[c], w1[c, :, 0:640])
        n1_grad[...] = grad[0:OWN]
        halo_out[...] = grad[OWN:EXT].astype(BF)

    edge_low, edge_high = (z == 0) & (row == 0), (z == 3) & (row == 7)
    left_row = jnp.where(z == 0, row - 1, row)
    right_row = jnp.where(z == 3, row + 1, row)
    left_col, right_col = (z + 3) % 4, (z + 1) % 4

    def halo_send():
        go(Link("z", halo_out.at[pl.ds(0, 64), :], halo_right, ha_r.at[1], left_row, left_col, jnp.logical_not(edge_low)))
        go(Link("z", halo_out.at[pl.ds(64, 64), :], halo_left, ha_r.at[0], right_row, right_col, jnp.logical_not(edge_high)))

    def halo_take():
        @pl.when(jnp.logical_not(edge_low))
        def _():
            arrived(halo_left, ha_r.at[0], left_row, left_col)
            n1_grad[0:32, :] += halo_left[0:32, :].astype(F32)
            n1_grad[128:160, :] += halo_left[32:64, :].astype(F32)

        @pl.when(jnp.logical_not(edge_high))
        def _():
            arrived(halo_right, ha_r.at[1], right_row, right_col)
            n1_grad[96:128, :] += halo_right[0:32, :].astype(F32)
            n1_grad[224:256, :] += halo_right[32:64, :].astype(F32)

    def backward_last():
        grad, hat = n1_grad[...], hat1[...]
        gain_part[0:1, :] = jnp.sum(grad * hat, axis=0, keepdims=True)
        total = mid_grad[...] + norm_back(grad, hat, stat[0][:, 0:1], gain_row(0))
        out = total.astype(BF)
        for k in range(4):
            mine = out[:, 192 * k : 192 * k + 192]
            input_send[k] = jnp.concatenate([mine[0:128], mine[128:256]], axis=1)
        for c in range(4):
            gain_part_c = gain_part[0:2, 192 * c : 192 * c + 192]
            gain_sum[c, 0:2, 0:192] = gain_part_c

    cores = (core1, core2, core3)
    xas, xbs, yas, ybs = (xa1, xa2, xa3), (xb1, xb2, xb3), (ya1, ya2, ya3), (yb1, yb2, yb3)
    zbs = (zb1, zb2, zb3)
    outs = (grad_one, grad_two, grad_three)

    def unpack_outs():
        one, two, three = grad_one[...], grad_two[...], grad_three[...]
        for n in range(3):
            qkv_out[n] = jnp.concatenate(
                [one[:, 128 * n : 128 * n + 128], one[:, 384 + 64 * n : 448 + 64 * n]], axis=1)
        out_out[...] = one[:, 576:768]
        for n in range(2):
            in_out[:, n, :] = jnp.concatenate(
                [two[:, 256 * n : 256 * n + 256], three[0:96, 192 + 32 * n : 224 + 32 * n]],
                axis=1)
        down_out[...] = three[:, 0:192]


    def place(i, c, r, part):
        size, cut = ROWS[i], SPLIT[i]
        start, count = {"all": (0, size), "a": (0, cut), "b": (cut, size - cut)}[part]
        return c, pl.ds(pl.multiple_of(r * size + start, 16), count)

    def piece(i, c, r, part):
        lead, span = place(i, c, r, part)
        return ds_[i].at[lead, span, :]

    def add_into(i, c, r, part, value):
        lead, span = place(i, c, r, part)
        ds_[i][lead, span, :] = ds_[i][lead, span, :] + value

    def sum_first(i, j):
        c = order[3 - j]
        for n in range(4):
            go(Link("c", piece(i, c, 2 * n + 1 - core, "all"), cores[i].at[c, n], rc_r.at[i, c],
                    rc, z))

    def sum_second(i, j):
        c = order[3 - j]
        arrived(cores[i].at[c], rc_r.at[i, c], rc, z)
        for n in range(4):
            add_into(i, c, 2 * n + core, "all", cores[i][c, n])
        for y in range(2):
            go(Link("x", piece(i, c, 4 * y + 2 * (1 - xc) + core, "a"), xas[i].at[c, y],
                    rx_r.at[i, c, 0], rx, z))
        for x in range(2):
            go(Link("y", piece(i, c, 4 * (1 - yc) + 2 * x + core, "b"), ybs[i].at[c, x],
                    ry_r.at[i, c, 0], ry, z))

    def sum_third_x(i, j):
        c = order[3 - j]
        arrived(xas[i].at[c], rx_r.at[i, c, 0], rx, z)
        for y in range(2):
            add_into(i, c, 4 * y + 2 * xc + core, "a", xas[i][c, y])
        go(Link("y", piece(i, c, ry, "a"), yas[i].at[c], ry_r.at[i, c, 1], ry, z))

    def sum_third_y(i, j):
        c = order[3 - j]
        arrived(ybs[i].at[c], ry_r.at[i, c, 0], ry, z)
        for x in range(2):
            add_into(i, c, 4 * yc + 2 * x + core, "b", ybs[i][c, x])
        go(Link("x", piece(i, c, rx, "b"), xbs[i].at[c], rx_r.at[i, c, 1], rx, z))

    def sum_fourth(i, j):
        c = order[3 - j]
        arrived(yas[i].at[c], ry_r.at[i, c, 1], ry, z)
        add_into(i, c, row, "a", yas[i][c])
        arrived(xbs[i].at[c], rx_r.at[i, c, 1], rx, z)
        add_into(i, c, row, "b", xbs[i][c])

        @pl.when(((c > z) & (z > 0)) | ((c < z) & (z < 3)))
        def _():
            arrived(zbs[i].at[c], rz_r.at[i, c], row, z)
            add_into(i, c, row, "all", zbs[i][c])

        go(Link("z", piece(i, c, row, "all"), zbs[i].at[c], rz_r.at[i, c], row, z + 1, c > z))
        slot = c + (4 - c) * (1 - jnp.minimum(jnp.abs(z - 1 - c), 1))
        go(Link("z", piece(i, c, row, "all"), zbs[i].at[slot], rz_r.at[i, slot], row, z - 1, c < z))

    def sum_last(i):
        lead, span = place(i, z, row, "all")
        outs[i][...] = ds_[i][lead, span, :].astype(F32)

        @pl.when(z > 0)
        def _():
            arrived(zbs[i].at[z], rz_r.at[i, z], row, z)
            outs[i][...] = outs[i][...] + zbs[i][z].astype(F32)

        @pl.when(z < 3)
        def _():
            arrived(zbs[i].at[4], rz_r.at[i, 4], row, z)
            outs[i][...] = outs[i][...] + zbs[i][4].astype(F32)

    def gains_first():
        gain_z[pl.ds(z, 1)] = gain_sum[pl.ds(z, 1)]
        arrived(gain_z.at[pl.ds(0, 3)], gz_r.at[0], row, z)
        gain_all[pl.ds(row, 1)] = (gain_z[0] + gain_z[1] + gain_z[2] + gain_z[3])[None]
        for step in range(1, 8):
            go(Link("x", gain_all.at[row], gain_all.at[row], gp_r.at[0], (row + step) % 8, z))

    def gains_last():
        arrived(gain_all.at[pl.ds(0, 7)], gp_r.at[0], row, z)
        total = gain_all[0]
        for r in range(1, 8):
            total = total + gain_all[r]
        gain_one_out[...] = total[0:1, 0:192].reshape(192)
        gain_two_out[...] = total[1:2, 0:192].reshape(192)

    def results(which, step):
        got, out, n = {"mx": (mixed_got, mixed_out, 2), "ig": (input_got, input_out, 3)}[which]
        step(pltpu.make_async_copy(got, out, io.at[n]))

    def finish(which):
        got, send, recv = {
            "mx": (mixed_got, mixed_send, mx_r), "ig": (input_got, input_send, ig_r)}[which]
        lines(got, z)[...] = send[z]
        arrived(got.at[pl.ds(0, 384), :], recv.at[0], row, z)
        results(which, lambda copy: copy.start())

    own_tokens(lambda copy: copy.start())
    pack_own()
    pl.semaphore_wait(barrier, peers)
    gather_z(0, 0)
    gather_xy(0, 0)
    hop_cot(3, 0)
    gather_second_x(0, 0)
    gather_z(2, 0)
    gather_z(1, 0)
    gather_second_y(0, 0)
    gather_xy(1, 0)
    gather_z(0, 1)
    gather_xy(0, 1)
    gather_z(2, 1)
    gather_xy(2, 1)
    hop_tok(3, 0)
    gather_z(0, 2)
    gather_xy(2, 0)
    gather_z(1, 1)
    hop_tok(2, 0)
    gather_xy(0, 2)
    gather_z(1, 2)
    gather_second_x(2, 1)
    gather_second_y(2, 1)
    gather_second_y(0, 1)
    tables()
    gather_second_x(0, 1)
    gather_z(0, 3)
    hop_cot(3, 1)
    gather_second_x(0, 2)
    gather_xy(1, 1)
    gather_z(2, 2)
    gather_second_y(1, 0)
    gather_second_x(2, 0)
    hop_tok(2, 1)
    gather_second_y(0, 2)
    hop_tok(3, 1)
    gather_z(1, 3)
    gather_second_x(1, 1)
    gather_third(0, 0)
    hop_tok(1, 0)
    send_gains_in()
    gather_xy(2, 2)
    hop_cot(2, 0)
    gather_xy(0, 3)
    gather_third(2, 1)
    gather_z(2, 3)
    gather_third(0, 1)
    gather_second_x(2, 2)
    gather_xy(2, 3)
    gather_done(0, 1)
    gather_second_x(1, 0)
    hop_tok(3, 2)
    gather_second_y(2, 0)
    gather_second_x(0, 3)
    gather_second_y(0, 3)
    hop_cot(3, 2)
    gather_third(0, 2)
    gather_done(0, 0)
    take_tokens()
    hop_cot(2, 1)
    norm_one()
    gather_second_y(2, 2)
    gather_second_y(1, 1)
    gather_xy(1, 3)
    hop_cot(1, 0)
    gather_xy(1, 2)
    forward_heads(1)
    gather_done(0, 2)
    gather_second_y(2, 3)
    gather_third(1, 0)
    forward_heads(2)
    gather_done(2, 1)
    gather_third(2, 2)
    gather_third(1, 1)
    gather_third(0, 3)
    gather_second_x(2, 3)
    forward_heads(0)
    gather_done(1, 0)
    take_cotangent()
    gather_third(2, 0)
    gather_done(0, 3)
    gather_second_x(1, 3)
    gather_second_y(1, 3)
    gather_second_x(1, 2)
    gather_second_y(1, 2)
    forward_heads(3)
    gather_third(2, 3)
    forward_middle()
    gather_third(1, 3)
    forward_hidden(0)
    gather_done(2, 2)
    gather_done(2, 3)
    gather_done(1, 1)
    forward_hidden(1)
    gather_done(2, 0)
    gather_third(1, 2)
    forward_tail()
    gather_done(1, 3)
    backward_tail()
    forward_hidden(3)
    gather_done(1, 2)
    forward_hidden(2)
    backward_hidden(0)
    grad_down()
    backward_hidden(2)
    grad_tail()
    sum_first(2, 0)
    backward_hidden(3)
    backward_hidden(1)
    grad_in(0)
    grad_in(1)
    sum_first(1, 0)
    sum_second(2, 0)
    sum_first(1, 1)
    forward_mixed()
    sum_second(1, 0)
    hop_mixed(2, 0)
    hop_mixed(1, 0)
    sum_second(1, 1)
    backward_middle()
    sum_first(2, 1)
    grad_in(2)
    sum_third_y(2, 0)
    grad_out()
    sum_first(1, 2)
    sum_third_y(1, 0)
    sum_second(2, 1)
    hop_mixed(2, 1)
    backward_heads(0)
    grad_qkv(0)
    sum_first(0, 0)
    sum_second(1, 2)
    backward_heads(3)
    sum_third_x(2, 0)
    hop_mixed(3, 0)
    sum_second(0, 0)
    backward_heads(1)
    backward_heads(2)
    backward_first()
    halo_send()
    sum_first(2, 2)
    sum_first(2, 3)
    sum_third_y(2, 1)
    hop_mixed(3, 1)
    sum_third_x(1, 0)
    sum_third_y(1, 1)
    sum_third_x(1, 1)
    sum_second(2, 2)
    sum_third_x(1, 2)
    sum_fourth(2, 0)
    sum_second(2, 3)
    grad_qkv(1)
    sum_third_y(0, 0)
    sum_fourth(1, 0)
    sum_third_x(0, 0)
    sum_first(0, 1)
    hop_mixed(3, 2)
    halo_take()
    sum_third_y(1, 2)
    backward_last()
    hop_input(2, 0)
    sum_third_x(2, 1)
    sum_second(0, 1)
    hop_input(3, 0)
    grad_qkv(2)
    grad_in(3)
    sum_first(0, 2)
    hop_input(1, 0)
    sum_first(1, 3)
    sum_second(0, 2)
    grad_qkv(3)
    sum_second(1, 3)
    hop_input(3, 1)
    hop_input(2, 1)
    sum_fourth(0, 0)
    sum_third_y(0, 1)
    sum_third_x(0, 1)
    sum_fourth(1, 1)
    sum_first(0, 3)
    send_gain()
    sum_fourth(1, 2)
    sum_third_x(0, 2)
    sum_third_x(2, 2)
    sum_third_y(0, 2)
    sum_third_x(2, 3)
    sum_third_y(2, 2)
    sum_second(0, 3)
    sum_fourth(2, 1)
    sum_third_y(2, 3)
    sum_fourth(0, 1)
    finish("mx")
    sum_fourth(2, 2)
    sum_third_y(1, 3)
    gains_first()
    hop_input(3, 2)
    sum_third_x(1, 3)
    sum_fourth(0, 2)
    sum_third_x(0, 3)
    sum_third_y(0, 3)
    sum_fourth(1, 3)
    sum_fourth(2, 3)
    finish("ig")
    sum_last(1)
    gains_last()
    sum_last(2)
    sum_fourth(0, 3)
    sum_last(0)
    unpack_outs()
    results("mx", lambda copy: copy.wait())
    results("ig", lambda copy: copy.wait())
    ways.drain()


def hand_over(*refs):
    for n in range(8):
        refs[8 + n][...] = refs[n][...].astype(refs[8 + n].dtype)


def fast_local(
    tokens, segment_ids, gain_one, qkv_weight, out_weight, gain_two, in_weight, down_weight,
    cotangent,
):
    rows_all = tokens.shape[1] * 2 * lax.axis_size("row")
    length = min(SEQ_MAX, rows_all)

    def start_of(row, z):
        return (row * 4 + z) * OWN, length

    frequency = 10000.0 ** (-(np.arange(HEAD_DIM // 2) * 2.0) / HEAD_DIM)
    frequency = jnp.asarray(np.tile(frequency.astype(np.float32), 4)[None, :].repeat(8, 0))
    vmem, dma = pltpu.VMEM, pltpu.SemaphoreType.DMA
    shapes = [
        vmem((4, 192, 384), BF), vmem((4, 128, 384), BF), vmem((4, 8, 256), F32),
        vmem((4, 768, 768), BF), vmem((4, 768, 512), BF), vmem((4, 1152, 256), BF),
        vmem((4, 768, 768), BF), vmem((4, 768, 512), BF), vmem((4, 1152, 256), BF),
    ]
    shapes += [vmem((4, 4, ROWS[i], COLS[i]), BF) for i in range(3)]
    shapes += [vmem((4, 2, SPLIT[i], COLS[i]), BF) for i in range(3)]
    shapes += [vmem((4, ROWS[i] - SPLIT[i], COLS[i]), BF) for i in range(3)]
    shapes += [vmem((4, SPLIT[i], COLS[i]), BF) for i in range(3)]
    shapes += [vmem((4, 2, ROWS[i] - SPLIT[i], COLS[i]), BF) for i in range(3)]
    shapes += [vmem((5, ROWS[i], COLS[i]), BF) for i in range(3)]
    shapes += [
        vmem((8, 256), F32), vmem((8, OWN), F32),
        vmem((EXT, 768), F32), vmem((EXT, 128), F32), vmem((EXT, 128), F32),
        vmem((OWN, EXT), F32), vmem((EXT, 768), BF), vmem((OWN, 768), F32),
        vmem((2, OWN, 128), F32), vmem((4, 2, OWN, 128), BF), vmem((4, 2, EXT, 128), BF),
        vmem((4, 2, EXT, 128), BF), vmem((12, OWN, EXT), F32),
        vmem((4, OWN, 256), BF), vmem((OWN, 768), BF),
        vmem((OWN, 768), F32), vmem((OWN, 768), F32), vmem((OWN, 768), BF),
        vmem((768, 512), BF), vmem((4, 128, 256), BF), vmem((4, OWN, 256), BF),
        vmem((OWN, 128), BF), vmem((4, OWN, 256), F32), vmem((4, OWN, 256), F32),
        vmem((4, OWN, 128), F32), vmem((4, OWN, 128), F32), vmem((OWN, 1024), BF),
        vmem((4, OWN, 512), BF), vmem((OWN, 512), BF),
        vmem((OWN, 768), F32), vmem((OWN, 1024), BF), vmem((4, OWN, 256), BF),
        vmem((4, EXT, 640), BF), vmem((OWN, 768), F32),
        vmem((128, 768), BF), vmem((64, 768), BF), vmem((64, 768), BF),
        vmem((4, 128, 384), BF), vmem((512, 384), BF),
        vmem((4, 128, 384), BF), vmem((512, 384), BF),
        vmem((2, 3, 192, 384), BF), vmem((2, 3, 128, 384), BF), vmem((2, 3, 128, 384), BF),
        vmem((2, 3, 128, 384), BF),
        vmem((8, 768), F32), vmem((4, 8, 256), F32), vmem((4, 8, 256), F32),
        vmem((8, 8, 256), F32), vmem((96, 768), F32), vmem((96, 512), F32), vmem((144, 256), F32),
        dma((16,)), dma((16,)), dma((24,)), dma((16,)), dma((4,)),
        dma((4, 2, 3)), dma((1,)), dma((1,)), dma((1,)), dma((1,)), dma((1,)),
        dma((3, 4)), dma((3, 4, 2)), dma((3, 4, 2)), dma((3, 4)),
        dma((3, 4)), dma((3, 4, 2)), dma((3, 4, 2)), dma((3, 5)),
        dma((2,)), dma((1,)), dma((1,)), dma((1,)), dma((1,)),
    ]
    whole, held = pl.BlockSpec(memory_space=pltpu.VMEM), pl.BlockSpec(memory_space=pl.ANY)
    results = (
        jax.ShapeDtypeStruct((512, 384), BF), jax.ShapeDtypeStruct((512, 384), F32),
        jax.ShapeDtypeStruct((3, 96, 192), F32), jax.ShapeDtypeStruct((96, 192), F32),
        jax.ShapeDtypeStruct((96, 2, 288), F32), jax.ShapeDtypeStruct((144, 192), F32),
        jax.ShapeDtypeStruct((192,), F32), jax.ShapeDtypeStruct((192,), F32),
    )
    outs = pl.pallas_call(
        functools.partial(layer_kernel, start_of=start_of),
        out_shape=(results[0], jax.ShapeDtypeStruct((512, 384), BF)) + results[2:],
        in_specs=[held] * 2 + [whole] * 8,
        out_specs=(held,) * 2 + (whole,) * 6,
        scratch_shapes=shapes,
        compiler_params=pltpu.CompilerParams(
            collective_id=0, has_side_effects=True, vmem_limit_bytes=62 * 1024 * 1024),
    )(tokens[0], cotangent[0], qkv_weight.transpose(1, 0, 2), out_weight, in_weight, down_weight,
      gain_one, gain_two, segment_ids.reshape(-1, 128), frequency)
    mixed, input_grad, qkv_grad, out_grad, in_grad, down_grad, one_grad, two_grad = pl.pallas_call(
        hand_over,
        out_shape=results,
        in_specs=[whole] * 8,
        out_specs=(whole,) * 8,
    )(*outs)
    return (
        mixed[None], input_grad[None], one_grad, qkv_grad.transpose(1, 0, 2), out_grad,
        two_grad, in_grad, down_grad,
    )


def solution(mesh):
    placed = (
        P("col", "row", None),
        P(),
        P("col"),
        P("row", None, "col"),
        P("row", "col"),
        P("col"),
        P("row", None, "col"),
        P("row", "col"),
        P("col", "row", None),
    )
    part = local
    if mesh.shape["row"] == 8 and mesh.shape["col"] == 4:
        part = fast_local
    return jax.shard_map(
        part,
        mesh=mesh,
        in_specs=placed,
        out_specs=(
            P("col", "row", None),
            P("col", "row", None),
            P("col"),
            P("row", None, "col"),
            P("row", "col"),
            P("col"),
            P("row", None, "col"),
            P("row", "col"),
        ),
        check_vma=False,
    )
```

```python
import functools

import jax
import jax.numpy as jnp
import numpy as np
from jax import lax
from jax.experimental import pallas as pl
from jax.experimental.pallas import tpu as pltpu
from jax.sharding import PartitionSpec as P

HEAD_DIM = 64
WINDOW = 128
SEQ_MAX = 4096


EPSILON = 1e-05


def with_halo(block, sides, width):
    for axis, dim in sides:
        count = lax.axis_size(axis)
        forward = [(i, i + 1) for i in range(count - 1)]
        backward = [(target, source) for source, target in forward]
        low = lax.ppermute(
            lax.slice_in_dim(block, block.shape[dim] - width, None, axis=dim), axis, forward
        )
        high = lax.ppermute(lax.slice_in_dim(block, 0, width, axis=dim), axis, backward)
        block = jnp.concatenate([low, block, high], axis=dim)
    return block


def rotate(values, cosine, sine_table):
    half_dim = values.shape[-1] // 2
    turned = jnp.concatenate([-values[..., half_dim:], values[..., :half_dim]], axis=-1)
    return values * cosine + turned * sine_table


def rotate_back(grad_rows, cosine, sine_table):
    half_dim = grad_rows.shape[-1] // 2
    turned = jnp.concatenate([-grad_rows[..., half_dim:], grad_rows[..., :half_dim]], axis=-1)
    return grad_rows * cosine - turned * sine_table


def spread(values):
    return lax.all_gather(values, "col", axis=1, tiled=True)


def collect(partial_rows):
    return lax.psum_scatter(partial_rows, "col", scatter_dimension=1, tiled=True)


def norm_forward(values, full_width):
    row_sums = lax.psum((jnp.sum(values, axis=1), jnp.sum(values * values, axis=1)), "col")
    mean_value = row_sums[0] / full_width
    variance = row_sums[1] / full_width - mean_value * mean_value
    inverse = lax.rsqrt(variance + EPSILON)
    return ((values - mean_value[:, None]) * inverse[:, None], inverse)


def norm_backward(grad_rows, scaled, inverse, gain_part, full_width):
    weighted = grad_rows * gain_part
    row_sums = lax.psum((jnp.sum(weighted, axis=1), jnp.sum(weighted * scaled, axis=1)), "col")
    input_part = inverse[:, None] * (
        weighted - row_sums[0][:, None] / full_width - scaled * (row_sums[1][:, None] / full_width)
    )
    return (input_part, jnp.sum(grad_rows * scaled, axis=0))


def geglu(gate_up):
    return jax.nn.gelu(gate_up[:, 0], approximate=False) * gate_up[:, 1]


def local(
    tokens,
    segment_ids,
    gain_one,
    qkv_weight,
    out_weight,
    gain_two,
    in_weight,
    down_weight,
    cotangent,
):
    pair_rows = tokens.shape[1]
    rows_here = pair_rows * 2
    tok_width = tokens.shape[2] // 2
    full_width = tok_width * lax.axis_size("col")
    heads_here = qkv_weight.shape[2] // HEAD_DIM
    head_width = heads_here * HEAD_DIM
    half_window = WINDOW // 2
    block_rows = min(512, rows_here)
    block_count = rows_here // block_rows
    key_span = block_rows + 2 * half_window
    score_scale = HEAD_DIM ** (-0.5)
    length = min(SEQ_MAX, rows_here * lax.axis_size("row"))
    first_row = lax.axis_index("row") * rows_here
    grad_rows = cotangent.reshape(rows_here, tok_width)
    qkv_full, out_full, in_full, down_full = (
        lax.all_gather(qkv_weight, "row", axis=0, tiled=True),
        lax.all_gather(out_weight, "row", axis=0, tiled=True),
        lax.all_gather(in_weight, "row", axis=0, tiled=True),
        lax.all_gather(down_weight, "row", axis=0, tiled=True),
    )
    global_rows = first_row + jnp.arange(rows_here, dtype=jnp.int32)
    places = (global_rows % length).astype(jnp.float32)
    frequencies = 10000.0 ** (-(jnp.arange(HEAD_DIM // 2, dtype=jnp.float32) * 2.0) / HEAD_DIM)
    angles = places[:, None] * frequencies[None, :]
    angles = jnp.concatenate([angles, angles], axis=1)[:, None, :]
    cosine = jnp.cos(angles)
    sine_table = jnp.sin(angles)
    query_ids = lax.dynamic_slice_in_dim(segment_ids, first_row, rows_here)
    padded_ids = jnp.pad(segment_ids, half_window, constant_values=-1)
    key_ids = lax.dynamic_slice_in_dim(padded_ids, first_row, rows_here + 2 * half_window)
    query_seqs = global_rows // length
    key_seqs = (
        first_row - half_window + jnp.arange(rows_here + 2 * half_window, dtype=jnp.int32)
    ) // length
    offsets = (
        jnp.arange(key_span, dtype=jnp.int32)[None, :]
        - half_window
        - jnp.arange(block_rows, dtype=jnp.int32)[:, None]
    )
    in_window = jnp.abs(offsets) <= half_window

    def block_scores(block_start, block_queries, block_keys):
        same_doc = (
            query_ids[block_start : block_start + block_rows, None]
            == key_ids[None, block_start : block_start + key_span]
        )
        same_seq = (
            query_seqs[block_start : block_start + block_rows, None]
            == key_seqs[None, block_start : block_start + key_span]
        )
        allowed = in_window & same_doc & same_seq
        scores = (
            jnp.einsum(
                "qhd,khd->hqk", block_queries, block_keys, preferred_element_type=jnp.float32
            )
            * score_scale
        )
        return jnp.where(allowed[None], scores, -1e30)

    token_values = tokens.reshape(rows_here, tok_width).astype(jnp.float32)
    scaled_one, inverse_one = norm_forward(token_values, full_width)
    normed_one_full = spread((scaled_one * gain_one).astype(jnp.bfloat16))
    projected = jnp.einsum(
        "td,dsf->tsf", normed_one_full, qkv_full, preferred_element_type=jnp.float32
    )
    projected = projected.reshape(rows_here, 3, heads_here, HEAD_DIM)
    queries = rotate(projected[:, 0], cosine, sine_table).astype(jnp.bfloat16)
    key_rows = rotate(projected[:, 1], cosine, sine_table).astype(jnp.bfloat16)
    value_rows = projected[:, 2].astype(jnp.bfloat16)
    key_value = jnp.concatenate(
        [key_rows.reshape(rows_here, head_width), value_rows.reshape(rows_here, head_width)], axis=1
    )
    padded_pair = with_halo(key_value, (("row", 0),), half_window)
    padded_keys = padded_pair[:, :head_width].reshape(
        rows_here + 2 * half_window, heads_here, HEAD_DIM
    )
    padded_values = padded_pair[:, head_width:].reshape(
        rows_here + 2 * half_window, heads_here, HEAD_DIM
    )
    output_blocks = []
    total_blocks = []
    for block_number in range(block_count):
        block_start = block_number * block_rows
        masked = block_scores(
            block_start,
            queries[block_start : block_start + block_rows],
            padded_keys[block_start : block_start + key_span],
        )
        largest = jnp.max(masked, axis=-1, keepdims=True)
        log_total = largest + jnp.log(jnp.sum(jnp.exp(masked - largest), axis=-1, keepdims=True))
        weights = jnp.exp(masked - log_total).astype(jnp.bfloat16)
        output_blocks.append(
            jnp.einsum(
                "hqk,khd->qhd",
                weights,
                padded_values[block_start : block_start + key_span],
                preferred_element_type=jnp.float32,
            )
        )
        total_blocks.append(log_total)
    attended = (
        jnp.concatenate(output_blocks, axis=0).reshape(rows_here, head_width).astype(jnp.bfloat16)
    )
    attended_full = spread(attended)
    middle = token_values + jnp.dot(attended_full, out_full, preferred_element_type=jnp.float32)
    scaled_two, inverse_two = norm_forward(middle, full_width)
    normed_two_full = spread((scaled_two * gain_two).astype(jnp.bfloat16))
    gate_up = jnp.einsum(
        "td,dsf->tsf", normed_two_full, in_full, preferred_element_type=jnp.float32
    )
    hidden_value, geglu_pull = jax.vjp(geglu, gate_up)
    hidden_full = spread(hidden_value.astype(jnp.bfloat16))
    mixed = (middle + jnp.dot(hidden_full, down_full, preferred_element_type=jnp.float32)).astype(
        jnp.bfloat16
    )
    qkv_back, out_back, in_back, down_back = (
        lax.all_gather(qkv_weight, "row", axis=0, tiled=True),
        lax.all_gather(out_weight, "row", axis=0, tiled=True),
        lax.all_gather(in_weight, "row", axis=0, tiled=True),
        lax.all_gather(down_weight, "row", axis=0, tiled=True),
    )
    down_part = jnp.einsum("tf,td->fd", hidden_full, grad_rows, preferred_element_type=jnp.float32)
    hidden_grad = collect(
        jnp.einsum("td,fd->tf", grad_rows, down_back, preferred_element_type=jnp.float32)
    )
    gate_up_grad = geglu_pull(hidden_grad)[0].astype(jnp.bfloat16)
    in_part = jnp.einsum(
        "td,tsf->dsf", normed_two_full, gate_up_grad, preferred_element_type=jnp.float32
    )
    normed_two_grad = collect(
        jnp.einsum("tsf,dsf->td", gate_up_grad, in_back, preferred_element_type=jnp.float32)
    )
    middle_norm_grad, gain_two_part = norm_backward(
        normed_two_grad, scaled_two, inverse_two, gain_two, full_width
    )
    middle_grad = grad_rows.astype(jnp.float32) + middle_norm_grad
    branch_grad = middle_grad.astype(jnp.bfloat16)
    out_part = jnp.einsum(
        "td,tf->df", attended_full, branch_grad, preferred_element_type=jnp.float32
    )
    attended_grad = collect(
        jnp.einsum("tf,df->td", branch_grad, out_back, preferred_element_type=jnp.float32)
    ).astype(jnp.bfloat16)
    attended_heads = attended_grad.reshape(rows_here, heads_here, HEAD_DIM)
    query_blocks = []
    key_grad_ext = jnp.zeros((rows_here + 2 * half_window, heads_here, HEAD_DIM), jnp.float32)
    value_grad_ext = jnp.zeros((rows_here + 2 * half_window, heads_here, HEAD_DIM), jnp.float32)
    for block_number in range(block_count):
        block_start = block_number * block_rows
        block_queries = queries[block_start : block_start + block_rows]
        block_keys = padded_keys[block_start : block_start + key_span]
        block_values = padded_values[block_start : block_start + key_span]
        block_grads = attended_heads[block_start : block_start + block_rows]
        masked = block_scores(block_start, block_queries, block_keys)
        probs = jnp.exp(masked - total_blocks[block_number])
        prob_grad = jnp.einsum(
            "qhd,khd->hqk", block_grads, block_values, preferred_element_type=jnp.float32
        )
        inner = jnp.sum(probs * prob_grad, axis=-1, keepdims=True)
        score_grad = (probs * (prob_grad - inner)).astype(jnp.bfloat16)
        query_blocks.append(
            jnp.einsum("hqk,khd->qhd", score_grad, block_keys, preferred_element_type=jnp.float32)
            * score_scale
        )
        key_grad_ext = key_grad_ext.at[block_start : block_start + key_span].add(
            jnp.einsum(
                "hqk,qhd->khd", score_grad, block_queries, preferred_element_type=jnp.float32
            )
            * score_scale
        )
        value_grad_ext = value_grad_ext.at[block_start : block_start + key_span].add(
            jnp.einsum(
                "hqk,qhd->khd",
                probs.astype(jnp.bfloat16),
                block_grads,
                preferred_element_type=jnp.float32,
            )
        )
    grad_pair = jnp.concatenate(
        [key_grad_ext.reshape(-1, head_width), value_grad_ext.reshape(-1, head_width)], axis=1
    )
    rim_rows = jnp.concatenate(
        [grad_pair[:half_window], grad_pair[rows_here + half_window :]], axis=0
    )
    beside_all = with_halo(rim_rows.astype(jnp.bfloat16), (("row", 0),), half_window).astype(
        rim_rows.dtype
    )
    own_grad = grad_pair[half_window : half_window + rows_here]
    own_grad = own_grad.at[:half_window].add(beside_all[:half_window])
    own_grad = own_grad.at[rows_here - half_window :].add(beside_all[3 * half_window :])
    key_grad = own_grad[:, :head_width].reshape(rows_here, heads_here, HEAD_DIM)
    value_grad = own_grad[:, head_width:].reshape(rows_here, heads_here, HEAD_DIM)
    query_grad = jnp.concatenate(query_blocks, axis=0)
    projected_grad = jnp.stack(
        [
            rotate_back(query_grad, cosine, sine_table),
            rotate_back(key_grad, cosine, sine_table),
            value_grad,
        ],
        axis=1,
    )
    projected_grad = projected_grad.reshape(rows_here, 3, head_width).astype(jnp.bfloat16)
    qkv_part = jnp.einsum(
        "td,tsf->dsf", normed_one_full, projected_grad, preferred_element_type=jnp.float32
    )
    normed_one_grad = collect(
        jnp.einsum("tsf,dsf->td", projected_grad, qkv_back, preferred_element_type=jnp.float32)
    )
    token_norm_grad, gain_one_part = norm_backward(
        normed_one_grad, scaled_one, inverse_one, gain_one, full_width
    )
    input_grad = middle_grad + token_norm_grad
    weight_grads = (
        lax.psum_scatter(qkv_part, "row", scatter_dimension=0, tiled=True),
        lax.psum_scatter(out_part, "row", scatter_dimension=0, tiled=True),
        lax.psum_scatter(in_part, "row", scatter_dimension=0, tiled=True),
        lax.psum_scatter(down_part, "row", scatter_dimension=0, tiled=True),
    )
    gain_grads = lax.psum((gain_one_part, gain_two_part), "row")
    mixed_out = mixed.reshape(1, pair_rows, 2 * tok_width)
    input_out = input_grad.reshape(1, pair_rows, 2 * tok_width)
    return (
        mixed_out,
        input_out,
        gain_grads[0],
        weight_grads[0],
        weight_grads[1],
        gain_grads[1],
        weight_grads[2],
        weight_grads[3],
    )


F32 = jnp.float32
BF = jnp.bfloat16
MESH = pl.DeviceIdType.MESH
ROWS = (96, 96, 144)
COLS = (768, 512, 256)
SPLIT = (48, 48, 64)
OWN = 256
EXT = 384
HALF = 64


def dot(a, b):
    return lax.dot_general(a, b, (((1,), (0,)), ((), ())), preferred_element_type=F32)


def dot_nt(a, b):
    return lax.dot_general(a, b, (((1,), (1,)), ((), ())), preferred_element_type=F32)


def dot_tn(a, b):
    return lax.dot_general(a, b, (((0,), (0,)), ((), ())), preferred_element_type=F32)


class Link:
    def __init__(self, way, src, dst, recv, row, col, when=None):
        self.way, self.src, self.dst, self.recv = way, src, dst, recv
        self.device = {"row": row, "col": col}
        self.when = when
        self.send = None

    def run(self, step):
        def body():
            copy = pltpu.make_async_remote_copy(
                src_ref=self.src,
                dst_ref=self.dst,
                send_sem=self.send,
                recv_sem=self.recv,
                device_id=self.device,
                device_id_type=MESH,
            )
            step(copy)

        if self.when is None:
            body()
        else:
            pl.when(self.when)(body)


class Ways:
    def __init__(self, **rings):
        self.rings = rings
        self.used = {way: [] for way in rings}

    def go(self, link):
        used, ring = self.used[link.way], self.rings[link.way]
        slot = len(used) % ring.shape[0]
        if len(used) >= ring.shape[0]:
            used[-ring.shape[0]].run(lambda copy: copy.wait_send())
        link.send = ring.at[slot]
        used.append(link)
        link.run(lambda copy: copy.start())

    def drain(self):
        for way, ring in self.rings.items():
            for link in self.used[way][-ring.shape[0] :]:
                link.run(lambda copy: copy.wait_send())


def arrived(ref, recv, row, col):
    pltpu.make_async_remote_copy(
        src_ref=ref,
        dst_ref=ref,
        send_sem=recv,
        recv_sem=recv,
        device_id={"row": row, "col": col},
        device_id_type=MESH,
    ).wait_recv()


def at_rows(ref, lead, start, size):
    return ref.at[lead, pl.ds(start, size), :]


def lane_iota(shape):
    return lax.broadcasted_iota(jnp.int32, shape, 1)


def swap_halves(tile):
    first = (lane_iota(tile.shape) % 64) < 32
    return jnp.where(first, pltpu.roll(tile, 96, 1), pltpu.roll(tile, 32, 1))


def layer_kernel(
    tok_in, cot_in, qkv_in, out_in, in_in, down_in, gain_one_in, gain_two_in, ids_in, freq_in,
    mixed_out, input_out, qkv_out, out_out, in_out, down_out, gain_one_out, gain_two_out,
    tok_ext, got_x, got_g, got_gain, w1, w2, w3, d1, d2, d3,
    core1, core2, core3, xa1, xa2, xa3, xb1, xb2, xb3, ya1, ya2, ya3, yb1, yb2, yb3,
    zb1, zb2, zb3,
    gains_in, own_ids, x_all, cos_t, sin_t, bias, n1, hat1, stat, qs, ks, vs, probs, att_c, att, mid, hat2, n2,
    tail_in, tail_down, hid, hid_tail, gel, gel_up, gel_t, gel_up_t, cot_pad, d_gate, d_tail,
    branch_pad, att_grad, d_proj,
    halo_out, halo_left, halo_right, mixed_send, mixed_got, input_send, input_got,
    relay_tok, relay_cot, relay_mixed, relay_input, gain_part, gain_z, gain_sum, gain_all, grad_one, grad_two, grad_three,
    way_x, way_y, way_z, way_c, io,
    hop_r, tok_r, tok_rl, tok_rr, cot_r, gn_r, az_r, ax_r, ay_r, al_r, ac_r,
    rc_r, rx_r, ry_r, rl_r, rz_r, ha_r, mx_r, ig_r, gz_r, gp_r,
    *, start_of,
):
    row = lax.axis_index("row")
    z = lax.axis_index("col")
    core = row % 2
    xc = (row // 2) % 2
    yc = row // 4
    rx = row + 2 - 4 * xc
    ry = row + 4 - 8 * yc
    rxy = ry + 2 - 4 * xc
    rc = row + 1 - 2 * core
    ws = (w1, w2, w3)
    ds_ = (d1, d2, d3)
    n1_grad, mid_grad = x_all.at[pl.ds(0, OWN), :], hat2
    ways = Ways(x=way_x, y=way_y, z=way_z, c=way_c)
    go = ways.go

    barrier = pltpu.get_barrier_semaphore()

    def greet(r, c):
        pl.semaphore_signal(barrier, inc=1, device_id={"row": r, "col": c}, device_id_type=MESH)

    for step in range(1, 8):
        greet((row + step) % 8, z)
    for step in range(1, 4):
        greet(row, (z + step) % 4)
    up, down = row < 7, row > 0
    low_end, high_end = (z == 0) & down, (z == 3) & up
    pl.when(low_end)(lambda: greet(row - 1, 3))
    pl.when(high_end)(lambda: greet(row + 1, 0))
    peers = 10 + jnp.maximum(1 - z, 0) * jnp.minimum(row, 1)
    peers += jnp.maximum(z - 2, 0) * jnp.minimum(7 - row, 1)

    def own_tokens(step):
        step(pltpu.make_async_copy(tok_in, tok_ext.at[pl.ds(32, 512), :], io.at[0]))
        step(pltpu.make_async_copy(lines(cot_in, z), got_g.at[z], io.at[1]))

    def send_edges():
        go(Link("x", tok_in.at[pl.ds(0, 32), :], tok_ext.at[pl.ds(544, 32), :], tok_rr.at[0],
                row - 1, z, down))
        go(Link("y", tok_in.at[pl.ds(480, 32), :], tok_ext.at[pl.ds(0, 32), :], tok_rl.at[0],
                row + 1, z, up))
        for step in range(1, 4):
            go(Link("z", gains_in, got_gain.at[z], gn_r.at[0], row, (z + step) % 4))

    def take_edges():
        own_tokens(lambda copy: copy.wait())

        @pl.when(down)
        def _():
            arrived(tok_ext.at[pl.ds(0, 32), :], tok_rl.at[0], row - 1, z)

        @pl.when(up)
        def _():
            arrived(tok_ext.at[pl.ds(544, 32), :], tok_rr.at[0], row + 1, z)

        @pl.when(row == 0)
        def _():
            tok_ext[0:32, :] = jnp.zeros((32, 384), BF)

        @pl.when(row == 7)
        def _():
            tok_ext[544:576, :] = jnp.zeros((32, 384), BF)

    def window(c):
        return tok_ext.at[pl.ds(pl.multiple_of(c * 128, 128), 192), :]

    slots = {(2, 1): 0, (3, 1): 1, (3, 2): 2}

    def hop(kind, relay, first, last, recv_last, d, k):
        for way, sign in enumerate((1, -1)):
            s, c = z - sign * k, z - sign * k + sign * d
            sends = (s >= 0) & (c <= 3) if sign == 1 else (s <= 3) & (c >= 0)
            src = first(jnp.clip(c, 0, 3))
            if k > 0:
                slot = slots[d, k]
                src = relay.at[way, slot]
                pl.when(sends)(
                    lambda: arrived(relay.at[way, slot], hop_r.at[kind, way, slot], row, z))
            if k == d - 1:
                dst, recv = last(jnp.clip(s, 0, 3)), recv_last.at[0]
            else:
                slot_on = slots[d, k + 1]
                dst, recv = relay.at[way, slot_on], hop_r.at[kind, way, slot_on]
            go(Link("z", src, dst, recv, row, z + sign, sends))

    def lines(ref, c):
        return ref.at[pl.ds(pl.multiple_of(c * 128, 128), 128), :]

    def hop_tok(d, k):
        hop(0, relay_tok, window, lambda s: got_x.at[s], tok_r, d, k)

    def hop_cot(d, k):
        hop(1, relay_cot, lambda c: lines(cot_in, c), lambda s: got_g.at[s], cot_r, d, k)

    def hop_mixed(d, k):
        hop(2, relay_mixed, lambda c: mixed_send.at[c], lambda s: lines(mixed_got, s), mx_r, d, k)

    def hop_input(d, k):
        hop(3, relay_input, lambda c: input_send.at[c], lambda s: lines(input_got, s), ig_r, d, k)

    def send_gain():
        for step in range(1, 4):
            c = (z + step) % 4
            go(Link("z", gain_sum.at[c], gain_z.at[z], gz_r.at[0], row, c))

    order = (z, 1 + z % 2, 2 - 2 * (z % 2) + z // 2, 3 - 3 * (z // 2))

    def near(i, c, r, part):
        size, cut = ROWS[i], SPLIT[i]
        start, count = {"all": (0, size), "a": (0, cut), "b": (cut, size - cut)}[part]
        return at_rows(ws[i], c, pl.multiple_of(r * size + start, 16), count)

    def gather_link(way, i, c, r, part, recv, to_row, to_col, when=None):
        ref = near(i, c, r, part)
        go(Link(way, ref, ref, recv, to_row, to_col, when))

    def gather_z(i, j):
        c = order[j]
        if j > 0:
            arrived(near(i, c, row, "all"), az_r.at[i, c], row, z)
        right = z < 3 if j == 0 else (c < z) & (z < 3)
        left = z > 0 if j == 0 else (c > z) & (z > 0)
        gather_link("z", i, c, row, "all", az_r.at[i, c], row, z + 1, right)
        gather_link("z", i, c, row, "all", az_r.at[i, c], row, z - 1, left)

    def gather_xy(i, j):
        c = order[j]
        gather_link("x", i, c, row, "a", ax_r.at[i, c], rx, z)
        gather_link("y", i, c, row, "b", ay_r.at[i, c], ry, z)
        gather_link("x", i, c, row, "b", al_r.at[i, c], rx, z)
        gather_link("y", i, c, row, "a", al_r.at[i, c], ry, z)
        gather_link("c", i, c, row, "all", ac_r.at[i, c], rc, z)

    def gather_second_x(i, j):
        c = order[j]
        arrived(near(i, c, rx, "a"), ax_r.at[i, c], rx, z)
        gather_link("y", i, c, rx, "a", al_r.at[i, c], ry, z)

    def gather_second_y(i, j):
        c = order[j]
        arrived(near(i, c, ry, "b"), ay_r.at[i, c], ry, z)
        gather_link("x", i, c, ry, "b", al_r.at[i, c], rx, z)

    def first_rows(i, c, count):
        return ws[i].at[c, pl.ds(0, count), :]

    def gather_third(i, j):
        c = order[j]
        arrived(first_rows(i, c, 2 * ROWS[i]), al_r.at[i, c], rx, z)
        for r in (rx, ry, rxy):
            gather_link("c", i, c, r, "all", ac_r.at[i, c], rc, z)

    def gather_done(i, j):
        c = order[j]
        arrived(first_rows(i, c, 4 * ROWS[i]), ac_r.at[i, c], rc, z)

    def pack_own():
        r96 = pl.ds(pl.multiple_of(row * 96, 16), 96)
        r144 = pl.ds(pl.multiple_of(row * 144, 16), 144)
        q, k, v = qkv_in[0], qkv_in[1], qkv_in[2]
        gate, other = in_in[:, 0, :], in_in[:, 1, :]
        w1[z, r96, :] = jnp.concatenate(
            [q[:, :128], k[:, :128], v[:, :128], q[:, 128:], k[:, 128:], v[:, 128:],
             out_in[...]], axis=1)
        w2[z, r96, :] = jnp.concatenate([gate[:, :256], other[:, :256]], axis=1)
        tail = jnp.concatenate([gate[:, 256:], other[:, 256:]], axis=1)
        tail = jnp.concatenate([tail, jnp.zeros((48, 64), BF)], axis=0)
        w3[z, r144, :] = jnp.concatenate([down_in[...], tail], axis=1)
        gains_in[...] = jnp.zeros((8, 256), F32)
        gains_in[0:1, 0:192] = gain_one_in[...].reshape(1, 192)
        gains_in[1:2, 0:192] = gain_two_in[...].reshape(1, 192)

    def take_tokens():
        got_x[z] = window(z)[...]
        arrived(got_x.at[pl.ds(0, 3)], tok_r.at[0], row, z)
        got_gain[pl.ds(z, 1)] = gains_in[...][None]
        arrived(got_gain.at[pl.ds(0, 3)], gn_r.at[0], row, z)
        at = 0
        for low, high, lane in ((32, 160, 0), (32, 160, 192), (0, 32, 0), (0, 32, 192),
                                (160, 192, 0), (160, 192, 192)):
            x_all[at : at + high - low, :] = jnp.concatenate(
                [got_x[c, low:high, lane : lane + 192].astype(F32) for c in range(4)], axis=1)
            at += high - low

    def gain_row(which):
        return jnp.concatenate([got_gain[c, which : which + 1, 0:192] for c in range(4)], axis=1)

    def window_ids(first, length):
        last = ids_in.shape[0] - 1
        spot = first // 128
        near_rows = [ids_in[pl.ds(jnp.clip(spot + n, 0, last), 1), :] for n in range(-1, 3)]
        base = near_rows[1][0:1, 0:1]
        rel = jnp.concatenate(near_rows, axis=0) - base
        rel = jnp.clip(rel, -200, 200).astype(BF)
        source = lax.broadcasted_iota(jnp.int32, (128, 128), 0)
        target = lane_iota((128, 128))
        pick = (source == jnp.where(target < 64, 2 * target, 2 * target - 127)).astype(BF)
        rel = jnp.concatenate([rel, jnp.zeros((4, 128), BF)], axis=0)
        rel = dot(rel, pick)
        keys = jnp.concatenate(
            [rel[1:2, :64], rel[2:3, :64], rel[1:2, 64:], rel[2:3, 64:], rel[0:1, 32:64],
             rel[0:1, 96:], rel[3:4, :32], rel[3:4, 64:96]], axis=1)
        lane = lane_iota((1, EXT))
        lost = (lane >= 256) & (lane < 320) & (first % length == 0)
        lost |= (lane >= 320) & ((first + OWN) % length == 0)
        keys = jnp.where(lost, 1000.0, keys)
        own_ids[...] = jnp.broadcast_to(keys[:, :OWN], (8, OWN))
        return keys, own_ids[...].T[:, 0:1]

    def tables():
        spot = lax.broadcasted_iota(jnp.int32, (EXT, 128), 0)
        halo = spot - 256
        place = jnp.where(
            spot < 128, 2 * spot, jnp.where(
                spot < 256, 2 * spot - 255, jnp.where(
                    halo < 32, 2 * halo - 64, jnp.where(
                        halo < 64, 2 * halo - 127, jnp.where(
                            halo < 96, 2 * halo + 128, 2 * halo + 65)))))
        first, length = start_of(row, z)
        place = (place + first + length) % length
        angle = place.astype(F32) * freq_in[0:1, :]
        cos_t[...] = jnp.cos(angle)
        turn = jnp.where((lane_iota((EXT, 128)) % 64) < 32, -1.0, 1.0)
        sin_t[...] = jnp.sin(angle) * turn
        key_ids, query_ids = window_ids(first, length)
        qrow = lax.broadcasted_iota(jnp.int32, (OWN, EXT), 0)
        qplace = jnp.where(qrow < 128, 2 * qrow, 2 * qrow - 255)
        kcol = lane_iota((OWN, EXT))
        khalo = kcol - 256
        kplace = jnp.where(
            kcol < 128, 2 * kcol, jnp.where(
                kcol < 256, 2 * kcol - 255, jnp.where(
                    khalo < 32, 2 * khalo - 64, jnp.where(
                        khalo < 64, 2 * khalo - 127, jnp.where(
                            khalo < 96, 2 * khalo + 128, 2 * khalo + 65)))))
        allowed = (jnp.abs(qplace - kplace) <= HALF) & (query_ids == key_ids)
        bias[...] = jnp.where(allowed, 0.0, -1e30)

    def statistics(v):
        mu = jnp.mean(v, axis=1, keepdims=True)
        inv = lax.rsqrt(jnp.mean(v * v, axis=1, keepdims=True) - mu * mu + EPSILON)
        return (v - mu) * inv, inv

    def norm_one():
        hat, inv = statistics(x_all[0:OWN, :])
        hat1[...] = hat
        stat[0] = jnp.broadcast_to(inv, (OWN, 128))
        gain = gain_row(0)
        n1[0:OWN, :] = (hat * gain).astype(BF)
        hat, _ = statistics(x_all[OWN:EXT, :])
        n1[OWN:EXT, :] = (hat * gain).astype(BF)

    def take_cotangent():
        arrived(got_g.at[pl.ds(0, 3)], cot_r.at[0], row, z)
        pad = jnp.zeros((128, 64), BF)
        for c in range(4):
            for odd in range(2):
                cot_pad[128 * odd : 128 * odd + 128, 256 * c : 256 * c + 256] = jnp.concatenate(
                    [got_g[c, :, 192 * odd : 192 * odd + 192], pad], axis=1)

    low_lanes = lambda shape: lane_iota(shape) < 64

    def forward_heads(j):
        c = order[j]
        proj = dot(n1[...], w1[c, :, 0:640])
        cos, sin = cos_t[...], sin_t[...]
        rot = lambda tile, n: tile * cos[0:n] + swap_halves(tile) * sin[0:n]
        qs[c, 0] = (rot(proj[0:OWN, 0:128], OWN) * 0.125).astype(BF)
        ks[c, 0] = rot(proj[:, 128:256], EXT).astype(BF)
        vs[c, 0] = proj[:, 256:384].astype(BF)
        third = rot(proj[:, 384:512], EXT)
        low = low_lanes((EXT, 128))
        qs[c, 1] = jnp.where(low[0:OWN], third[0:OWN] * 0.125, 0.0).astype(BF)
        ks[c, 1] = jnp.where(low, pltpu.roll(third, 64, 1), 0.0).astype(BF)
        vs[c, 1] = jnp.where(low, proj[:, 512:640], 0.0).astype(BF)

        def head(h, q, k):
            scores = dot_nt(q, k) + bias[...]
            weight = jnp.exp(scores - jnp.max(scores, axis=1, keepdims=True))
            weight = weight * (1.0 / jnp.sum(weight, axis=1, keepdims=True))
            probs[3 * c + h] = weight
            return weight.astype(BF)

        zero = jnp.zeros((), BF)
        lowq, lowk = low_lanes((OWN, 128)), low
        q, k, v = qs[c, 0], ks[c, 0], vs[c, 0]
        both = dot(head(0, jnp.where(lowq, q, zero), k), jnp.where(lowk, v, zero))
        both += dot(head(1, jnp.where(lowq, zero, q), k), jnp.where(lowk, zero, v))
        att_c[c, :, 0:128] = both.astype(BF)
        att_c[c, :, 128:256] = dot(head(2, qs[c, 1], ks[c, 1]), vs[c, 1]).astype(BF)

    def forward_middle():
        for c in range(4):
            att[:, 192 * c : 192 * c + 192] = att_c[c, :, 0:192]
        for c in range(4):
            out = dot(att[...], w1[c, :, 512:768])
            mid[:, 192 * c : 192 * c + 192] = (
                x_all[0:OWN, 192 * c : 192 * c + 192] + out[:, 64:256])
        hat, inv = statistics(mid[...])
        hat2[...] = hat
        stat[1] = jnp.broadcast_to(inv, (OWN, 128))
        n2[...] = (hat * gain_row(1)).astype(BF)

    def gelu_parts(g):
        phi = 0.5 * (1.0 + lax.erf(g * 0.7071067811865476))
        return g * phi, phi + g * (jnp.exp(g * g * -0.5) * 0.3989422804014327)

    def forward_hidden(j):
        c = order[j]
        both = dot(n2[...], w2[c])
        value, slope = gelu_parts(both[:, 0:256])
        other = both[:, 256:512]
        gel[c] = value
        gel_up[c] = other * slope
        hid[c] = (value * other).astype(BF)

    def forward_tail():
        for c in range(4):
            for r in range(8):
                tail_in[96 * r : 96 * r + 96, 128 * c : 128 * c + 128] = (
                    w3[c, 144 * r : 144 * r + 96, 128:256])
                if r < 4:
                    tail_down[c, 32 * r : 32 * r + 32, :] = (
                        w3[c, 288 * r + 256 : 288 * r + 288, :])
        tails = dot(n2[...], tail_in[...])
        lanes = lane_iota((OWN, 128)) // 32
        packed = jnp.zeros((OWN, 128), F32)
        for c in range(4):
            tile = tails[:, 128 * c : 128 * c + 128]
            value, slope = gelu_parts(tile)
            other = pltpu.roll(tile, 96, 1)
            gel_t[c] = value
            gel_up_t[c] = other * slope
            moved = pltpu.roll(value * other, (32 * c + 64) % 128, 1)
            packed = jnp.where(lanes == c, moved, packed)
        hid_tail[...] = packed.astype(BF)

    def forward_mixed():
        for k in range(4):
            total = dot(hid_tail[...], tail_down[k])
            for c in range(4):
                total += dot(hid[c], w3[k, 288 * c : 288 * c + 256, :])
            out = (mid[:, 192 * k : 192 * k + 192] + total[:, 0:192]).astype(BF)
            mixed_send[k] = jnp.concatenate([out[0:128], out[128:256]], axis=1)

    def hidden_rows(c):
        return pl.ds(pl.multiple_of(c * 288, 16), 256)

    def backward_hidden(j):
        c = order[j]
        grad = dot_nt(cot_pad[:, 0:256], w3[0, hidden_rows(c), :])
        for k in range(1, 4):
            grad += dot_nt(cot_pad[:, 256 * k : 256 * k + 256], w3[k, hidden_rows(c), :])
        d_gate[c] = jnp.concatenate([grad * gel_up[c], grad * gel[c]], axis=1).astype(BF)

    def backward_tail():
        grad = dot_nt(cot_pad[:, 0:256], tail_down[0])
        for k in range(1, 4):
            grad += dot_nt(cot_pad[:, 256 * k : 256 * k + 256], tail_down[k])
        lanes = lane_iota((OWN, 128))
        for c in range(4):
            gate = pltpu.roll(grad, (64 - 32 * c) % 128, 1) * gel_up_t[c]
            other = pltpu.roll(grad, (96 - 32 * c) % 128, 1) * pltpu.roll(gel_t[c], 32, 1)
            d_tail[:, 128 * c : 128 * c + 128] = jnp.where(
                lanes >= 96, other, jnp.where(lanes >= 64, gate, 0.0)).astype(BF)

    def grad_down(j):
        c = order[j]
        part = dot_tn(hid[c], cot_pad[...]).astype(BF)
        for k in range(4):
            d3[k, hidden_rows(c), :] = part[:, 256 * k : 256 * k + 256]

    def grad_tail():
        part = dot_tn(hid_tail[...], cot_pad[...]).astype(BF)
        for c in range(4):
            for k in range(4):
                d3[k, 288 * c + 256 : 288 * c + 288, :] = (
                    part[32 * c : 32 * c + 32, 256 * k : 256 * k + 256])
        part = dot_tn(n2[...], d_tail[...]).astype(BF)
        for c in range(4):
            for r in range(8):
                d3[c, 144 * r : 144 * r + 96, 128:256] = (
                    d3[c, 144 * r : 144 * r + 96, 128:256]
                    + part[96 * r : 96 * r + 96, 128 * c : 128 * c + 128])

    def grad_in(j):
        c = order[3 - j]
        d2[c] = dot_tn(n2[...], d_gate[c]).astype(BF)

    def norm_back(grad, hat, inv, gain):
        e = grad * gain
        return inv * (e - jnp.mean(e, axis=1, keepdims=True)
                      - hat * jnp.mean(e * hat, axis=1, keepdims=True))

    def backward_middle():
        grad = dot_nt(d_tail[...], tail_in[...])
        for c in range(4):
            grad += dot_nt(d_gate[c], w2[c])
        hat = hat2[...]
        gain_part[1:2, :] = jnp.sum(grad * hat, axis=0, keepdims=True)
        back = norm_back(grad, hat, stat[1][:, 0:1], gain_row(1))
        pad = jnp.zeros((OWN, 64), BF)
        total = jnp.concatenate(
            [cot_pad[:, 256 * c : 256 * c + 192].astype(F32) for c in range(4)], axis=1) + back
        mid_grad[...] = total
        branch = total.astype(BF)
        for c in range(4):
            branch_pad[:, 256 * c : 256 * c + 256] = jnp.concatenate(
                [pad, branch[:, 192 * c : 192 * c + 192]], axis=1)
        grad = dot_nt(branch_pad[:, 0:256], w1[0, :, 512:768])
        for c in range(1, 4):
            grad += dot_nt(branch_pad[:, 256 * c : 256 * c + 256], w1[c, :, 512:768])
        grad = grad.astype(BF)
        for c in range(4):
            att_grad[c] = jnp.concatenate([grad[:, 192 * c : 192 * c + 192], pad], axis=1)

    def grad_out():
        part = dot_tn(att[...], branch_pad[...]).astype(BF)
        for c in range(4):
            d1[c, :, 512:768] = part[:, 256 * c : 256 * c + 256]

    def backward_heads(j):
        c = order[3 - j]
        zero = jnp.zeros((), BF)
        lowq, lowk = low_lanes((OWN, 128)), low_lanes((EXT, 128))

        def head(h, g, v):
            weight = probs[3 * c + h]
            prob_grad = dot_nt(g, v)
            inner = jnp.sum(weight * prob_grad, axis=1, keepdims=True)
            return (weight * (prob_grad - inner)).astype(BF), weight.astype(BF)

        q, k, v = qs[c, 0], ks[c, 0], vs[c, 0]
        g = att_grad[c, :, 0:128]
        g0, g1 = jnp.where(lowq, g, zero), jnp.where(lowq, zero, g)
        s0, p0 = head(0, g0, v)
        s1, p1 = head(1, g1, v)
        dq = dot(s0, jnp.where(lowk, k, zero)) + dot(s1, jnp.where(lowk, zero, k))
        dk = dot_tn(s0, jnp.where(lowq, q, zero)) + dot_tn(s1, jnp.where(lowq, zero, q))
        dv = dot_tn(p0, g0) + dot_tn(p1, g1)
        g2 = att_grad[c, :, 128:256]
        s2, p2 = head(2, g2, vs[c, 1])
        dq2 = dot(s2, ks[c, 1]) * 0.125
        dk2 = pltpu.roll(dot_tn(s2, qs[c, 1]), 64, 1)
        dv2 = dot_tn(p2, g2)
        cos, sin = cos_t[...], sin_t[...]
        back = lambda tile: tile * cos - swap_halves(tile) * sin
        none = jnp.zeros((EXT - OWN, 128), F32)
        dq = jnp.concatenate([dq * 0.125, none], axis=0)
        d_proj[c, :, 0:128] = back(dq).astype(BF)
        d_proj[c, :, 128:256] = back(dk).astype(BF)
        d_proj[c, :, 256:384] = dv.astype(BF)
        d_proj[c, :, 384:512] = back(jnp.concatenate([dq2, none], axis=0) + dk2).astype(BF)
        d_proj[c, :, 512:640] = dv2.astype(BF)

    def grad_qkv(j):
        c = order[3 - j]
        part = dot_tn(n1[...], d_proj[c]).astype(BF)
        d1[c, :, 0:512] = part[:, 0:512]
        d1[c, :, 512:640] = d1[c, :, 512:640] + part[:, 512:640]

    def backward_first():
        grad = dot_nt(d_proj[0], w1[0, :, 0:640])
        for c in range(1, 4):
            grad += dot_nt(d_proj[c], w1[c, :, 0:640])
        n1_grad[...] = grad[0:OWN]
        halo_out[...] = grad[OWN:EXT].astype(BF)

    edge_low, edge_high = (z == 0) & (row == 0), (z == 3) & (row == 7)
    left_row = jnp.where(z == 0, row - 1, row)
    right_row = jnp.where(z == 3, row + 1, row)
    left_col, right_col = (z + 3) % 4, (z + 1) % 4

    def halo_send():
        go(Link("z", halo_out.at[pl.ds(0, 64), :], halo_right, ha_r.at[1], left_row, left_col, jnp.logical_not(edge_low)))
        go(Link("z", halo_out.at[pl.ds(64, 64), :], halo_left, ha_r.at[0], right_row, right_col, jnp.logical_not(edge_high)))

    def halo_take():
        @pl.when(jnp.logical_not(edge_low))
        def _():
            arrived(halo_left, ha_r.at[0], left_row, left_col)
            n1_grad[0:32, :] += halo_left[0:32, :].astype(F32)
            n1_grad[128:160, :] += halo_left[32:64, :].astype(F32)

        @pl.when(jnp.logical_not(edge_high))
        def _():
            arrived(halo_right, ha_r.at[1], right_row, right_col)
            n1_grad[96:128, :] += halo_right[0:32, :].astype(F32)
            n1_grad[224:256, :] += halo_right[32:64, :].astype(F32)

    def backward_last():
        grad, hat = n1_grad[...], hat1[...]
        gain_part[0:1, :] = jnp.sum(grad * hat, axis=0, keepdims=True)
        total = mid_grad[...] + norm_back(grad, hat, stat[0][:, 0:1], gain_row(0))
        out = total.astype(BF)
        for k in range(4):
            mine = out[:, 192 * k : 192 * k + 192]
            input_send[k] = jnp.concatenate([mine[0:128], mine[128:256]], axis=1)
        for c in range(4):
            gain_part_c = gain_part[0:2, 192 * c : 192 * c + 192]
            gain_sum[c, 0:2, 0:192] = gain_part_c

    cores = (core1, core2, core3)
    xas, xbs, yas, ybs = (xa1, xa2, xa3), (xb1, xb2, xb3), (ya1, ya2, ya3), (yb1, yb2, yb3)
    zbs = (zb1, zb2, zb3)
    outs = (grad_one, grad_two, grad_three)

    def unpack_outs():
        one, two, three = grad_one[...], grad_two[...], grad_three[...]
        for n in range(3):
            qkv_out[n] = jnp.concatenate(
                [one[:, 128 * n : 128 * n + 128], one[:, 384 + 64 * n : 448 + 64 * n]], axis=1)
        out_out[...] = one[:, 576:768]
        for n in range(2):
            in_out[:, n, :] = jnp.concatenate(
                [two[:, 256 * n : 256 * n + 256], three[0:96, 192 + 32 * n : 224 + 32 * n]],
                axis=1)
        down_out[...] = three[:, 0:192]


    def place(i, c, r, part):
        size, cut = ROWS[i], SPLIT[i]
        start, count = {"all": (0, size), "a": (0, cut), "b": (cut, size - cut)}[part]
        return c, pl.ds(pl.multiple_of(r * size + start, 16), count)

    def piece(i, c, r, part):
        lead, span = place(i, c, r, part)
        return ds_[i].at[lead, span, :]

    def add_into(i, c, r, part, value):
        lead, span = place(i, c, r, part)
        ds_[i][lead, span, :] = ds_[i][lead, span, :] + value

    def sum_first(i, j):
        c = order[3 - j]
        for n in range(4):
            go(Link("c", piece(i, c, 2 * n + 1 - core, "all"), cores[i].at[c, n], rc_r.at[i, c],
                    rc, z))

    def sum_second(i, j):
        c = order[3 - j]
        arrived(cores[i].at[c], rc_r.at[i, c], rc, z)
        for n in range(4):
            add_into(i, c, 2 * n + core, "all", cores[i][c, n])
        for y in range(2):
            go(Link("x", piece(i, c, 4 * y + 2 * (1 - xc) + core, "a"), xas[i].at[c, y],
                    rx_r.at[i, c], rx, z))
        for x in range(2):
            go(Link("y", piece(i, c, 4 * (1 - yc) + 2 * x + core, "b"), ybs[i].at[c, x],
                    ry_r.at[i, c], ry, z))

    def sum_third_x(i, j):
        c = order[3 - j]
        arrived(xas[i].at[c], rx_r.at[i, c], rx, z)
        for y in range(2):
            add_into(i, c, 4 * y + 2 * xc + core, "a", xas[i][c, y])
        go(Link("y", piece(i, c, ry, "a"), yas[i].at[c], rl_r.at[i, c], ry, z))

    def sum_third_y(i, j):
        c = order[3 - j]
        arrived(ybs[i].at[c], ry_r.at[i, c], ry, z)
        for x in range(2):
            add_into(i, c, 4 * yc + 2 * x + core, "b", ybs[i][c, x])
        go(Link("x", piece(i, c, rx, "b"), xbs[i].at[c], rl_r.at[i, c], rx, z))

    def sum_fourth(i, j):
        c = order[3 - j]
        arrived(zbs[i].at[c], rl_r.at[i, c], ry, z)
        add_into(i, c, row, "a", yas[i][c])
        add_into(i, c, row, "b", xbs[i][c])

        @pl.when(((c > z) & (z > 0)) | ((c < z) & (z < 3)))
        def _():
            arrived(zbs[i].at[c], rz_r.at[i, c], row, z)
            add_into(i, c, row, "all", zbs[i][c])

        go(Link("z", piece(i, c, row, "all"), zbs[i].at[c], rz_r.at[i, c], row, z + 1, c > z))
        slot = c + (4 - c) * (1 - jnp.minimum(jnp.abs(z - 1 - c), 1))
        go(Link("z", piece(i, c, row, "all"), zbs[i].at[slot], rz_r.at[i, slot], row, z - 1, c < z))

    def sum_last(i):
        lead, span = place(i, z, row, "all")
        outs[i][...] = ds_[i][lead, span, :].astype(F32)

        @pl.when(z > 0)
        def _():
            arrived(zbs[i].at[z], rz_r.at[i, z], row, z)
            outs[i][...] = outs[i][...] + zbs[i][z].astype(F32)

        @pl.when(z < 3)
        def _():
            arrived(zbs[i].at[4], rz_r.at[i, 4], row, z)
            outs[i][...] = outs[i][...] + zbs[i][4].astype(F32)

    def gains_first():
        gain_z[pl.ds(z, 1)] = gain_sum[pl.ds(z, 1)]
        arrived(gain_z.at[pl.ds(0, 3)], gz_r.at[0], row, z)
        gain_all[pl.ds(row, 1)] = (gain_z[0] + gain_z[1] + gain_z[2] + gain_z[3])[None]
        for step in range(1, 8):
            go(Link("x", gain_all.at[row], gain_all.at[row], gp_r.at[0], (row + step) % 8, z))

    def gains_last():
        arrived(gain_all.at[pl.ds(0, 7)], gp_r.at[0], row, z)
        total = gain_all[0]
        for r in range(1, 8):
            total = total + gain_all[r]
        gain_one_out[...] = total[0:1, 0:192].reshape(192)
        gain_two_out[...] = total[1:2, 0:192].reshape(192)

    def results(which, step):
        got, out, n = {"mx": (mixed_got, mixed_out, 2), "ig": (input_got, input_out, 3)}[which]
        step(pltpu.make_async_copy(got, out, io.at[n]))

    def finish(which):
        got, send, recv = {
            "mx": (mixed_got, mixed_send, mx_r), "ig": (input_got, input_send, ig_r)}[which]
        lines(got, z)[...] = send[z]
        arrived(got.at[pl.ds(0, 384), :], recv.at[0], row, z)
        results(which, lambda copy: copy.start())

    own_tokens(lambda copy: copy.start())
    pack_own()
    pl.semaphore_wait(barrier, peers)
    gather_z(0, 0)
    send_edges()
    gather_xy(0, 0)
    gather_z(1, 0)
    take_edges()
    gather_xy(1, 0)
    hop_tok(1, 0)
    gather_z(0, 1)
    gather_z(2, 0)
    gather_xy(0, 1)
    gather_z(1, 1)
    gather_xy(1, 1)
    gather_second_x(1, 0)
    hop_tok(3, 0)
    gather_second_y(1, 0)
    gather_second_y(0, 1)
    gather_second_x(0, 1)
    gather_z(0, 2)
    gather_xy(2, 0)
    hop_tok(2, 0)
    gather_second_x(0, 0)
    gather_second_y(0, 0)
    gather_second_y(1, 1)
    gather_second_x(1, 1)
    gather_xy(0, 2)
    gather_z(0, 3)
    hop_tok(3, 1)
    gather_z(2, 1)
    gather_xy(2, 1)
    gather_xy(0, 3)
    gather_third(1, 0)
    hop_tok(2, 1)
    gather_z(2, 2)
    gather_xy(2, 2)
    gather_third(0, 0)
    gather_second_x(2, 0)
    hop_cot(3, 0)
    gather_third(1, 1)
    gather_third(0, 1)
    gather_second_x(0, 2)
    gather_z(1, 2)
    hop_cot(2, 0)
    gather_done(1, 0)
    gather_done(1, 1)
    hop_tok(3, 2)
    tables()
    gather_second_y(2, 0)
    gather_done(0, 1)
    gather_second_y(0, 2)
    gather_second_y(2, 1)
    gather_done(0, 0)
    take_tokens()
    norm_one()
    gather_second_x(2, 1)
    gather_z(2, 3)
    gather_second_x(0, 3)
    gather_second_y(0, 3)
    forward_heads(1)
    gather_xy(2, 3)
    gather_z(1, 3)
    gather_xy(1, 3)
    hop_cot(3, 1)
    gather_third(0, 2)
    gather_third(2, 0)
    gather_second_x(2, 2)
    gather_second_y(2, 2)
    hop_cot(2, 1)
    forward_heads(0)
    hop_cot(1, 0)
    gather_done(0, 2)
    gather_third(0, 3)
    forward_heads(2)
    gather_second_y(2, 3)
    gather_done(0, 3)
    gather_second_x(2, 3)
    hop_cot(3, 2)
    gather_third(2, 1)
    gather_second_y(1, 3)
    gather_done(2, 0)
    gather_second_x(1, 3)
    gather_xy(1, 2)
    forward_heads(3)
    gather_third(2, 2)
    gather_done(2, 1)
    forward_middle()
    gather_third(2, 3)
    forward_hidden(0)
    take_cotangent()
    forward_hidden(1)
    gather_second_y(1, 2)
    gather_third(1, 3)
    gather_done(2, 3)
    gather_done(2, 2)
    grad_down(1)
    gather_second_x(1, 2)
    backward_hidden(1)
    backward_hidden(0)
    grad_in(2)
    sum_first(1, 2)
    grad_in(3)
    forward_tail()
    backward_tail()
    gather_done(1, 3)
    grad_down(0)
    forward_hidden(3)
    backward_hidden(3)
    gather_third(1, 2)
    grad_down(3)
    sum_second(1, 2)
    sum_first(1, 3)
    grad_in(0)
    sum_first(1, 0)
    gather_done(1, 2)
    forward_hidden(2)
    backward_hidden(2)
    backward_middle()
    sum_second(1, 0)
    grad_down(2)
    grad_tail()
    sum_first(2, 2)
    sum_first(2, 0)
    sum_first(2, 1)
    forward_mixed()
    sum_second(1, 3)
    backward_heads(1)
    sum_second(2, 1)
    sum_second(2, 0)
    sum_second(2, 2)
    sum_first(2, 3)
    hop_mixed(3, 0)
    backward_heads(0)
    backward_heads(2)
    hop_mixed(2, 0)
    backward_heads(3)
    sum_second(2, 3)
    backward_first()
    halo_send()
    grad_in(1)
    hop_mixed(3, 1)
    sum_third_x(2, 2)
    sum_third_y(2, 0)
    grad_out()
    sum_first(1, 1)
    grad_qkv(0)
    hop_mixed(1, 0)
    sum_third_x(2, 0)
    sum_first(0, 0)
    sum_second(1, 1)
    halo_take()
    backward_last()
    hop_input(3, 0)
    sum_second(0, 0)
    grad_qkv(2)
    send_gain()
    sum_third_x(2, 3)
    sum_third_y(2, 1)
    hop_input(1, 0)
    hop_input(2, 0)
    sum_first(0, 2)
    grad_qkv(1)
    sum_third_x(1, 0)
    sum_first(0, 1)
    sum_third_y(2, 2)
    hop_input(3, 1)
    sum_third_y(1, 0)
    sum_third_x(2, 1)
    sum_third_x(0, 0)
    sum_third_y(0, 0)
    hop_mixed(2, 1)
    sum_second(0, 1)
    hop_input(2, 1)
    hop_input(3, 2)
    sum_fourth(2, 0)
    sum_third_y(1, 1)
    sum_third_x(1, 1)
    sum_second(0, 2)
    sum_fourth(1, 0)
    grad_qkv(3)
    hop_mixed(3, 2)
    sum_fourth(0, 0)
    sum_third_y(0, 1)
    sum_third_x(0, 1)
    sum_fourth(2, 1)
    sum_first(0, 3)
    sum_third_x(1, 2)
    sum_third_y(1, 2)
    sum_fourth(2, 2)
    sum_fourth(1, 1)
    sum_third_y(0, 2)
    sum_third_x(0, 2)
    sum_second(0, 3)
    sum_third_y(2, 3)
    finish("mx")
    sum_fourth(0, 1)
    sum_fourth(1, 2)
    gains_first()
    sum_fourth(0, 2)
    sum_third_x(1, 3)
    sum_third_y(1, 3)
    sum_third_x(0, 3)
    finish("ig")
    sum_third_y(0, 3)
    sum_fourth(2, 3)
    gains_last()
    sum_fourth(1, 3)
    sum_last(1)
    sum_last(2)
    sum_fourth(0, 3)
    sum_last(0)
    unpack_outs()
    results("mx", lambda copy: copy.wait())
    results("ig", lambda copy: copy.wait())
    ways.drain()


def hand_over(*refs):
    for n in range(8):
        refs[8 + n][...] = refs[n][...].astype(refs[8 + n].dtype)


def fast_local(
    tokens, segment_ids, gain_one, qkv_weight, out_weight, gain_two, in_weight, down_weight,
    cotangent,
):
    rows_all = tokens.shape[1] * 2 * lax.axis_size("row")
    length = min(SEQ_MAX, rows_all)

    def start_of(row, z):
        return (row * 4 + z) * OWN, length

    frequency = 10000.0 ** (-(np.arange(HEAD_DIM // 2) * 2.0) / HEAD_DIM)
    frequency = jnp.asarray(np.tile(frequency.astype(np.float32), 4)[None, :].repeat(8, 0))
    vmem, dma = pltpu.VMEM, pltpu.SemaphoreType.DMA
    shapes = [
        vmem((576, 384), BF), vmem((4, 192, 384), BF), vmem((4, 128, 384), BF),
        vmem((4, 8, 256), F32),
        vmem((4, 768, 768), BF), vmem((4, 768, 512), BF), vmem((4, 1152, 256), BF),
        vmem((4, 768, 768), BF), vmem((4, 768, 512), BF), vmem((4, 1152, 256), BF),
    ]
    shapes += [vmem((4, 4, ROWS[i], COLS[i]), BF) for i in range(3)]
    shapes += [vmem((4, 2, SPLIT[i], COLS[i]), BF) for i in range(3)]
    shapes += [vmem((4, ROWS[i] - SPLIT[i], COLS[i]), BF) for i in range(3)]
    shapes += [vmem((4, SPLIT[i], COLS[i]), BF) for i in range(3)]
    shapes += [vmem((4, 2, ROWS[i] - SPLIT[i], COLS[i]), BF) for i in range(3)]
    shapes += [vmem((5, ROWS[i], COLS[i]), BF) for i in range(3)]
    shapes += [
        vmem((8, 256), F32), vmem((8, OWN), F32),
        vmem((EXT, 768), F32), vmem((EXT, 128), F32), vmem((EXT, 128), F32),
        vmem((OWN, EXT), F32), vmem((EXT, 768), BF), vmem((OWN, 768), F32),
        vmem((2, OWN, 128), F32), vmem((4, 2, OWN, 128), BF), vmem((4, 2, EXT, 128), BF),
        vmem((4, 2, EXT, 128), BF), vmem((12, OWN, EXT), F32),
        vmem((4, OWN, 256), BF), vmem((OWN, 768), BF),
        vmem((OWN, 768), F32), vmem((OWN, 768), F32), vmem((OWN, 768), BF),
        vmem((768, 512), BF), vmem((4, 128, 256), BF), vmem((4, OWN, 256), BF),
        vmem((OWN, 128), BF), vmem((4, OWN, 256), F32), vmem((4, OWN, 256), F32),
        vmem((4, OWN, 128), F32), vmem((4, OWN, 128), F32), vmem((OWN, 1024), BF),
        vmem((4, OWN, 512), BF), vmem((OWN, 512), BF),
        vmem((OWN, 1024), BF), vmem((4, OWN, 256), BF), vmem((4, EXT, 640), BF),
        vmem((128, 768), BF), vmem((64, 768), BF), vmem((64, 768), BF),
        vmem((4, 128, 384), BF), vmem((512, 384), BF),
        vmem((4, 128, 384), BF), vmem((512, 384), BF),
        vmem((2, 3, 192, 384), BF), vmem((2, 3, 128, 384), BF), vmem((2, 3, 128, 384), BF),
        vmem((2, 3, 128, 384), BF),
        vmem((8, 768), F32), vmem((4, 8, 256), F32), vmem((4, 8, 256), F32),
        vmem((8, 8, 256), F32), vmem((96, 768), F32), vmem((96, 512), F32), vmem((144, 256), F32),
        dma((16,)), dma((16,)), dma((24,)), dma((16,)), dma((4,)),
        dma((4, 2, 3)), dma((1,)), dma((1,)), dma((1,)), dma((1,)), dma((1,)),
        dma((3, 4)), dma((3, 4)), dma((3, 4)), dma((3, 4)), dma((3, 4)),
        dma((3, 4)), dma((3, 4)), dma((3, 4)), dma((3, 4)), dma((3, 5)),
        dma((2,)), dma((1,)), dma((1,)), dma((1,)), dma((1,)),
    ]
    whole, held = pl.BlockSpec(memory_space=pltpu.VMEM), pl.BlockSpec(memory_space=pl.ANY)
    results = (
        jax.ShapeDtypeStruct((512, 384), BF), jax.ShapeDtypeStruct((512, 384), F32),
        jax.ShapeDtypeStruct((3, 96, 192), F32), jax.ShapeDtypeStruct((96, 192), F32),
        jax.ShapeDtypeStruct((96, 2, 288), F32), jax.ShapeDtypeStruct((144, 192), F32),
        jax.ShapeDtypeStruct((192,), F32), jax.ShapeDtypeStruct((192,), F32),
    )
    outs = pl.pallas_call(
        functools.partial(layer_kernel, start_of=start_of),
        out_shape=(results[0], jax.ShapeDtypeStruct((512, 384), BF)) + results[2:],
        in_specs=[held] * 2 + [whole] * 8,
        out_specs=(held,) * 2 + (whole,) * 6,
        scratch_shapes=shapes,
        compiler_params=pltpu.CompilerParams(
            collective_id=0, has_side_effects=True, vmem_limit_bytes=63 * 1024 * 1024),
    )(tokens[0], cotangent[0], qkv_weight.transpose(1, 0, 2), out_weight, in_weight, down_weight,
      gain_one, gain_two, segment_ids.reshape(-1, 128), frequency)
    mixed, input_grad, qkv_grad, out_grad, in_grad, down_grad, one_grad, two_grad = pl.pallas_call(
        hand_over,
        out_shape=results,
        in_specs=[whole] * 8,
        out_specs=(whole,) * 8,
    )(*outs)
    return (
        mixed[None], input_grad[None], one_grad, qkv_grad.transpose(1, 0, 2), out_grad,
        two_grad, in_grad, down_grad,
    )


def solution(mesh):
    placed = (
        P("col", "row", None),
        P(),
        P("col"),
        P("row", None, "col"),
        P("row", "col"),
        P("col"),
        P("row", None, "col"),
        P("row", "col"),
        P("col", "row", None),
    )
    part = local
    if mesh.shape["row"] == 8 and mesh.shape["col"] == 4:
        part = fast_local
    return jax.shard_map(
        part,
        mesh=mesh,
        in_specs=placed,
        out_specs=(
            P("col", "row", None),
            P("col", "row", None),
            P("col"),
            P("row", None, "col"),
            P("row", "col"),
            P("col"),
            P("row", None, "col"),
            P("row", "col"),
        ),
        check_vma=False,
    )
```

```python
import functools

import jax
import jax.numpy as jnp
import numpy as np
from jax import lax
from jax.experimental import pallas as pl
from jax.experimental.pallas import tpu as pltpu
from jax.sharding import PartitionSpec as P

HEAD_DIM = 64
WINDOW = 128
SEQ_MAX = 4096


EPSILON = 1e-05


def with_halo(block, sides, width):
    for axis, dim in sides:
        count = lax.axis_size(axis)
        forward = [(i, i + 1) for i in range(count - 1)]
        backward = [(target, source) for source, target in forward]
        low = lax.ppermute(
            lax.slice_in_dim(block, block.shape[dim] - width, None, axis=dim), axis, forward
        )
        high = lax.ppermute(lax.slice_in_dim(block, 0, width, axis=dim), axis, backward)
        block = jnp.concatenate([low, block, high], axis=dim)
    return block


def rotate(values, cosine, sine_table):
    half_dim = values.shape[-1] // 2
    turned = jnp.concatenate([-values[..., half_dim:], values[..., :half_dim]], axis=-1)
    return values * cosine + turned * sine_table


def rotate_back(grad_rows, cosine, sine_table):
    half_dim = grad_rows.shape[-1] // 2
    turned = jnp.concatenate([-grad_rows[..., half_dim:], grad_rows[..., :half_dim]], axis=-1)
    return grad_rows * cosine - turned * sine_table


def spread(values):
    return lax.all_gather(values, "col", axis=1, tiled=True)


def collect(partial_rows):
    return lax.psum_scatter(partial_rows, "col", scatter_dimension=1, tiled=True)


def norm_forward(values, full_width):
    row_sums = lax.psum((jnp.sum(values, axis=1), jnp.sum(values * values, axis=1)), "col")
    mean_value = row_sums[0] / full_width
    variance = row_sums[1] / full_width - mean_value * mean_value
    inverse = lax.rsqrt(variance + EPSILON)
    return ((values - mean_value[:, None]) * inverse[:, None], inverse)


def norm_backward(grad_rows, scaled, inverse, gain_part, full_width):
    weighted = grad_rows * gain_part
    row_sums = lax.psum((jnp.sum(weighted, axis=1), jnp.sum(weighted * scaled, axis=1)), "col")
    input_part = inverse[:, None] * (
        weighted - row_sums[0][:, None] / full_width - scaled * (row_sums[1][:, None] / full_width)
    )
    return (input_part, jnp.sum(grad_rows * scaled, axis=0))


def geglu(gate_up):
    return jax.nn.gelu(gate_up[:, 0], approximate=False) * gate_up[:, 1]


def local(
    tokens,
    segment_ids,
    gain_one,
    qkv_weight,
    out_weight,
    gain_two,
    in_weight,
    down_weight,
    cotangent,
):
    pair_rows = tokens.shape[1]
    rows_here = pair_rows * 2
    tok_width = tokens.shape[2] // 2
    full_width = tok_width * lax.axis_size("col")
    heads_here = qkv_weight.shape[2] // HEAD_DIM
    head_width = heads_here * HEAD_DIM
    half_window = WINDOW // 2
    block_rows = min(512, rows_here)
    block_count = rows_here // block_rows
    key_span = block_rows + 2 * half_window
    score_scale = HEAD_DIM ** (-0.5)
    length = min(SEQ_MAX, rows_here * lax.axis_size("row"))
    first_row = lax.axis_index("row") * rows_here
    grad_rows = cotangent.reshape(rows_here, tok_width)
    qkv_full, out_full, in_full, down_full = (
        lax.all_gather(qkv_weight, "row", axis=0, tiled=True),
        lax.all_gather(out_weight, "row", axis=0, tiled=True),
        lax.all_gather(in_weight, "row", axis=0, tiled=True),
        lax.all_gather(down_weight, "row", axis=0, tiled=True),
    )
    global_rows = first_row + jnp.arange(rows_here, dtype=jnp.int32)
    places = (global_rows % length).astype(jnp.float32)
    frequencies = 10000.0 ** (-(jnp.arange(HEAD_DIM // 2, dtype=jnp.float32) * 2.0) / HEAD_DIM)
    angles = places[:, None] * frequencies[None, :]
    angles = jnp.concatenate([angles, angles], axis=1)[:, None, :]
    cosine = jnp.cos(angles)
    sine_table = jnp.sin(angles)
    query_ids = lax.dynamic_slice_in_dim(segment_ids, first_row, rows_here)
    padded_ids = jnp.pad(segment_ids, half_window, constant_values=-1)
    key_ids = lax.dynamic_slice_in_dim(padded_ids, first_row, rows_here + 2 * half_window)
    query_seqs = global_rows // length
    key_seqs = (
        first_row - half_window + jnp.arange(rows_here + 2 * half_window, dtype=jnp.int32)
    ) // length
    offsets = (
        jnp.arange(key_span, dtype=jnp.int32)[None, :]
        - half_window
        - jnp.arange(block_rows, dtype=jnp.int32)[:, None]
    )
    in_window = jnp.abs(offsets) <= half_window

    def block_scores(block_start, block_queries, block_keys):
        same_doc = (
            query_ids[block_start : block_start + block_rows, None]
            == key_ids[None, block_start : block_start + key_span]
        )
        same_seq = (
            query_seqs[block_start : block_start + block_rows, None]
            == key_seqs[None, block_start : block_start + key_span]
        )
        allowed = in_window & same_doc & same_seq
        scores = (
            jnp.einsum(
                "qhd,khd->hqk", block_queries, block_keys, preferred_element_type=jnp.float32
            )
            * score_scale
        )
        return jnp.where(allowed[None], scores, -1e30)

    token_values = tokens.reshape(rows_here, tok_width).astype(jnp.float32)
    scaled_one, inverse_one = norm_forward(token_values, full_width)
    normed_one_full = spread((scaled_one * gain_one).astype(jnp.bfloat16))
    projected = jnp.einsum(
        "td,dsf->tsf", normed_one_full, qkv_full, preferred_element_type=jnp.float32
    )
    projected = projected.reshape(rows_here, 3, heads_here, HEAD_DIM)
    queries = rotate(projected[:, 0], cosine, sine_table).astype(jnp.bfloat16)
    key_rows = rotate(projected[:, 1], cosine, sine_table).astype(jnp.bfloat16)
    value_rows = projected[:, 2].astype(jnp.bfloat16)
    key_value = jnp.concatenate(
        [key_rows.reshape(rows_here, head_width), value_rows.reshape(rows_here, head_width)], axis=1
    )
    padded_pair = with_halo(key_value, (("row", 0),), half_window)
    padded_keys = padded_pair[:, :head_width].reshape(
        rows_here + 2 * half_window, heads_here, HEAD_DIM
    )
    padded_values = padded_pair[:, head_width:].reshape(
        rows_here + 2 * half_window, heads_here, HEAD_DIM
    )
    output_blocks = []
    total_blocks = []
    for block_number in range(block_count):
        block_start = block_number * block_rows
        masked = block_scores(
            block_start,
            queries[block_start : block_start + block_rows],
            padded_keys[block_start : block_start + key_span],
        )
        largest = jnp.max(masked, axis=-1, keepdims=True)
        log_total = largest + jnp.log(jnp.sum(jnp.exp(masked - largest), axis=-1, keepdims=True))
        weights = jnp.exp(masked - log_total).astype(jnp.bfloat16)
        output_blocks.append(
            jnp.einsum(
                "hqk,khd->qhd",
                weights,
                padded_values[block_start : block_start + key_span],
                preferred_element_type=jnp.float32,
            )
        )
        total_blocks.append(log_total)
    attended = (
        jnp.concatenate(output_blocks, axis=0).reshape(rows_here, head_width).astype(jnp.bfloat16)
    )
    attended_full = spread(attended)
    middle = token_values + jnp.dot(attended_full, out_full, preferred_element_type=jnp.float32)
    scaled_two, inverse_two = norm_forward(middle, full_width)
    normed_two_full = spread((scaled_two * gain_two).astype(jnp.bfloat16))
    gate_up = jnp.einsum(
        "td,dsf->tsf", normed_two_full, in_full, preferred_element_type=jnp.float32
    )
    hidden_value, geglu_pull = jax.vjp(geglu, gate_up)
    hidden_full = spread(hidden_value.astype(jnp.bfloat16))
    mixed = (middle + jnp.dot(hidden_full, down_full, preferred_element_type=jnp.float32)).astype(
        jnp.bfloat16
    )
    qkv_back, out_back, in_back, down_back = (
        lax.all_gather(qkv_weight, "row", axis=0, tiled=True),
        lax.all_gather(out_weight, "row", axis=0, tiled=True),
        lax.all_gather(in_weight, "row", axis=0, tiled=True),
        lax.all_gather(down_weight, "row", axis=0, tiled=True),
    )
    down_part = jnp.einsum("tf,td->fd", hidden_full, grad_rows, preferred_element_type=jnp.float32)
    hidden_grad = collect(
        jnp.einsum("td,fd->tf", grad_rows, down_back, preferred_element_type=jnp.float32)
    )
    gate_up_grad = geglu_pull(hidden_grad)[0].astype(jnp.bfloat16)
    in_part = jnp.einsum(
        "td,tsf->dsf", normed_two_full, gate_up_grad, preferred_element_type=jnp.float32
    )
    normed_two_grad = collect(
        jnp.einsum("tsf,dsf->td", gate_up_grad, in_back, preferred_element_type=jnp.float32)
    )
    middle_norm_grad, gain_two_part = norm_backward(
        normed_two_grad, scaled_two, inverse_two, gain_two, full_width
    )
    middle_grad = grad_rows.astype(jnp.float32) + middle_norm_grad
    branch_grad = middle_grad.astype(jnp.bfloat16)
    out_part = jnp.einsum(
        "td,tf->df", attended_full, branch_grad, preferred_element_type=jnp.float32
    )
    attended_grad = collect(
        jnp.einsum("tf,df->td", branch_grad, out_back, preferred_element_type=jnp.float32)
    ).astype(jnp.bfloat16)
    attended_heads = attended_grad.reshape(rows_here, heads_here, HEAD_DIM)
    query_blocks = []
    key_grad_ext = jnp.zeros((rows_here + 2 * half_window, heads_here, HEAD_DIM), jnp.float32)
    value_grad_ext = jnp.zeros((rows_here + 2 * half_window, heads_here, HEAD_DIM), jnp.float32)
    for block_number in range(block_count):
        block_start = block_number * block_rows
        block_queries = queries[block_start : block_start + block_rows]
        block_keys = padded_keys[block_start : block_start + key_span]
        block_values = padded_values[block_start : block_start + key_span]
        block_grads = attended_heads[block_start : block_start + block_rows]
        masked = block_scores(block_start, block_queries, block_keys)
        probs = jnp.exp(masked - total_blocks[block_number])
        prob_grad = jnp.einsum(
            "qhd,khd->hqk", block_grads, block_values, preferred_element_type=jnp.float32
        )
        inner = jnp.sum(probs * prob_grad, axis=-1, keepdims=True)
        score_grad = (probs * (prob_grad - inner)).astype(jnp.bfloat16)
        query_blocks.append(
            jnp.einsum("hqk,khd->qhd", score_grad, block_keys, preferred_element_type=jnp.float32)
            * score_scale
        )
        key_grad_ext = key_grad_ext.at[block_start : block_start + key_span].add(
            jnp.einsum(
                "hqk,qhd->khd", score_grad, block_queries, preferred_element_type=jnp.float32
            )
            * score_scale
        )
        value_grad_ext = value_grad_ext.at[block_start : block_start + key_span].add(
            jnp.einsum(
                "hqk,qhd->khd",
                probs.astype(jnp.bfloat16),
                block_grads,
                preferred_element_type=jnp.float32,
            )
        )
    grad_pair = jnp.concatenate(
        [key_grad_ext.reshape(-1, head_width), value_grad_ext.reshape(-1, head_width)], axis=1
    )
    rim_rows = jnp.concatenate(
        [grad_pair[:half_window], grad_pair[rows_here + half_window :]], axis=0
    )
    beside_all = with_halo(rim_rows.astype(jnp.bfloat16), (("row", 0),), half_window).astype(
        rim_rows.dtype
    )
    own_grad = grad_pair[half_window : half_window + rows_here]
    own_grad = own_grad.at[:half_window].add(beside_all[:half_window])
    own_grad = own_grad.at[rows_here - half_window :].add(beside_all[3 * half_window :])
    key_grad = own_grad[:, :head_width].reshape(rows_here, heads_here, HEAD_DIM)
    value_grad = own_grad[:, head_width:].reshape(rows_here, heads_here, HEAD_DIM)
    query_grad = jnp.concatenate(query_blocks, axis=0)
    projected_grad = jnp.stack(
        [
            rotate_back(query_grad, cosine, sine_table),
            rotate_back(key_grad, cosine, sine_table),
            value_grad,
        ],
        axis=1,
    )
    projected_grad = projected_grad.reshape(rows_here, 3, head_width).astype(jnp.bfloat16)
    qkv_part = jnp.einsum(
        "td,tsf->dsf", normed_one_full, projected_grad, preferred_element_type=jnp.float32
    )
    normed_one_grad = collect(
        jnp.einsum("tsf,dsf->td", projected_grad, qkv_back, preferred_element_type=jnp.float32)
    )
    token_norm_grad, gain_one_part = norm_backward(
        normed_one_grad, scaled_one, inverse_one, gain_one, full_width
    )
    input_grad = middle_grad + token_norm_grad
    weight_grads = (
        lax.psum_scatter(qkv_part, "row", scatter_dimension=0, tiled=True),
        lax.psum_scatter(out_part, "row", scatter_dimension=0, tiled=True),
        lax.psum_scatter(in_part, "row", scatter_dimension=0, tiled=True),
        lax.psum_scatter(down_part, "row", scatter_dimension=0, tiled=True),
    )
    gain_grads = lax.psum((gain_one_part, gain_two_part), "row")
    mixed_out = mixed.reshape(1, pair_rows, 2 * tok_width)
    input_out = input_grad.reshape(1, pair_rows, 2 * tok_width)
    return (
        mixed_out,
        input_out,
        gain_grads[0],
        weight_grads[0],
        weight_grads[1],
        gain_grads[1],
        weight_grads[2],
        weight_grads[3],
    )


F32 = jnp.float32
BF = jnp.bfloat16
MESH = pl.DeviceIdType.MESH
ROWS = (96, 96, 144)
COLS = (768, 512, 256)
SPLIT = (48, 48, 64)
OWN = 256
EXT = 384
HALF = 64


def dot(a, b):
    return lax.dot_general(a, b, (((1,), (0,)), ((), ())), preferred_element_type=F32)


def dot_nt(a, b):
    return lax.dot_general(a, b, (((1,), (1,)), ((), ())), preferred_element_type=F32)


def dot_tn(a, b):
    return lax.dot_general(a, b, (((0,), (0,)), ((), ())), preferred_element_type=F32)


class Link:
    def __init__(self, way, src, dst, recv, row, col, when=None):
        self.way, self.src, self.dst, self.recv = way, src, dst, recv
        self.device = {"row": row, "col": col}
        self.when = when
        self.send = None

    def run(self, step):
        def body():
            copy = pltpu.make_async_remote_copy(
                src_ref=self.src,
                dst_ref=self.dst,
                send_sem=self.send,
                recv_sem=self.recv,
                device_id=self.device,
                device_id_type=MESH,
            )
            step(copy)

        if self.when is None:
            body()
        else:
            pl.when(self.when)(body)


class Ways:
    def __init__(self, **rings):
        self.rings = rings
        self.used = {way: [] for way in rings}

    def go(self, link):
        used, ring = self.used[link.way], self.rings[link.way]
        slot = len(used) % ring.shape[0]
        if len(used) >= ring.shape[0]:
            used[-ring.shape[0]].run(lambda copy: copy.wait_send())
        link.send = ring.at[slot]
        used.append(link)
        link.run(lambda copy: copy.start())

    def drain(self):
        for way, ring in self.rings.items():
            for link in self.used[way][-ring.shape[0] :]:
                link.run(lambda copy: copy.wait_send())


def arrived(ref, recv, row, col):
    pltpu.make_async_remote_copy(
        src_ref=ref,
        dst_ref=ref,
        send_sem=recv,
        recv_sem=recv,
        device_id={"row": row, "col": col},
        device_id_type=MESH,
    ).wait_recv()


def at_rows(ref, lead, start, size):
    return ref.at[lead, pl.ds(start, size), :]


def lane_iota(shape):
    return lax.broadcasted_iota(jnp.int32, shape, 1)


def swap_halves(tile):
    first = (lane_iota(tile.shape) % 64) < 32
    return jnp.where(first, pltpu.roll(tile, 96, 1), pltpu.roll(tile, 32, 1))


def layer_kernel(
    tok_in, cot_in, qkv_in, out_in, in_in, down_in, gain_one_in, gain_two_in, ids_in, freq_in,
    mixed_out, input_out, qkv_out, out_out, in_out, down_out, gain_one_out, gain_two_out,
    tok_ext, got_x, got_g, got_gain, w1, w2, w3, d1, d2, d3,
    core1, core2, core3, xa1, xa2, xa3, xb1, xb2, xb3, ya1, ya2, ya3, yb1, yb2, yb3,
    zb1, zb2, zb3,
    gains_in, own_ids, x_all, cos_t, sin_t, bias, n1, hat1, stat, qs, ks, vs, probs, att_c, att, mid, hat2, n2,
    tail_in, tail_down, hid, hid_tail, gel, gel_up, gel_t, gel_up_t, cot_pad, d_gate, d_tail,
    branch_pad, att_grad, d_proj,
    halo_out, halo_left, halo_right, mixed_send, mixed_got, input_send, input_got,
    relay_tok, relay_cot, relay_mixed, relay_input, gain_part, gain_z, gain_sum, gain_all, grad_one, grad_two, grad_three,
    way_x, way_y, way_z, way_c, io,
    hop_r, tok_r, tok_rl, tok_rr, cot_r, gn_r, az_r, ax_r, ay_r, al_r, ac_r,
    rc_r, rx_r, ry_r, rl_r, rz_r, ha_r, mx_r, ig_r, gz_r, gp_r,
    *, start_of,
):
    row = lax.axis_index("row")
    z = lax.axis_index("col")
    core = row % 2
    xc = (row // 2) % 2
    yc = row // 4
    rx = row + 2 - 4 * xc
    ry = row + 4 - 8 * yc
    rxy = ry + 2 - 4 * xc
    rc = row + 1 - 2 * core
    ws = (w1, w2, w3)
    ds_ = (d1, d2, d3)
    n1_grad, mid_grad = x_all.at[pl.ds(0, OWN), :], hat2
    ways = Ways(x=way_x, y=way_y, z=way_z, c=way_c)
    go = ways.go

    barrier = pltpu.get_barrier_semaphore()

    def greet(r, c):
        pl.semaphore_signal(barrier, inc=1, device_id={"row": r, "col": c}, device_id_type=MESH)

    for step in range(1, 8):
        greet((row + step) % 8, z)
    for step in range(1, 4):
        greet(row, (z + step) % 4)
    up, down = row < 7, row > 0
    low_end, high_end = (z == 0) & down, (z == 3) & up
    pl.when(low_end)(lambda: greet(row - 1, 3))
    pl.when(high_end)(lambda: greet(row + 1, 0))
    peers = 10 + jnp.maximum(1 - z, 0) * jnp.minimum(row, 1)
    peers += jnp.maximum(z - 2, 0) * jnp.minimum(7 - row, 1)

    def own_tokens(step):
        step(pltpu.make_async_copy(tok_in, tok_ext.at[pl.ds(32, 512), :], io.at[0]))
        step(pltpu.make_async_copy(lines(cot_in, z), got_g.at[z], io.at[1]))

    def send_edges():
        go(Link("x", tok_in.at[pl.ds(0, 32), :], tok_ext.at[pl.ds(544, 32), :], tok_rr.at[0],
                row - 1, z, down))
        go(Link("y", tok_in.at[pl.ds(480, 32), :], tok_ext.at[pl.ds(0, 32), :], tok_rl.at[0],
                row + 1, z, up))
        for step in range(1, 4):
            go(Link("z", gains_in, got_gain.at[z], gn_r.at[0], row, (z + step) % 4))

    def take_edges():
        own_tokens(lambda copy: copy.wait())

        @pl.when(down)
        def _():
            arrived(tok_ext.at[pl.ds(0, 32), :], tok_rl.at[0], row - 1, z)

        @pl.when(up)
        def _():
            arrived(tok_ext.at[pl.ds(544, 32), :], tok_rr.at[0], row + 1, z)

        @pl.when(row == 0)
        def _():
            tok_ext[0:32, :] = jnp.zeros((32, 384), BF)

        @pl.when(row == 7)
        def _():
            tok_ext[544:576, :] = jnp.zeros((32, 384), BF)

    def window(c):
        return tok_ext.at[pl.ds(pl.multiple_of(c * 128, 128), 192), :]

    slots = {(2, 1): 0, (3, 1): 1, (3, 2): 2}

    def hop(kind, relay, first, last, recv_last, d, k):
        for way, sign in enumerate((1, -1)):
            s, c = z - sign * k, z - sign * k + sign * d
            sends = (s >= 0) & (c <= 3) if sign == 1 else (s <= 3) & (c >= 0)
            src = first(jnp.clip(c, 0, 3))
            if k > 0:
                slot = slots[d, k]
                src = relay.at[way, slot]
                pl.when(sends)(
                    lambda: arrived(relay.at[way, slot], hop_r.at[kind, way, slot], row, z))
            if k == d - 1:
                dst, recv = last(jnp.clip(s, 0, 3)), recv_last.at[0]
            else:
                slot_on = slots[d, k + 1]
                dst, recv = relay.at[way, slot_on], hop_r.at[kind, way, slot_on]
            go(Link("z", src, dst, recv, row, z + sign, sends))

    def lines(ref, c):
        return ref.at[pl.ds(pl.multiple_of(c * 128, 128), 128), :]

    def hop_tok(d, k):
        hop(0, relay_tok, window, lambda s: got_x.at[s], tok_r, d, k)

    def hop_cot(d, k):
        hop(1, relay_cot, lambda c: lines(cot_in, c), lambda s: got_g.at[s], cot_r, d, k)

    def hop_mixed(d, k):
        hop(2, relay_mixed, lambda c: mixed_send.at[c], lambda s: lines(mixed_got, s), mx_r, d, k)

    def hop_input(d, k):
        hop(3, relay_input, lambda c: input_send.at[c], lambda s: lines(input_got, s), ig_r, d, k)

    def send_gain():
        for step in range(1, 4):
            c = (z + step) % 4
            go(Link("z", gain_sum.at[c], gain_z.at[z], gz_r.at[0], row, c))

    order = (z, 1 + z % 2, 2 - 2 * (z % 2) + z // 2, 3 - 3 * (z // 2))

    def near(i, c, r, part):
        size, cut = ROWS[i], SPLIT[i]
        start, count = {"all": (0, size), "a": (0, cut), "b": (cut, size - cut)}[part]
        return at_rows(ws[i], c, pl.multiple_of(r * size + start, 16), count)

    def gather_link(way, i, c, r, part, recv, to_row, to_col, when=None):
        ref = near(i, c, r, part)
        go(Link(way, ref, ref, recv, to_row, to_col, when))

    def gather_z(i, j):
        c = order[j]
        if j > 0:
            arrived(near(i, c, row, "all"), az_r.at[i, c], row, z)
        right = z < 3 if j == 0 else (c < z) & (z < 3)
        left = z > 0 if j == 0 else (c > z) & (z > 0)
        gather_link("z", i, c, row, "all", az_r.at[i, c], row, z + 1, right)
        gather_link("z", i, c, row, "all", az_r.at[i, c], row, z - 1, left)

    def gather_xy(i, j):
        c = order[j]
        gather_link("x", i, c, row, "a", ax_r.at[i, c], rx, z)
        gather_link("y", i, c, row, "b", ay_r.at[i, c], ry, z)
        gather_link("x", i, c, row, "b", al_r.at[i, c], rx, z)
        gather_link("y", i, c, row, "a", al_r.at[i, c], ry, z)
        gather_link("c", i, c, row, "all", ac_r.at[i, c], rc, z)

    def gather_second_x(i, j):
        c = order[j]
        arrived(near(i, c, rx, "a"), ax_r.at[i, c], rx, z)
        gather_link("y", i, c, rx, "a", al_r.at[i, c], ry, z)

    def gather_second_y(i, j):
        c = order[j]
        arrived(near(i, c, ry, "b"), ay_r.at[i, c], ry, z)
        gather_link("x", i, c, ry, "b", al_r.at[i, c], rx, z)

    def first_rows(i, c, count):
        return ws[i].at[c, pl.ds(0, count), :]

    def gather_third(i, j):
        c = order[j]
        arrived(first_rows(i, c, 2 * ROWS[i]), al_r.at[i, c], rx, z)
        for r in (rx, ry, rxy):
            gather_link("c", i, c, r, "all", ac_r.at[i, c], rc, z)

    def gather_done(i, j):
        c = order[j]
        arrived(first_rows(i, c, 4 * ROWS[i]), ac_r.at[i, c], rc, z)

    def pack_own():
        r96 = pl.ds(pl.multiple_of(row * 96, 16), 96)
        r144 = pl.ds(pl.multiple_of(row * 144, 16), 144)
        q, k, v = qkv_in[0], qkv_in[1], qkv_in[2]
        gate, other = in_in[:, 0, :], in_in[:, 1, :]
        w1[z, r96, :] = jnp.concatenate(
            [q[:, :128], k[:, :128], v[:, :128], q[:, 128:], k[:, 128:], v[:, 128:],
             out_in[...]], axis=1)
        w2[z, r96, :] = jnp.concatenate([gate[:, :256], other[:, :256]], axis=1)
        tail = jnp.concatenate([gate[:, 256:], other[:, 256:]], axis=1)
        tail = jnp.concatenate([tail, jnp.zeros((48, 64), BF)], axis=0)
        w3[z, r144, :] = jnp.concatenate([down_in[...], tail], axis=1)
        gains_in[...] = jnp.zeros((8, 256), F32)
        gains_in[0:1, 0:192] = gain_one_in[...].reshape(1, 192)
        gains_in[1:2, 0:192] = gain_two_in[...].reshape(1, 192)

    def take_tokens():
        got_x[z] = window(z)[...]
        arrived(got_x.at[pl.ds(0, 3)], tok_r.at[0], row, z)
        got_gain[pl.ds(z, 1)] = gains_in[...][None]
        arrived(got_gain.at[pl.ds(0, 3)], gn_r.at[0], row, z)
        at = 0
        for low, high, lane in ((32, 160, 0), (32, 160, 192), (0, 32, 0), (0, 32, 192),
                                (160, 192, 0), (160, 192, 192)):
            x_all[at : at + high - low, :] = jnp.concatenate(
                [got_x[c, low:high, lane : lane + 192].astype(F32) for c in range(4)], axis=1)
            at += high - low

    def gain_row(which):
        return jnp.concatenate([got_gain[c, which : which + 1, 0:192] for c in range(4)], axis=1)

    def window_ids(first, length):
        last = ids_in.shape[0] - 1
        spot = first // 128
        near_rows = [ids_in[pl.ds(jnp.clip(spot + n, 0, last), 1), :] for n in range(-1, 3)]
        base = near_rows[1][0:1, 0:1]
        rel = jnp.concatenate(near_rows, axis=0) - base
        rel = jnp.clip(rel, -200, 200).astype(BF)
        source = lax.broadcasted_iota(jnp.int32, (128, 128), 0)
        target = lane_iota((128, 128))
        pick = (source == jnp.where(target < 64, 2 * target, 2 * target - 127)).astype(BF)
        rel = jnp.concatenate([rel, jnp.zeros((4, 128), BF)], axis=0)
        rel = dot(rel, pick)
        keys = jnp.concatenate(
            [rel[1:2, :64], rel[2:3, :64], rel[1:2, 64:], rel[2:3, 64:], rel[0:1, 32:64],
             rel[0:1, 96:], rel[3:4, :32], rel[3:4, 64:96]], axis=1)
        lane = lane_iota((1, EXT))
        lost = (lane >= 256) & (lane < 320) & (first % length == 0)
        lost |= (lane >= 320) & ((first + OWN) % length == 0)
        keys = jnp.where(lost, 1000.0, keys)
        own_ids[...] = jnp.broadcast_to(keys[:, :OWN], (8, OWN))
        return keys, own_ids[...].T[:, 0:1]

    def tables():
        spot = lax.broadcasted_iota(jnp.int32, (EXT, 128), 0)
        halo = spot - 256
        place = jnp.where(
            spot < 128, 2 * spot, jnp.where(
                spot < 256, 2 * spot - 255, jnp.where(
                    halo < 32, 2 * halo - 64, jnp.where(
                        halo < 64, 2 * halo - 127, jnp.where(
                            halo < 96, 2 * halo + 128, 2 * halo + 65)))))
        first, length = start_of(row, z)
        place = (place + first + length) % length
        angle = place.astype(F32) * freq_in[0:1, :]
        cos_t[...] = jnp.cos(angle)
        turn = jnp.where((lane_iota((EXT, 128)) % 64) < 32, -1.0, 1.0)
        sin_t[...] = jnp.sin(angle) * turn
        key_ids, query_ids = window_ids(first, length)
        qrow = lax.broadcasted_iota(jnp.int32, (OWN, EXT), 0)
        qplace = jnp.where(qrow < 128, 2 * qrow, 2 * qrow - 255)
        kcol = lane_iota((OWN, EXT))
        khalo = kcol - 256
        kplace = jnp.where(
            kcol < 128, 2 * kcol, jnp.where(
                kcol < 256, 2 * kcol - 255, jnp.where(
                    khalo < 32, 2 * khalo - 64, jnp.where(
                        khalo < 64, 2 * khalo - 127, jnp.where(
                            khalo < 96, 2 * khalo + 128, 2 * khalo + 65)))))
        allowed = (jnp.abs(qplace - kplace) <= HALF) & (query_ids == key_ids)
        bias[...] = jnp.where(allowed, 0.0, -1e30)

    def statistics(v):
        mu = jnp.mean(v, axis=1, keepdims=True)
        inv = lax.rsqrt(jnp.mean(v * v, axis=1, keepdims=True) - mu * mu + EPSILON)
        return (v - mu) * inv, inv

    def norm_one():
        hat, inv = statistics(x_all[0:OWN, :])
        hat1[...] = hat
        stat[0] = jnp.broadcast_to(inv, (OWN, 128))
        gain = gain_row(0)
        n1[0:OWN, :] = (hat * gain).astype(BF)
        hat, _ = statistics(x_all[OWN:EXT, :])
        n1[OWN:EXT, :] = (hat * gain).astype(BF)

    def take_cotangent():
        arrived(got_g.at[pl.ds(0, 3)], cot_r.at[0], row, z)
        pad = jnp.zeros((128, 64), BF)
        for c in range(4):
            for odd in range(2):
                cot_pad[128 * odd : 128 * odd + 128, 256 * c : 256 * c + 256] = jnp.concatenate(
                    [got_g[c, :, 192 * odd : 192 * odd + 192], pad], axis=1)

    low_lanes = lambda shape: lane_iota(shape) < 64

    def forward_heads(j):
        c = order[j]
        proj = dot(n1[...], w1[c, :, 0:640])
        cos, sin = cos_t[...], sin_t[...]
        rot = lambda tile, n: tile * cos[0:n] + swap_halves(tile) * sin[0:n]
        qs[c, 0] = (rot(proj[0:OWN, 0:128], OWN) * 0.125).astype(BF)
        ks[c, 0] = rot(proj[:, 128:256], EXT).astype(BF)
        vs[c, 0] = proj[:, 256:384].astype(BF)
        third = rot(proj[:, 384:512], EXT)
        low = low_lanes((EXT, 128))
        qs[c, 1] = jnp.where(low[0:OWN], third[0:OWN] * 0.125, 0.0).astype(BF)
        ks[c, 1] = jnp.where(low, pltpu.roll(third, 64, 1), 0.0).astype(BF)
        vs[c, 1] = jnp.where(low, proj[:, 512:640], 0.0).astype(BF)

        def head(h, q, k):
            scores = dot_nt(q, k) + bias[...]
            weight = jnp.exp(scores - jnp.max(scores, axis=1, keepdims=True))
            weight = weight * (1.0 / jnp.sum(weight, axis=1, keepdims=True))
            probs[3 * c + h] = weight
            return weight.astype(BF)

        zero = jnp.zeros((), BF)
        lowq, lowk = low_lanes((OWN, 128)), low
        q, k, v = qs[c, 0], ks[c, 0], vs[c, 0]
        both = dot(head(0, jnp.where(lowq, q, zero), k), jnp.where(lowk, v, zero))
        both += dot(head(1, jnp.where(lowq, zero, q), k), jnp.where(lowk, zero, v))
        att_c[c, :, 0:128] = both.astype(BF)
        att_c[c, :, 128:256] = dot(head(2, qs[c, 1], ks[c, 1]), vs[c, 1]).astype(BF)

    def forward_middle():
        for c in range(4):
            att[:, 192 * c : 192 * c + 192] = att_c[c, :, 0:192]
        for c in range(4):
            out = dot(att[...], w1[c, :, 512:768])
            mid[:, 192 * c : 192 * c + 192] = (
                x_all[0:OWN, 192 * c : 192 * c + 192] + out[:, 64:256])
        hat, inv = statistics(mid[...])
        hat2[...] = hat
        stat[1] = jnp.broadcast_to(inv, (OWN, 128))
        n2[...] = (hat * gain_row(1)).astype(BF)

    def gelu_parts(g):
        phi = 0.5 * (1.0 + lax.erf(g * 0.7071067811865476))
        return g * phi, phi + g * (jnp.exp(g * g * -0.5) * 0.3989422804014327)

    def forward_hidden(j):
        c = order[j]
        both = dot(n2[...], w2[c])
        value, slope = gelu_parts(both[:, 0:256])
        other = both[:, 256:512]
        gel[c] = value
        gel_up[c] = other * slope
        hid[c] = (value * other).astype(BF)

    def forward_tail():
        for c in range(4):
            for r in range(8):
                tail_in[96 * r : 96 * r + 96, 128 * c : 128 * c + 128] = (
                    w3[c, 144 * r : 144 * r + 96, 128:256])
                if r < 4:
                    tail_down[c, 32 * r : 32 * r + 32, :] = (
                        w3[c, 288 * r + 256 : 288 * r + 288, :])
        tails = dot(n2[...], tail_in[...])
        lanes = lane_iota((OWN, 128)) // 32
        packed = jnp.zeros((OWN, 128), F32)
        for c in range(4):
            tile = tails[:, 128 * c : 128 * c + 128]
            value, slope = gelu_parts(tile)
            other = pltpu.roll(tile, 96, 1)
            gel_t[c] = value
            gel_up_t[c] = other * slope
            moved = pltpu.roll(value * other, (32 * c + 64) % 128, 1)
            packed = jnp.where(lanes == c, moved, packed)
        hid_tail[...] = packed.astype(BF)

    def forward_mixed():
        for k in range(4):
            total = dot(hid_tail[...], tail_down[k])
            for c in range(4):
                total += dot(hid[c], w3[k, 288 * c : 288 * c + 256, :])
            out = (mid[:, 192 * k : 192 * k + 192] + total[:, 0:192]).astype(BF)
            mixed_send[k] = jnp.concatenate([out[0:128], out[128:256]], axis=1)

    def hidden_rows(c):
        return pl.ds(pl.multiple_of(c * 288, 16), 256)

    def backward_hidden(j):
        c = order[j]
        grad = dot_nt(cot_pad[:, 0:256], w3[0, hidden_rows(c), :])
        for k in range(1, 4):
            grad += dot_nt(cot_pad[:, 256 * k : 256 * k + 256], w3[k, hidden_rows(c), :])
        d_gate[c] = jnp.concatenate([grad * gel_up[c], grad * gel[c]], axis=1).astype(BF)

    def backward_tail():
        grad = dot_nt(cot_pad[:, 0:256], tail_down[0])
        for k in range(1, 4):
            grad += dot_nt(cot_pad[:, 256 * k : 256 * k + 256], tail_down[k])
        lanes = lane_iota((OWN, 128))
        for c in range(4):
            gate = pltpu.roll(grad, (64 - 32 * c) % 128, 1) * gel_up_t[c]
            other = pltpu.roll(grad, (96 - 32 * c) % 128, 1) * pltpu.roll(gel_t[c], 32, 1)
            d_tail[:, 128 * c : 128 * c + 128] = jnp.where(
                lanes >= 96, other, jnp.where(lanes >= 64, gate, 0.0)).astype(BF)

    def grad_down(j):
        c = order[j]
        part = dot_tn(hid[c], cot_pad[...]).astype(BF)
        for k in range(4):
            d3[k, hidden_rows(c), :] = part[:, 256 * k : 256 * k + 256]

    def grad_tail():
        part = dot_tn(hid_tail[...], cot_pad[...]).astype(BF)
        for c in range(4):
            for k in range(4):
                d3[k, 288 * c + 256 : 288 * c + 288, :] = (
                    part[32 * c : 32 * c + 32, 256 * k : 256 * k + 256])
        part = dot_tn(n2[...], d_tail[...]).astype(BF)
        for c in range(4):
            for r in range(8):
                d3[c, 144 * r : 144 * r + 96, 128:256] = (
                    d3[c, 144 * r : 144 * r + 96, 128:256]
                    + part[96 * r : 96 * r + 96, 128 * c : 128 * c + 128])

    def grad_in(j):
        c = order[3 - j]
        d2[c] = dot_tn(n2[...], d_gate[c]).astype(BF)

    def norm_back(grad, hat, inv, gain):
        e = grad * gain
        return inv * (e - jnp.mean(e, axis=1, keepdims=True)
                      - hat * jnp.mean(e * hat, axis=1, keepdims=True))

    def backward_middle():
        grad = dot_nt(d_tail[...], tail_in[...])
        for c in range(4):
            grad += dot_nt(d_gate[c], w2[c])
        hat = hat2[...]
        gain_part[1:2, :] = jnp.sum(grad * hat, axis=0, keepdims=True)
        back = norm_back(grad, hat, stat[1][:, 0:1], gain_row(1))
        pad = jnp.zeros((OWN, 64), BF)
        total = jnp.concatenate(
            [cot_pad[:, 256 * c : 256 * c + 192].astype(F32) for c in range(4)], axis=1) + back
        mid_grad[...] = total
        branch = total.astype(BF)
        for c in range(4):
            branch_pad[:, 256 * c : 256 * c + 256] = jnp.concatenate(
                [pad, branch[:, 192 * c : 192 * c + 192]], axis=1)
        grad = dot_nt(branch_pad[:, 0:256], w1[0, :, 512:768])
        for c in range(1, 4):
            grad += dot_nt(branch_pad[:, 256 * c : 256 * c + 256], w1[c, :, 512:768])
        grad = grad.astype(BF)
        for c in range(4):
            att_grad[c] = jnp.concatenate([grad[:, 192 * c : 192 * c + 192], pad], axis=1)

    def grad_out():
        part = dot_tn(att[...], branch_pad[...]).astype(BF)
        for c in range(4):
            d1[c, :, 512:768] = part[:, 256 * c : 256 * c + 256]

    def backward_heads(j):
        c = order[3 - j]
        zero = jnp.zeros((), BF)
        lowq, lowk = low_lanes((OWN, 128)), low_lanes((EXT, 128))

        def head(h, g, v):
            weight = probs[3 * c + h]
            prob_grad = dot_nt(g, v)
            inner = jnp.sum(weight * prob_grad, axis=1, keepdims=True)
            return (weight * (prob_grad - inner)).astype(BF), weight.astype(BF)

        q, k, v = qs[c, 0], ks[c, 0], vs[c, 0]
        g = att_grad[c, :, 0:128]
        g0, g1 = jnp.where(lowq, g, zero), jnp.where(lowq, zero, g)
        s0, p0 = head(0, g0, v)
        s1, p1 = head(1, g1, v)
        dq = dot(s0, jnp.where(lowk, k, zero)) + dot(s1, jnp.where(lowk, zero, k))
        dk = dot_tn(s0, jnp.where(lowq, q, zero)) + dot_tn(s1, jnp.where(lowq, zero, q))
        dv = dot_tn(p0, g0) + dot_tn(p1, g1)
        g2 = att_grad[c, :, 128:256]
        s2, p2 = head(2, g2, vs[c, 1])
        dq2 = dot(s2, ks[c, 1]) * 0.125
        dk2 = pltpu.roll(dot_tn(s2, qs[c, 1]), 64, 1)
        dv2 = dot_tn(p2, g2)
        cos, sin = cos_t[...], sin_t[...]
        back = lambda tile: tile * cos - swap_halves(tile) * sin
        none = jnp.zeros((EXT - OWN, 128), F32)
        dq = jnp.concatenate([dq * 0.125, none], axis=0)
        d_proj[c, :, 0:128] = back(dq).astype(BF)
        d_proj[c, :, 128:256] = back(dk).astype(BF)
        d_proj[c, :, 256:384] = dv.astype(BF)
        d_proj[c, :, 384:512] = back(jnp.concatenate([dq2, none], axis=0) + dk2).astype(BF)
        d_proj[c, :, 512:640] = dv2.astype(BF)

    def grad_qkv(j):
        c = order[3 - j]
        part = dot_tn(n1[...], d_proj[c]).astype(BF)
        d1[c, :, 0:512] = part[:, 0:512]
        d1[c, :, 512:640] = d1[c, :, 512:640] + part[:, 512:640]

    def backward_first():
        grad = dot_nt(d_proj[0], w1[0, :, 0:640])
        for c in range(1, 4):
            grad += dot_nt(d_proj[c], w1[c, :, 0:640])
        n1_grad[...] = grad[0:OWN]
        halo_out[...] = grad[OWN:EXT].astype(BF)

    edge_low, edge_high = (z == 0) & (row == 0), (z == 3) & (row == 7)
    left_row = jnp.where(z == 0, row - 1, row)
    right_row = jnp.where(z == 3, row + 1, row)
    left_col, right_col = (z + 3) % 4, (z + 1) % 4

    def halo_send():
        go(Link("z", halo_out.at[pl.ds(0, 64), :], halo_right, ha_r.at[1], left_row, left_col, jnp.logical_not(edge_low)))
        go(Link("z", halo_out.at[pl.ds(64, 64), :], halo_left, ha_r.at[0], right_row, right_col, jnp.logical_not(edge_high)))

    def halo_take():
        @pl.when(jnp.logical_not(edge_low))
        def _():
            arrived(halo_left, ha_r.at[0], left_row, left_col)
            n1_grad[0:32, :] += halo_left[0:32, :].astype(F32)
            n1_grad[128:160, :] += halo_left[32:64, :].astype(F32)

        @pl.when(jnp.logical_not(edge_high))
        def _():
            arrived(halo_right, ha_r.at[1], right_row, right_col)
            n1_grad[96:128, :] += halo_right[0:32, :].astype(F32)
            n1_grad[224:256, :] += halo_right[32:64, :].astype(F32)

    def backward_last():
        grad, hat = n1_grad[...], hat1[...]
        gain_part[0:1, :] = jnp.sum(grad * hat, axis=0, keepdims=True)
        total = mid_grad[...] + norm_back(grad, hat, stat[0][:, 0:1], gain_row(0))
        out = total.astype(BF)
        for k in range(4):
            mine = out[:, 192 * k : 192 * k + 192]
            input_send[k] = jnp.concatenate([mine[0:128], mine[128:256]], axis=1)
        for c in range(4):
            gain_part_c = gain_part[0:2, 192 * c : 192 * c + 192]
            gain_sum[c, 0:2, 0:192] = gain_part_c

    cores = (core1, core2, core3)
    xas, xbs, yas, ybs = (xa1, xa2, xa3), (xb1, xb2, xb3), (ya1, ya2, ya3), (yb1, yb2, yb3)
    zbs = (zb1, zb2, zb3)
    outs = (grad_one, grad_two, grad_three)

    def unpack_outs():
        one, two, three = grad_one[...], grad_two[...], grad_three[...]
        for n in range(3):
            qkv_out[n] = jnp.concatenate(
                [one[:, 128 * n : 128 * n + 128], one[:, 384 + 64 * n : 448 + 64 * n]], axis=1)
        out_out[...] = one[:, 576:768]
        for n in range(2):
            in_out[:, n, :] = jnp.concatenate(
                [two[:, 256 * n : 256 * n + 256], three[0:96, 192 + 32 * n : 224 + 32 * n]],
                axis=1)
        down_out[...] = three[:, 0:192]


    def place(i, c, r, part):
        size, cut = ROWS[i], SPLIT[i]
        start, count = {"all": (0, size), "a": (0, cut), "b": (cut, size - cut)}[part]
        return c, pl.ds(pl.multiple_of(r * size + start, 16), count)

    def piece(i, c, r, part):
        lead, span = place(i, c, r, part)
        return ds_[i].at[lead, span, :]

    def add_into(i, c, r, part, value):
        lead, span = place(i, c, r, part)
        ds_[i][lead, span, :] = ds_[i][lead, span, :] + value

    def sum_first(i, j):
        c = order[3 - j]
        for n in range(4):
            go(Link("c", piece(i, c, 2 * n + 1 - core, "all"), cores[i].at[c, n], rc_r.at[i, c],
                    rc, z))

    def sum_second(i, j):
        c = order[3 - j]
        arrived(cores[i].at[c], rc_r.at[i, c], rc, z)

        def take(n):
            add_into(i, c, 2 * n + core, "all", cores[i][c, n])

        for y in range(2):
            take(2 * y + 1 - xc)
            go(Link("x", piece(i, c, 4 * y + 2 * (1 - xc) + core, "a"), xas[i].at[c, y],
                    rx_r.at[i, c], rx, z))
        take(2 * (1 - yc) + xc)
        for x in range(2):
            go(Link("y", piece(i, c, 4 * (1 - yc) + 2 * x + core, "b"), ybs[i].at[c, x],
                    ry_r.at[i, c], ry, z))
        take(2 * yc + xc)

    def sum_third_x(i, j):
        c = order[3 - j]
        arrived(xas[i].at[c], rx_r.at[i, c], rx, z)
        add_into(i, c, ry, "a", xas[i][c, 1 - yc])
        go(Link("y", piece(i, c, ry, "a"), yas[i].at[c], rl_r.at[i, c], ry, z))
        add_into(i, c, row, "a", xas[i][c, yc])

    def sum_third_y(i, j):
        c = order[3 - j]
        arrived(ybs[i].at[c], ry_r.at[i, c], ry, z)
        add_into(i, c, rx, "b", ybs[i][c, 1 - xc])
        go(Link("x", piece(i, c, rx, "b"), xbs[i].at[c], rl_r.at[i, c], rx, z))
        add_into(i, c, row, "b", ybs[i][c, xc])

    def sum_fourth(i, j):
        c = order[3 - j]
        arrived(zbs[i].at[c], rl_r.at[i, c], ry, z)
        add_into(i, c, row, "a", yas[i][c])
        add_into(i, c, row, "b", xbs[i][c])

        @pl.when(((c > z) & (z > 0)) | ((c < z) & (z < 3)))
        def _():
            arrived(zbs[i].at[c], rz_r.at[i, c], row, z)
            add_into(i, c, row, "all", zbs[i][c])

        go(Link("z", piece(i, c, row, "all"), zbs[i].at[c], rz_r.at[i, c], row, z + 1, c > z))
        slot = c + (4 - c) * (1 - jnp.minimum(jnp.abs(z - 1 - c), 1))
        go(Link("z", piece(i, c, row, "all"), zbs[i].at[slot], rz_r.at[i, slot], row, z - 1, c < z))

    def sum_last(i):
        lead, span = place(i, z, row, "all")
        outs[i][...] = ds_[i][lead, span, :].astype(F32)

        @pl.when(z > 0)
        def _():
            arrived(zbs[i].at[z], rz_r.at[i, z], row, z)
            outs[i][...] = outs[i][...] + zbs[i][z].astype(F32)

        @pl.when(z < 3)
        def _():
            arrived(zbs[i].at[4], rz_r.at[i, 4], row, z)
            outs[i][...] = outs[i][...] + zbs[i][4].astype(F32)

    def gains_first():
        gain_z[pl.ds(z, 1)] = gain_sum[pl.ds(z, 1)]
        arrived(gain_z.at[pl.ds(0, 3)], gz_r.at[0], row, z)
        gain_all[pl.ds(row, 1)] = (gain_z[0] + gain_z[1] + gain_z[2] + gain_z[3])[None]
        for step in range(1, 8):
            go(Link("x", gain_all.at[row], gain_all.at[row], gp_r.at[0], (row + step) % 8, z))

    def gains_last():
        arrived(gain_all.at[pl.ds(0, 7)], gp_r.at[0], row, z)
        total = gain_all[0]
        for r in range(1, 8):
            total = total + gain_all[r]
        gain_one_out[...] = total[0:1, 0:192].reshape(192)
        gain_two_out[...] = total[1:2, 0:192].reshape(192)

    def results(which, step):
        got, out, n = {"mx": (mixed_got, mixed_out, 2), "ig": (input_got, input_out, 3)}[which]
        step(pltpu.make_async_copy(got, out, io.at[n]))

    def finish(which):
        got, send, recv = {
            "mx": (mixed_got, mixed_send, mx_r), "ig": (input_got, input_send, ig_r)}[which]
        lines(got, z)[...] = send[z]
        arrived(got.at[pl.ds(0, 384), :], recv.at[0], row, z)
        results(which, lambda copy: copy.start())

    own_tokens(lambda copy: copy.start())
    pack_own()
    pl.semaphore_wait(barrier, peers)
    gather_z(0, 0)
    send_edges()
    gather_xy(0, 0)
    gather_z(1, 0)
    take_edges()
    gather_xy(1, 0)
    hop_tok(1, 0)
    gather_z(0, 1)
    gather_z(2, 0)
    gather_xy(0, 1)
    gather_z(1, 1)
    gather_xy(1, 1)
    gather_second_x(1, 0)
    hop_tok(3, 0)
    gather_second_y(1, 0)
    gather_second_y(0, 1)
    gather_second_x(0, 1)
    gather_z(0, 2)
    gather_xy(2, 0)
    hop_tok(2, 0)
    gather_second_x(0, 0)
    gather_second_y(0, 0)
    gather_second_y(1, 1)
    gather_second_x(1, 1)
    gather_xy(0, 2)
    gather_z(0, 3)
    hop_tok(3, 1)
    gather_z(2, 1)
    gather_xy(2, 1)
    gather_xy(0, 3)
    gather_third(1, 0)
    hop_tok(2, 1)
    gather_z(2, 2)
    gather_xy(2, 2)
    gather_third(0, 0)
    gather_second_x(2, 0)
    hop_cot(3, 0)
    gather_third(1, 1)
    gather_third(0, 1)
    gather_second_x(0, 2)
    gather_z(1, 2)
    hop_cot(2, 0)
    gather_done(1, 0)
    gather_done(1, 1)
    hop_tok(3, 2)
    tables()
    gather_second_y(2, 0)
    gather_done(0, 1)
    gather_second_y(0, 2)
    gather_second_y(2, 1)
    gather_done(0, 0)
    take_tokens()
    norm_one()
    gather_second_x(2, 1)
    gather_z(2, 3)
    gather_second_x(0, 3)
    gather_second_y(0, 3)
    forward_heads(1)
    gather_xy(2, 3)
    gather_z(1, 3)
    gather_xy(1, 3)
    hop_cot(3, 1)
    gather_third(0, 2)
    gather_third(2, 0)
    gather_second_x(2, 2)
    gather_second_y(2, 2)
    hop_cot(2, 1)
    forward_heads(0)
    hop_cot(1, 0)
    gather_done(0, 2)
    gather_third(0, 3)
    forward_heads(2)
    gather_second_y(2, 3)
    gather_done(0, 3)
    gather_second_x(2, 3)
    hop_cot(3, 2)
    gather_third(2, 1)
    gather_second_y(1, 3)
    gather_done(2, 0)
    gather_second_x(1, 3)
    gather_xy(1, 2)
    forward_heads(3)
    gather_third(2, 2)
    gather_done(2, 1)
    forward_middle()
    gather_third(2, 3)
    forward_hidden(0)
    take_cotangent()
    forward_hidden(1)
    gather_second_y(1, 2)
    gather_third(1, 3)
    gather_done(2, 3)
    gather_done(2, 2)
    grad_down(1)
    gather_second_x(1, 2)
    backward_hidden(1)
    backward_hidden(0)
    grad_in(2)
    sum_first(1, 2)
    grad_in(3)
    forward_tail()
    backward_tail()
    gather_done(1, 3)
    grad_down(0)
    forward_hidden(3)
    backward_hidden(3)
    gather_third(1, 2)
    grad_down(3)
    sum_second(1, 2)
    sum_first(1, 3)
    grad_in(0)
    sum_first(1, 0)
    gather_done(1, 2)
    forward_hidden(2)
    backward_hidden(2)
    backward_middle()
    sum_second(1, 0)
    grad_down(2)
    grad_tail()
    sum_first(2, 2)
    sum_first(2, 0)
    sum_first(2, 1)
    forward_mixed()
    sum_second(1, 3)
    backward_heads(1)
    sum_second(2, 1)
    sum_second(2, 0)
    sum_second(2, 2)
    sum_first(2, 3)
    hop_mixed(3, 0)
    backward_heads(0)
    backward_heads(2)
    hop_mixed(2, 0)
    backward_heads(3)
    sum_second(2, 3)
    backward_first()
    halo_send()
    grad_in(1)
    hop_mixed(3, 1)
    sum_third_x(2, 2)
    sum_third_y(2, 0)
    grad_out()
    sum_first(1, 1)
    grad_qkv(0)
    hop_mixed(1, 0)
    sum_third_x(2, 0)
    sum_first(0, 0)
    sum_second(1, 1)
    halo_take()
    backward_last()
    hop_input(3, 0)
    sum_second(0, 0)
    grad_qkv(2)
    send_gain()
    sum_third_x(2, 3)
    sum_third_y(2, 1)
    hop_input(1, 0)
    hop_input(2, 0)
    sum_first(0, 2)
    grad_qkv(1)
    sum_third_x(1, 0)
    sum_first(0, 1)
    sum_third_y(2, 2)
    hop_input(3, 1)
    sum_third_y(1, 0)
    sum_third_x(2, 1)
    sum_third_x(0, 0)
    sum_third_y(0, 0)
    hop_mixed(2, 1)
    sum_second(0, 1)
    hop_input(2, 1)
    hop_input(3, 2)
    sum_fourth(2, 0)
    sum_third_y(1, 1)
    sum_third_x(1, 1)
    sum_second(0, 2)
    sum_fourth(1, 0)
    grad_qkv(3)
    hop_mixed(3, 2)
    sum_fourth(0, 0)
    sum_third_y(0, 1)
    sum_third_x(0, 1)
    sum_fourth(2, 1)
    sum_first(0, 3)
    sum_third_x(1, 2)
    sum_third_y(1, 2)
    sum_fourth(2, 2)
    sum_fourth(1, 1)
    sum_third_y(0, 2)
    sum_third_x(0, 2)
    sum_second(0, 3)
    sum_third_y(2, 3)
    finish("mx")
    sum_fourth(0, 1)
    sum_fourth(1, 2)
    gains_first()
    sum_fourth(0, 2)
    sum_third_x(1, 3)
    sum_third_y(1, 3)
    sum_third_x(0, 3)
    finish("ig")
    sum_third_y(0, 3)
    sum_fourth(2, 3)
    gains_last()
    sum_fourth(1, 3)
    sum_last(1)
    sum_last(2)
    sum_fourth(0, 3)
    sum_last(0)
    unpack_outs()
    results("mx", lambda copy: copy.wait())
    results("ig", lambda copy: copy.wait())
    ways.drain()


def hand_over(*refs):
    for n in range(8):
        refs[8 + n][...] = refs[n][...].astype(refs[8 + n].dtype)


def fast_local(
    tokens, segment_ids, gain_one, qkv_weight, out_weight, gain_two, in_weight, down_weight,
    cotangent,
):
    rows_all = tokens.shape[1] * 2 * lax.axis_size("row")
    length = min(SEQ_MAX, rows_all)

    def start_of(row, z):
        return (row * 4 + z) * OWN, length

    frequency = 10000.0 ** (-(np.arange(HEAD_DIM // 2) * 2.0) / HEAD_DIM)
    frequency = jnp.asarray(np.tile(frequency.astype(np.float32), 4)[None, :].repeat(8, 0))
    vmem, dma = pltpu.VMEM, pltpu.SemaphoreType.DMA
    shapes = [
        vmem((576, 384), BF), vmem((4, 192, 384), BF), vmem((4, 128, 384), BF),
        vmem((4, 8, 256), F32),
        vmem((4, 768, 768), BF), vmem((4, 768, 512), BF), vmem((4, 1152, 256), BF),
        vmem((4, 768, 768), BF), vmem((4, 768, 512), BF), vmem((4, 1152, 256), BF),
    ]
    shapes += [vmem((4, 4, ROWS[i], COLS[i]), BF) for i in range(3)]
    shapes += [vmem((4, 2, SPLIT[i], COLS[i]), BF) for i in range(3)]
    shapes += [vmem((4, ROWS[i] - SPLIT[i], COLS[i]), BF) for i in range(3)]
    shapes += [vmem((4, SPLIT[i], COLS[i]), BF) for i in range(3)]
    shapes += [vmem((4, 2, ROWS[i] - SPLIT[i], COLS[i]), BF) for i in range(3)]
    shapes += [vmem((5, ROWS[i], COLS[i]), BF) for i in range(3)]
    shapes += [
        vmem((8, 256), F32), vmem((8, OWN), F32),
        vmem((EXT, 768), F32), vmem((EXT, 128), F32), vmem((EXT, 128), F32),
        vmem((OWN, EXT), F32), vmem((EXT, 768), BF), vmem((OWN, 768), F32),
        vmem((2, OWN, 128), F32), vmem((4, 2, OWN, 128), BF), vmem((4, 2, EXT, 128), BF),
        vmem((4, 2, EXT, 128), BF), vmem((12, OWN, EXT), F32),
        vmem((4, OWN, 256), BF), vmem((OWN, 768), BF),
        vmem((OWN, 768), F32), vmem((OWN, 768), F32), vmem((OWN, 768), BF),
        vmem((768, 512), BF), vmem((4, 128, 256), BF), vmem((4, OWN, 256), BF),
        vmem((OWN, 128), BF), vmem((4, OWN, 256), F32), vmem((4, OWN, 256), F32),
        vmem((4, OWN, 128), F32), vmem((4, OWN, 128), F32), vmem((OWN, 1024), BF),
        vmem((4, OWN, 512), BF), vmem((OWN, 512), BF),
        vmem((OWN, 1024), BF), vmem((4, OWN, 256), BF), vmem((4, EXT, 640), BF),
        vmem((128, 768), BF), vmem((64, 768), BF), vmem((64, 768), BF),
        vmem((4, 128, 384), BF), vmem((512, 384), BF),
        vmem((4, 128, 384), BF), vmem((512, 384), BF),
        vmem((2, 3, 192, 384), BF), vmem((2, 3, 128, 384), BF), vmem((2, 3, 128, 384), BF),
        vmem((2, 3, 128, 384), BF),
        vmem((8, 768), F32), vmem((4, 8, 256), F32), vmem((4, 8, 256), F32),
        vmem((8, 8, 256), F32), vmem((96, 768), F32), vmem((96, 512), F32), vmem((144, 256), F32),
        dma((16,)), dma((16,)), dma((24,)), dma((16,)), dma((4,)),
        dma((4, 2, 3)), dma((1,)), dma((1,)), dma((1,)), dma((1,)), dma((1,)),
        dma((3, 4)), dma((3, 4)), dma((3, 4)), dma((3, 4)), dma((3, 4)),
        dma((3, 4)), dma((3, 4)), dma((3, 4)), dma((3, 4)), dma((3, 5)),
        dma((2,)), dma((1,)), dma((1,)), dma((1,)), dma((1,)),
    ]
    whole, held = pl.BlockSpec(memory_space=pltpu.VMEM), pl.BlockSpec(memory_space=pl.ANY)
    results = (
        jax.ShapeDtypeStruct((512, 384), BF), jax.ShapeDtypeStruct((512, 384), F32),
        jax.ShapeDtypeStruct((3, 96, 192), F32), jax.ShapeDtypeStruct((96, 192), F32),
        jax.ShapeDtypeStruct((96, 2, 288), F32), jax.ShapeDtypeStruct((144, 192), F32),
        jax.ShapeDtypeStruct((192,), F32), jax.ShapeDtypeStruct((192,), F32),
    )
    outs = pl.pallas_call(
        functools.partial(layer_kernel, start_of=start_of),
        out_shape=(results[0], jax.ShapeDtypeStruct((512, 384), BF)) + results[2:],
        in_specs=[held] * 2 + [whole] * 8,
        out_specs=(held,) * 2 + (whole,) * 6,
        scratch_shapes=shapes,
        compiler_params=pltpu.CompilerParams(
            collective_id=0, has_side_effects=True, vmem_limit_bytes=63 * 1024 * 1024),
    )(tokens[0], cotangent[0], qkv_weight.transpose(1, 0, 2), out_weight, in_weight, down_weight,
      gain_one, gain_two, segment_ids.reshape(-1, 128), frequency)
    mixed, input_grad, qkv_grad, out_grad, in_grad, down_grad, one_grad, two_grad = pl.pallas_call(
        hand_over,
        out_shape=results,
        in_specs=[whole] * 8,
        out_specs=(whole,) * 8,
    )(*outs)
    return (
        mixed[None], input_grad[None], one_grad, qkv_grad.transpose(1, 0, 2), out_grad,
        two_grad, in_grad, down_grad,
    )


def solution(mesh):
    placed = (
        P("col", "row", None),
        P(),
        P("col"),
        P("row", None, "col"),
        P("row", "col"),
        P("col"),
        P("row", None, "col"),
        P("row", "col"),
        P("col", "row", None),
    )
    part = local
    if mesh.shape["row"] == 8 and mesh.shape["col"] == 4:
        part = fast_local
    return jax.shard_map(
        part,
        mesh=mesh,
        in_specs=placed,
        out_specs=(
            P("col", "row", None),
            P("col", "row", None),
            P("col"),
            P("row", None, "col"),
            P("row", "col"),
            P("col"),
            P("row", None, "col"),
            P("row", "col"),
        ),
        check_vma=False,
    )
```
